256 devices in a mesh: seq: 32 (over z, y), head: 8 (over x, core).
Axes of the slice: x: 4, y: 4, z: 8, core: 2. Of those that a mesh axis runs over, the one named last changes fastest.
Arguments:
- query: bfloat16 [16384, 6144], P('seq', 'head'), may hold values from -6 to 6
- key: bfloat16 [16384, 6144], P('seq', 'head'), may hold values from -6 to 6
- value: bfloat16 [16384, 6144], P('seq', 'head'), may hold values from -6 to 6
- init_state: float32 [48, 128, 128], P('head'), may hold values from -768 to 768
- out_weight: bfloat16 [6144, 6144], P(('head', 'seq')), may hold values from -0.078125 to 0.078125
- out_grad: bfloat16 [16384, 6144], P('seq'), may hold values from -24 to 24
Outputs:
- mixed: bfloat16 [16384, 6144], P('seq', 'head')
- grad_query: bfloat16 [16384, 6144], P('seq', 'head')
- grad_key: bfloat16 [16384, 6144], P('seq', 'head')
- grad_value: bfloat16 [16384, 6144], P('seq', 'head')
- init_grad: float32 [48, 128, 128], P('head')
The draws below stay inside these ranges and needn't reach their ends.
All inputs are finite; a program needn't handle non-finite values.
Results may differ from the reference program's by a relative error of at most 0.017.
Values may be sent and summed in bfloat16 or wider, within the bound.
A program may use at most 128 MiB of HBM per device.

```python
import jax
import jax.numpy as jnp
from jax import lax

HEADS = 48
HEAD_DIM = 128
D = 6144
TOK_DEV = 512
TOKENS = 16384
N_SEQ = 32
N_HEAD = 8


def levels(own_key, extent, split, smallest, top_value):
    level, own = 1.0, jax.random.fold_in(own_key, 6)
    for dim, shards_of in split:
        steps = jnp.exp(jax.random.uniform(jax.random.fold_in(own, dim), (shards_of,), jnp.float32, smallest / len(split), top_value / len(split)))
        level = level * jnp.repeat(steps, extent[dim] // shards_of).reshape([-1 if axis == dim else 1 for axis in range(len(extent))])
    return level


def bell_draw(rng, shape, width, bound, shards=(), held_as=jnp.bfloat16):
    values = jax.random.normal(rng, shape, jnp.float32) * width
    if len(shards) > 0:
        values = levels(rng, shape, shards, -0.22, 0.18) * values
    return jnp.clip(values, min=-bound, max=bound).astype(held_as)


def setup_inputs(seed: int = 0) -> dict:
    key_list = jax.random.split(jax.random.key(seed), 7)
    query = bell_draw(key_list[0], (TOKENS, D), 1.0, 6.0, ((0, 32), (1, 8)))
    key = bell_draw(key_list[1], (TOKENS, D), 1.0, 6.0, ((0, 32), (1, 8)))
    value = bell_draw(key_list[2], (TOKENS, D), 1.0, 6.0, ((0, 32), (1, 8)))
    init_state = bell_draw(key_list[3], (HEADS, HEAD_DIM, HEAD_DIM), (TOKENS ** 0.5), 768.0, ((0, 8),), jnp.float32)
    out_weight = bell_draw(key_list[4], (D, D), D ** -0.5, 0.078125, ((0, 256),))
    out_grad = bell_draw(key_list[5], (TOKENS, D), 4.0, 24.0, ((0, 32),))
    return {"query": query, "key": key, "value": value, "init_state": init_state, "out_weight": out_weight, "out_grad": out_grad}


EPS = 1e-06

def normalize(attended):
    return attended * lax.rsqrt(lax.optimization_barrier(jnp.mean(attended * attended, axis=-1, keepdims=True)) + EPS)

def reference(query, key, value, init_state, out_weight, out_grad):
    split_shape = (N_SEQ, TOK_DEV, HEADS, HEAD_DIM)
    query_blocks = query.reshape(split_shape)
    key_blocks = key.reshape(split_shape)
    value_blocks = value.reshape(split_shape)
    grad_blocks = out_grad.reshape(N_SEQ, TOK_DEV, D)
    row_index = lax.broadcasted_iota(jnp.int32, (TOK_DEV, TOK_DEV), 0)
    col_index = lax.broadcasted_iota(jnp.int32, (TOK_DEV, TOK_DEV), 1)
    causal = col_index <= row_index
    weight_groups = out_weight.reshape(N_HEAD, D // N_HEAD, D).astype(jnp.float32)

    def forward(state, inputs):
        queries, key_rows, val_rows, grad_rows = inputs
        state_half = state.astype(jnp.bfloat16)
        scores = jnp.einsum('thi,shi->hts', queries.astype(jnp.float32), key_rows.astype(jnp.float32))
        attn_weights = jnp.where(causal, scores, 0.0).astype(jnp.bfloat16)
        attended = jnp.einsum('hts,shj->thj', attn_weights.astype(jnp.float32), val_rows.astype(jnp.float32))
        attended = attended + jnp.einsum('thi,hij->thj', queries.astype(jnp.float32), state_half.astype(jnp.float32))
        normed = normalize(attended).astype(jnp.bfloat16).reshape(TOK_DEV, D)
        groups = normed.reshape(TOK_DEV, N_HEAD, D // N_HEAD).astype(jnp.float32)
        pieces = jnp.einsum('tgc,gcd->tgd', groups, weight_groups, precision=lax.Precision.HIGHEST)
        rounded = lax.optimization_barrier(pieces.astype(jnp.bfloat16))
        mixed_rows = lax.optimization_barrier(jnp.sum(rounded.astype(jnp.float32), axis=1)).astype(jnp.bfloat16)
        grad_normed = lax.dot_general(grad_rows, out_weight, (((1,), (1,)), ((), ())), preferred_element_type=jnp.float32)
        _, norm_back = jax.vjp(normalize, attended)
        grad_att = norm_back(grad_normed.reshape(TOK_DEV, HEADS, HEAD_DIM))[0].astype(jnp.bfloat16)
        grad_scores = jnp.einsum('thj,shj->hts', grad_att.astype(jnp.float32), val_rows.astype(jnp.float32))
        grad_scores = jnp.where(causal, grad_scores, 0.0).astype(jnp.bfloat16)
        own_adjoint = jnp.einsum('thi,thj->hij', queries.astype(jnp.float32), grad_att.astype(jnp.float32))
        grad_query = jnp.einsum('hts,shi->thi', grad_scores.astype(jnp.float32), key_rows.astype(jnp.float32))
        grad_query = grad_query + jnp.einsum('thj,hij->thi', grad_att.astype(jnp.float32), state_half.astype(jnp.float32))
        local_state = jnp.einsum('thi,thj->hij', key_rows.astype(jnp.float32), val_rows.astype(jnp.float32))
        return (state + local_state, (mixed_rows, grad_query.astype(jnp.bfloat16), grad_att, own_adjoint))
    _, (mixed, grad_query, grad_atts, adjoints) = lax.scan(forward, init_state, (query_blocks, key_blocks, value_blocks, grad_blocks))

    def backward(accum, own):
        return (accum + own, accum)
    _, later_all = lax.scan(backward, jnp.zeros_like(init_state), adjoints, reverse=True)

    def key_value_grads(inputs):
        queries, key_rows, val_rows, grad_att, later = inputs
        later_half = later.astype(jnp.bfloat16).astype(jnp.float32)
        scores = jnp.einsum('thi,shi->hts', queries.astype(jnp.float32), key_rows.astype(jnp.float32))
        attn_weights = jnp.where(causal, scores, 0.0).astype(jnp.bfloat16).astype(jnp.float32)
        grad_scores = jnp.einsum('thj,shj->hts', grad_att.astype(jnp.float32), val_rows.astype(jnp.float32))
        grad_scores = jnp.where(causal, grad_scores, 0.0).astype(jnp.bfloat16).astype(jnp.float32)
        grad_key = jnp.einsum('hts,thi->shi', grad_scores, queries.astype(jnp.float32))
        grad_key = grad_key + jnp.einsum('thj,hij->thi', val_rows.astype(jnp.float32), later_half)
        grad_value = jnp.einsum('hts,thj->shj', attn_weights, grad_att.astype(jnp.float32))
        grad_value = grad_value + jnp.einsum('thi,hij->thj', key_rows.astype(jnp.float32), later_half)
        return (grad_key.astype(jnp.bfloat16), grad_value.astype(jnp.bfloat16))
    grad_key, grad_value = lax.map(key_value_grads, (query_blocks, key_blocks, value_blocks, grad_atts, later_all))
    init_grad = lax.optimization_barrier(jnp.sum(adjoints, axis=0))
    return (mixed.reshape(TOKENS, D), grad_query.reshape(TOKENS, D), grad_key.reshape(TOKENS, D), grad_value.reshape(TOKENS, D), init_grad)
```

```python
import jax
import jax.numpy as jnp
from jax import lax
from jax.sharding import PartitionSpec as P

EPS = 1e-06


def butterfly(value, axis, backward):
    count = lax.axis_size(axis)
    place = lax.axis_index(axis)
    total = value
    partial = jnp.zeros_like(value)
    step = 1
    while step < count:
        pairs = [(i, i ^ step) for i in range(count)]
        other = lax.ppermute(total, axis, perm=pairs)
        upper = (place & step) != 0
        take = jnp.logical_not(upper) if backward else upper
        partial = jnp.where(take, partial + other, partial)
        total = total + other
        step *= 2
    return partial, total


def normalize(attended):
    return attended * lax.rsqrt(jnp.mean(attended * attended, axis=-1, keepdims=True) + EPS)


def shards(query, key, value, init_state, out_weight, out_grad):
    tok_rows = query.shape[0]
    width = query.shape[1]
    heads_here = init_state.shape[0]
    head_dim = init_state.shape[2]
    queries = query.reshape(tok_rows, heads_here, head_dim)
    key_rows = key.reshape(tok_rows, heads_here, head_dim)
    val_rows = value.reshape(tok_rows, heads_here, head_dim)
    local_state = jnp.einsum("thi,thj->hij", key_rows, val_rows, preferred_element_type=jnp.float32)
    earlier, _ = butterfly(local_state, "seq", False)
    state_half = (init_state + earlier).astype(jnp.bfloat16)
    row_index = lax.broadcasted_iota(jnp.int32, (tok_rows, tok_rows), 0)
    col_index = lax.broadcasted_iota(jnp.int32, (tok_rows, tok_rows), 1)
    causal = col_index <= row_index
    scores = jnp.einsum("thi,shi->hts", queries, key_rows, preferred_element_type=jnp.float32)
    attn_weights = jnp.where(causal, scores, 0.0).astype(jnp.bfloat16)
    attended = jnp.einsum(
        "hts,shj->thj", attn_weights, val_rows, preferred_element_type=jnp.float32
    )
    attended = attended + jnp.einsum(
        "thi,hij->thj", queries, state_half, preferred_element_type=jnp.float32
    )
    normed = normalize(attended).astype(jnp.bfloat16).reshape(tok_rows, width)
    weight_rows = lax.all_gather(out_weight, "seq", axis=0, tiled=True)
    projected = jnp.dot(normed, weight_rows, preferred_element_type=jnp.float32)
    grad_normed = lax.dot_general(
        out_grad, weight_rows, (((1,), (1,)), ((), ())), preferred_element_type=jnp.float32
    )
    mixed = lax.psum_scatter(
        projected.astype(jnp.bfloat16), "head", scatter_dimension=1, tiled=True
    )
    _, norm_back = jax.vjp(normalize, attended)
    grad_att = norm_back(grad_normed.reshape(tok_rows, heads_here, head_dim))[0].astype(
        jnp.bfloat16
    )
    grad_scores = jnp.einsum("thj,shj->hts", grad_att, val_rows, preferred_element_type=jnp.float32)
    grad_scores = jnp.where(causal, grad_scores, 0.0).astype(jnp.bfloat16)
    own_adjoint = jnp.einsum("thi,thj->hij", queries, grad_att, preferred_element_type=jnp.float32)
    later, adjoint_total = butterfly(own_adjoint, "seq", True)
    later_half = later.astype(jnp.bfloat16)
    grad_query = jnp.einsum(
        "hts,shi->thi", grad_scores, key_rows, preferred_element_type=jnp.float32
    )
    grad_query = grad_query + jnp.einsum(
        "thj,hij->thi", grad_att, state_half, preferred_element_type=jnp.float32
    )
    grad_key = jnp.einsum("hts,thi->shi", grad_scores, queries, preferred_element_type=jnp.float32)
    grad_key = grad_key + jnp.einsum(
        "thj,hij->thi", val_rows, later_half, preferred_element_type=jnp.float32
    )
    grad_value = jnp.einsum(
        "hts,thj->shj", attn_weights, grad_att, preferred_element_type=jnp.float32
    )
    grad_value = grad_value + jnp.einsum(
        "thi,hij->thj", key_rows, later_half, preferred_element_type=jnp.float32
    )
    init_grad = adjoint_total
    return (
        mixed,
        grad_query.reshape(tok_rows, width).astype(jnp.bfloat16),
        grad_key.reshape(tok_rows, width).astype(jnp.bfloat16),
        grad_value.reshape(tok_rows, width).astype(jnp.bfloat16),
        init_grad,
    )


def solution(mesh):
    return jax.shard_map(
        shards,
        mesh=mesh,
        in_specs=(
            P("seq", "head"),
            P("seq", "head"),
            P("seq", "head"),
            P("head", None, None),
            P(("head", "seq"), None),
            P("seq", None),
        ),
        out_specs=(
            P("seq", "head"),
            P("seq", "head"),
            P("seq", "head"),
            P("seq", "head"),
            P("head", None, None),
        ),
        check_vma=False,
    )
```

```python
import functools

import jax
import jax.numpy as jnp
from jax import lax
from jax.experimental import pallas as pl
from jax.experimental.pallas import tpu as pltpu
from jax.sharding import PartitionSpec as P

EPS = 1e-06


MESH = pl.DeviceIdType.MESH


def butterfly_kernel(count, backward, value_ref, partial_ref, total_ref, sendbuf, recvbuf, send_sem, recv_sem):
    me = lax.axis_index("seq")
    head = lax.axis_index("head")
    rounds = count.bit_length() - 1
    partners = []
    for k in range(rounds):
        step = 1 << k
        bit = (me // step) % 2
        partners.append((me + step - 2 * step * bit, bit))
    barrier = pltpu.get_barrier_semaphore()
    for partner, _ in partners:
        pl.semaphore_signal(barrier, inc=1, device_id=(partner, head), device_id_type=MESH)
    pl.semaphore_wait(barrier, rounds)
    total = value_ref[...]
    partial = jnp.zeros_like(total)
    for k, (partner, bit) in enumerate(partners):
        sendbuf[k] = total
        copy = pltpu.make_async_remote_copy(
            src_ref=sendbuf.at[k],
            dst_ref=recvbuf.at[k],
            send_sem=send_sem.at[k],
            recv_sem=recv_sem.at[k],
            device_id=(partner, head),
            device_id_type=MESH,
        )
        copy.start()
        copy.wait()
        other = recvbuf[k]
        take = (bit == 0) if backward else (bit == 1)
        partial = jnp.where(take, partial + other, partial)
        total = total + other
    partial_ref[...] = partial
    total_ref[...] = total


def butterfly(value, axis, backward):
    count = lax.axis_size(axis)
    rounds = count.bit_length() - 1
    shape = jax.ShapeDtypeStruct(value.shape, jnp.float32)
    return pl.pallas_call(
        functools.partial(butterfly_kernel, count, backward),
        out_shape=(shape, shape),
        in_specs=[pl.BlockSpec(memory_space=pltpu.VMEM)],
        out_specs=(pl.BlockSpec(memory_space=pltpu.VMEM), pl.BlockSpec(memory_space=pltpu.VMEM)),
        scratch_shapes=[
            pltpu.VMEM((rounds,) + value.shape, jnp.float32),
            pltpu.VMEM((rounds,) + value.shape, jnp.float32),
            pltpu.SemaphoreType.DMA((rounds,)),
            pltpu.SemaphoreType.DMA((rounds,)),
        ],
        compiler_params=pltpu.CompilerParams(
            collective_id=1 if backward else 0, has_side_effects=True
        ),
    )(value.astype(jnp.float32))


def normalize(attended):
    return attended * lax.rsqrt(jnp.mean(attended * attended, axis=-1, keepdims=True) + EPS)


def shards(query, key, value, init_state, out_weight, out_grad):
    tok_rows = query.shape[0]
    width = query.shape[1]
    heads_here = init_state.shape[0]
    head_dim = init_state.shape[2]
    queries = query.reshape(tok_rows, heads_here, head_dim)
    key_rows = key.reshape(tok_rows, heads_here, head_dim)
    val_rows = value.reshape(tok_rows, heads_here, head_dim)
    local_state = jnp.einsum("thi,thj->hij", key_rows, val_rows, preferred_element_type=jnp.float32)
    earlier, _ = butterfly(local_state, "seq", False)
    state_half = (init_state + earlier).astype(jnp.bfloat16)
    row_index = lax.broadcasted_iota(jnp.int32, (tok_rows, tok_rows), 0)
    col_index = lax.broadcasted_iota(jnp.int32, (tok_rows, tok_rows), 1)
    causal = col_index <= row_index
    scores = jnp.einsum("thi,shi->hts", queries, key_rows, preferred_element_type=jnp.float32)
    attn_weights = jnp.where(causal, scores, 0.0).astype(jnp.bfloat16)
    attended = jnp.einsum(
        "hts,shj->thj", attn_weights, val_rows, preferred_element_type=jnp.float32
    )
    attended = attended + jnp.einsum(
        "thi,hij->thj", queries, state_half, preferred_element_type=jnp.float32
    )
    normed = normalize(attended).astype(jnp.bfloat16).reshape(tok_rows, width)
    weight_rows = lax.all_gather(out_weight, "seq", axis=0, tiled=True)
    projected = jnp.dot(normed, weight_rows, preferred_element_type=jnp.float32)
    grad_normed = lax.dot_general(
        out_grad, weight_rows, (((1,), (1,)), ((), ())), preferred_element_type=jnp.float32
    )
    mixed = lax.psum_scatter(
        projected.astype(jnp.bfloat16), "head", scatter_dimension=1, tiled=True
    )
    _, norm_back = jax.vjp(normalize, attended)
    grad_att = norm_back(grad_normed.reshape(tok_rows, heads_here, head_dim))[0].astype(
        jnp.bfloat16
    )
    grad_scores = jnp.einsum("thj,shj->hts", grad_att, val_rows, preferred_element_type=jnp.float32)
    grad_scores = jnp.where(causal, grad_scores, 0.0).astype(jnp.bfloat16)
    own_adjoint = jnp.einsum("thi,thj->hij", queries, grad_att, preferred_element_type=jnp.float32)
    later, adjoint_total = butterfly(own_adjoint, "seq", True)
    later_half = later.astype(jnp.bfloat16)
    grad_query = jnp.einsum(
        "hts,shi->thi", grad_scores, key_rows, preferred_element_type=jnp.float32
    )
    grad_query = grad_query + jnp.einsum(
        "thj,hij->thi", grad_att, state_half, preferred_element_type=jnp.float32
    )
    grad_key = jnp.einsum("hts,thi->shi", grad_scores, queries, preferred_element_type=jnp.float32)
    grad_key = grad_key + jnp.einsum(
        "thj,hij->thi", val_rows, later_half, preferred_element_type=jnp.float32
    )
    grad_value = jnp.einsum(
        "hts,thj->shj", attn_weights, grad_att, preferred_element_type=jnp.float32
    )
    grad_value = grad_value + jnp.einsum(
        "thi,hij->thj", key_rows, later_half, preferred_element_type=jnp.float32
    )
    init_grad = adjoint_total
    return (
        mixed,
        grad_query.reshape(tok_rows, width).astype(jnp.bfloat16),
        grad_key.reshape(tok_rows, width).astype(jnp.bfloat16),
        grad_value.reshape(tok_rows, width).astype(jnp.bfloat16),
        init_grad,
    )


def solution(mesh):
    return jax.shard_map(
        shards,
        mesh=mesh,
        in_specs=(
            P("seq", "head"),
            P("seq", "head"),
            P("seq", "head"),
            P("head", None, None),
            P(("head", "seq"), None),
            P("seq", None),
        ),
        out_specs=(
            P("seq", "head"),
            P("seq", "head"),
            P("seq", "head"),
            P("seq", "head"),
            P("head", None, None),
        ),
        check_vma=False,
    )
```

```python
import functools

import jax
import jax.numpy as jnp
from jax import lax
from jax.experimental import pallas as pl
from jax.experimental.pallas import tpu as pltpu
from jax.sharding import PartitionSpec as P

EPS = 1e-06


MESH = pl.DeviceIdType.MESH


def butterfly_kernel(count, backward, value_ref, partial_ref, total_ref, sendbuf, recvbuf, send_sem, recv_sem):
    me = lax.axis_index("seq")
    head = lax.axis_index("head")
    rounds = count.bit_length() - 1
    partners = []
    for k in range(rounds):
        step = 1 << k
        bit = (me // step) % 2
        partners.append((me + step - 2 * step * bit, bit))
    barrier = pltpu.get_barrier_semaphore()
    for partner, _ in partners:
        pl.semaphore_signal(barrier, inc=1, device_id=(partner, head), device_id_type=MESH)
    pl.semaphore_wait(barrier, rounds)
    total = value_ref[...]
    partial = jnp.zeros_like(total)
    for k, (partner, bit) in enumerate(partners):
        sent = total.astype(jnp.bfloat16)
        sendbuf[k] = sent
        copy = pltpu.make_async_remote_copy(
            src_ref=sendbuf.at[k],
            dst_ref=recvbuf.at[k],
            send_sem=send_sem.at[k],
            recv_sem=recv_sem.at[k],
            device_id=(partner, head),
            device_id_type=MESH,
        )
        copy.start()
        copy.wait()
        other = recvbuf[k].astype(jnp.float32)
        take = (bit == 0) if backward else (bit == 1)
        partial = jnp.where(take, partial + other, partial)
        total = sent.astype(jnp.float32) + other
    partial_ref[...] = partial
    total_ref[...] = total


def butterfly(value, axis, backward):
    count = lax.axis_size(axis)
    rounds = count.bit_length() - 1
    shape = jax.ShapeDtypeStruct(value.shape, jnp.float32)
    return pl.pallas_call(
        functools.partial(butterfly_kernel, count, backward),
        out_shape=(shape, shape),
        in_specs=[pl.BlockSpec(memory_space=pltpu.VMEM)],
        out_specs=(pl.BlockSpec(memory_space=pltpu.VMEM), pl.BlockSpec(memory_space=pltpu.VMEM)),
        scratch_shapes=[
            pltpu.VMEM((rounds,) + value.shape, jnp.bfloat16),
            pltpu.VMEM((rounds,) + value.shape, jnp.bfloat16),
            pltpu.SemaphoreType.DMA((rounds,)),
            pltpu.SemaphoreType.DMA((rounds,)),
        ],
        compiler_params=pltpu.CompilerParams(
            collective_id=1 if backward else 0, has_side_effects=True
        ),
    )(value.astype(jnp.float32))


def normalize(attended):
    return attended * lax.rsqrt(jnp.mean(attended * attended, axis=-1, keepdims=True) + EPS)


def shards(query, key, value, init_state, out_weight, out_grad):
    tok_rows = query.shape[0]
    width = query.shape[1]
    heads_here = init_state.shape[0]
    head_dim = init_state.shape[2]
    queries = query.reshape(tok_rows, heads_here, head_dim)
    key_rows = key.reshape(tok_rows, heads_here, head_dim)
    val_rows = value.reshape(tok_rows, heads_here, head_dim)
    local_state = jnp.einsum("thi,thj->hij", key_rows, val_rows, preferred_element_type=jnp.float32)
    earlier, _ = butterfly(local_state, "seq", False)
    state_half = (init_state + earlier).astype(jnp.bfloat16)
    row_index = lax.broadcasted_iota(jnp.int32, (tok_rows, tok_rows), 0)
    col_index = lax.broadcasted_iota(jnp.int32, (tok_rows, tok_rows), 1)
    causal = col_index <= row_index
    scores = jnp.einsum("thi,shi->hts", queries, key_rows, preferred_element_type=jnp.float32)
    attn_weights = jnp.where(causal, scores, 0.0).astype(jnp.bfloat16)
    attended = jnp.einsum(
        "hts,shj->thj", attn_weights, val_rows, preferred_element_type=jnp.float32
    )
    attended = attended + jnp.einsum(
        "thi,hij->thj", queries, state_half, preferred_element_type=jnp.float32
    )
    normed = normalize(attended).astype(jnp.bfloat16).reshape(tok_rows, width)
    weight_rows = lax.all_gather(out_weight, "seq", axis=0, tiled=True)
    projected = jnp.dot(normed, weight_rows, preferred_element_type=jnp.float32)
    grad_normed = lax.dot_general(
        out_grad, weight_rows, (((1,), (1,)), ((), ())), preferred_element_type=jnp.float32
    )
    mixed = lax.psum_scatter(
        projected.astype(jnp.bfloat16), "head", scatter_dimension=1, tiled=True
    )
    _, norm_back = jax.vjp(normalize, attended)
    grad_att = norm_back(grad_normed.reshape(tok_rows, heads_here, head_dim))[0].astype(
        jnp.bfloat16
    )
    grad_scores = jnp.einsum("thj,shj->hts", grad_att, val_rows, preferred_element_type=jnp.float32)
    grad_scores = jnp.where(causal, grad_scores, 0.0).astype(jnp.bfloat16)
    own_adjoint = jnp.einsum("thi,thj->hij", queries, grad_att, preferred_element_type=jnp.float32)
    later, adjoint_total = butterfly(own_adjoint, "seq", True)
    later_half = later.astype(jnp.bfloat16)
    grad_query = jnp.einsum(
        "hts,shi->thi", grad_scores, key_rows, preferred_element_type=jnp.float32
    )
    grad_query = grad_query + jnp.einsum(
        "thj,hij->thi", grad_att, state_half, preferred_element_type=jnp.float32
    )
    grad_key = jnp.einsum("hts,thi->shi", grad_scores, queries, preferred_element_type=jnp.float32)
    grad_key = grad_key + jnp.einsum(
        "thj,hij->thi", val_rows, later_half, preferred_element_type=jnp.float32
    )
    grad_value = jnp.einsum(
        "hts,thj->shj", attn_weights, grad_att, preferred_element_type=jnp.float32
    )
    grad_value = grad_value + jnp.einsum(
        "thi,hij->thj", key_rows, later_half, preferred_element_type=jnp.float32
    )
    init_grad = adjoint_total
    return (
        mixed,
        grad_query.reshape(tok_rows, width).astype(jnp.bfloat16),
        grad_key.reshape(tok_rows, width).astype(jnp.bfloat16),
        grad_value.reshape(tok_rows, width).astype(jnp.bfloat16),
        init_grad,
    )


def solution(mesh):
    return jax.shard_map(
        shards,
        mesh=mesh,
        in_specs=(
            P("seq", "head"),
            P("seq", "head"),
            P("seq", "head"),
            P("head", None, None),
            P(("head", "seq"), None),
            P("seq", None),
        ),
        out_specs=(
            P("seq", "head"),
            P("seq", "head"),
            P("seq", "head"),
            P("seq", "head"),
            P("head", None, None),
        ),
        check_vma=False,
    )
```

```python
import functools

import jax
import jax.numpy as jnp
from jax import lax
from jax.experimental import pallas as pl
from jax.experimental.pallas import tpu as pltpu
from jax.sharding import PartitionSpec as P

EPS = 1e-06


MESH = pl.DeviceIdType.MESH


def butterfly_kernel(count, backward, value_ref, partial_ref, total_ref, sendbuf, recvbuf, send_sem, recv_sem):
    me = lax.axis_index("seq")
    head = lax.axis_index("head")
    rounds = count.bit_length() - 1
    partners = []
    for k in range(rounds):
        step = 1 << k
        bit = (me // step) % 2
        partners.append((me + step - 2 * step * bit, bit))
    barrier = pltpu.get_barrier_semaphore()
    for partner, _ in partners:
        pl.semaphore_signal(barrier, inc=1, device_id=(partner, head), device_id_type=MESH)
    pl.semaphore_wait(barrier, rounds)
    total = value_ref[...]
    partial = jnp.zeros_like(total)
    for k, (partner, bit) in enumerate(partners):
        sent = total.astype(jnp.bfloat16)
        sendbuf[k] = sent
        copy = pltpu.make_async_remote_copy(
            src_ref=sendbuf.at[k],
            dst_ref=recvbuf.at[k],
            send_sem=send_sem.at[k],
            recv_sem=recv_sem.at[k],
            device_id=(partner, head),
            device_id_type=MESH,
        )
        copy.start()
        copy.wait()
        other = recvbuf[k].astype(jnp.float32)
        take = (bit == 0) if backward else (bit == 1)
        partial = jnp.where(take, partial + other, partial)
        total = sent.astype(jnp.float32) + other
    partial_ref[...] = partial
    total_ref[...] = total


def butterfly(value, axis, backward):
    count = lax.axis_size(axis)
    rounds = count.bit_length() - 1
    shape = jax.ShapeDtypeStruct(value.shape, jnp.float32)
    return pl.pallas_call(
        functools.partial(butterfly_kernel, count, backward),
        out_shape=(shape, shape),
        in_specs=[pl.BlockSpec(memory_space=pltpu.VMEM)],
        out_specs=(pl.BlockSpec(memory_space=pltpu.VMEM), pl.BlockSpec(memory_space=pltpu.VMEM)),
        scratch_shapes=[
            pltpu.VMEM((rounds,) + value.shape, jnp.bfloat16),
            pltpu.VMEM((rounds,) + value.shape, jnp.bfloat16),
            pltpu.SemaphoreType.DMA((rounds,)),
            pltpu.SemaphoreType.DMA((rounds,)),
        ],
        compiler_params=pltpu.CompilerParams(
            collective_id=1 if backward else 0, has_side_effects=True
        ),
    )(value.astype(jnp.float32))


def gather_kernel(ny, ca, value_ref, w_ref, rows_ref, partial_ref, sendbuf, recvbuf, send_sem, recv_sem, bf_send, bf_recv, local_sem):
    me = lax.axis_index("seq")
    head = lax.axis_index("head")
    count = lax.axis_size("seq")
    nz = count // ny
    y = me % ny
    z = me // ny
    piece, cols = w_ref.shape
    A = pl.ds(0, ca)
    B = pl.ds(ca, cols - ca)
    hy, hz = ny // 2, nz // 2
    hb = (cols - ca) // 2
    B1 = pl.ds(ca, hb)
    B2 = pl.ds(ca + hb, cols - ca - hb)

    def zz(k):
        return (z + nz + k) % nz

    def yy(k):
        return (y + ny + k) % ny

    def dev(zi, yi):
        return (zi * ny + yi, head)

    rounds = count.bit_length() - 1
    partners = []
    for k in range(rounds):
        step = 1 << k
        bit = (me // step) % 2
        partners.append((me + step - 2 * step * bit, bit))
    ring = [dev(z, yy(1)), dev(z, yy(-1)), dev(zz(1), y), dev(zz(-1), y)]
    barrier = pltpu.get_barrier_semaphore()
    for target in ring:
        pl.semaphore_signal(barrier, inc=1, device_id=target, device_id_type=MESH)
    for partner, _ in partners:
        pl.semaphore_signal(barrier, inc=1, device_id=(partner, head), device_id_type=MESH)
    pl.semaphore_wait(barrier, len(ring) + rounds)

    local = pltpu.make_async_copy(w_ref, rows_ref.at[z, y], local_sem)
    local.start()
    R = rows_ref
    yr, yl, zr, zl = dev(z, yy(1)), dev(z, yy(-1)), dev(zz(1), y), dev(zz(-1), y)
    ticks = [
        [(w_ref.at[:, A], R.at[z, y, :, A], yr), (w_ref.at[:, A], R.at[z, y, :, A], yl),
         (w_ref.at[:, B], R.at[z, y, :, B], zr), (w_ref.at[:, B], R.at[z, y, :, B], zl)],
        [(R.at[z, yy(-1), :, A], R.at[z, yy(-1), :, A], yr),
         (R.at[zz(-1), y, :, B], R.at[zz(-1), y, :, B], zr), (R.at[zz(1), y, :, B], R.at[zz(1), y, :, B], zl)],
        [(R.at[z, :, :, A], R.at[z, :, :, A], zr), (R.at[z, :, :, A], R.at[z, :, :, A], zl),
         (R.at[zz(-2), y, :, B], R.at[zz(-2), y, :, B], zr), (R.at[zz(2), y, :, B], R.at[zz(2), y, :, B], zl)],
        [(R.at[zz(-1), :, :, A], R.at[zz(-1), :, :, A], zr), (R.at[zz(1), :, :, A], R.at[zz(1), :, :, A], zl),
         (R.at[zz(-3), y, :, B1], R.at[zz(-3), y, :, B1], zr),
         (R.at[zz(3), y, :, B2], R.at[zz(3), y, :, B2], zl)],
        [(R.at[zz(-2), :, :, A], R.at[zz(-2), :, :, A], zr), (R.at[zz(2), :, :, A], R.at[zz(2), :, :, A], zl),
         (R.at[:, y, :, B], R.at[:, y, :, B], yr), (R.at[:, y, :, B], R.at[:, y, :, B], yl)],
        [(R.at[zz(-3), pl.ds(0, hy), :, A], R.at[zz(-3), pl.ds(0, hy), :, A], zr),
         (R.at[zz(3), pl.ds(hy, ny - hy), :, A], R.at[zz(3), pl.ds(hy, ny - hy), :, A], zl),
         (R.at[pl.ds(0, hz), yy(-1), :, B], R.at[pl.ds(0, hz), yy(-1), :, B], yr),
         (R.at[pl.ds(hz, nz - hz), yy(1), :, B], R.at[pl.ds(hz, nz - hz), yy(1), :, B], yl)],
    ]
    total = value_ref[...]
    partial = jnp.zeros_like(total)
    n = 0
    for t, moves in enumerate(ticks):
        if t == 2:
            local.wait()
        started = []
        for src, dst, target in moves:
            copy = pltpu.make_async_remote_copy(
                src_ref=src, dst_ref=dst, send_sem=send_sem.at[n], recv_sem=recv_sem.at[n],
                device_id=target, device_id_type=MESH,
            )
            copy.start()
            started.append(copy)
            n += 1
        scan = None
        if t < rounds:
            partner, bit = partners[t]
            sent = total.astype(jnp.bfloat16)
            sendbuf[t] = sent
            scan = pltpu.make_async_remote_copy(
                src_ref=sendbuf.at[t], dst_ref=recvbuf.at[t], send_sem=bf_send.at[t],
                recv_sem=bf_recv.at[t], device_id=(partner, head), device_id_type=MESH,
            )
            scan.start()
        for copy in started:
            copy.wait()
        if scan is not None:
            scan.wait()
            other = recvbuf[t].astype(jnp.float32)
            partial = jnp.where(bit == 1, partial + other, partial)
            total = sent.astype(jnp.float32) + other
    partial_ref[...] = partial


def gather_and_scan(value, weight):
    count = lax.axis_size("seq")
    ny = 4
    piece, cols = weight.shape
    rounds = count.bit_length() - 1
    ca = (cols * 2 // 3) // 128 * 128
    n_copies = 23
    return pl.pallas_call(
        functools.partial(gather_kernel, ny, ca),
        out_shape=(
            jax.ShapeDtypeStruct((count // ny, ny, piece, cols), weight.dtype),
            jax.ShapeDtypeStruct(value.shape, jnp.float32),
        ),
        in_specs=[pl.BlockSpec(memory_space=pltpu.VMEM), pl.BlockSpec(memory_space=pl.ANY)],
        out_specs=(pl.BlockSpec(memory_space=pl.ANY), pl.BlockSpec(memory_space=pltpu.VMEM)),
        scratch_shapes=[
            pltpu.VMEM((rounds,) + value.shape, jnp.bfloat16),
            pltpu.VMEM((rounds,) + value.shape, jnp.bfloat16),
            pltpu.SemaphoreType.DMA((n_copies,)),
            pltpu.SemaphoreType.DMA((n_copies,)),
            pltpu.SemaphoreType.DMA((rounds,)),
            pltpu.SemaphoreType.DMA((rounds,)),
            pltpu.SemaphoreType.DMA(()),
        ],
        compiler_params=pltpu.CompilerParams(collective_id=2, has_side_effects=True),
    )(value.astype(jnp.float32), weight)


def normalize(attended):
    return attended * lax.rsqrt(jnp.mean(attended * attended, axis=-1, keepdims=True) + EPS)


def shards(query, key, value, init_state, out_weight, out_grad):
    tok_rows = query.shape[0]
    width = query.shape[1]
    heads_here = init_state.shape[0]
    head_dim = init_state.shape[2]
    queries = query.reshape(tok_rows, heads_here, head_dim)
    key_rows = key.reshape(tok_rows, heads_here, head_dim)
    val_rows = value.reshape(tok_rows, heads_here, head_dim)
    local_state = jnp.einsum("thi,thj->hij", key_rows, val_rows, preferred_element_type=jnp.float32)
    gathered, earlier = gather_and_scan(local_state, out_weight)
    state_half = (init_state + earlier).astype(jnp.bfloat16)
    row_index = lax.broadcasted_iota(jnp.int32, (tok_rows, tok_rows), 0)
    col_index = lax.broadcasted_iota(jnp.int32, (tok_rows, tok_rows), 1)
    causal = col_index <= row_index
    scores = jnp.einsum("thi,shi->hts", queries, key_rows, preferred_element_type=jnp.float32)
    attn_weights = jnp.where(causal, scores, 0.0).astype(jnp.bfloat16)
    attended = jnp.einsum(
        "hts,shj->thj", attn_weights, val_rows, preferred_element_type=jnp.float32
    )
    attended = attended + jnp.einsum(
        "thi,hij->thj", queries, state_half, preferred_element_type=jnp.float32
    )
    normed = normalize(attended).astype(jnp.bfloat16).reshape(tok_rows, width)
    weight_rows = gathered.reshape(-1, out_weight.shape[1])
    projected = jnp.dot(normed, weight_rows, preferred_element_type=jnp.float32)
    grad_normed = lax.dot_general(
        out_grad, weight_rows, (((1,), (1,)), ((), ())), preferred_element_type=jnp.float32
    )
    mixed = lax.psum_scatter(
        projected.astype(jnp.bfloat16), "head", scatter_dimension=1, tiled=True
    )
    _, norm_back = jax.vjp(normalize, attended)
    grad_att = norm_back(grad_normed.reshape(tok_rows, heads_here, head_dim))[0].astype(
        jnp.bfloat16
    )
    grad_scores = jnp.einsum("thj,shj->hts", grad_att, val_rows, preferred_element_type=jnp.float32)
    grad_scores = jnp.where(causal, grad_scores, 0.0).astype(jnp.bfloat16)
    own_adjoint = jnp.einsum("thi,thj->hij", queries, grad_att, preferred_element_type=jnp.float32)
    later, adjoint_total = butterfly(own_adjoint, "seq", True)
    later_half = later.astype(jnp.bfloat16)
    grad_query = jnp.einsum(
        "hts,shi->thi", grad_scores, key_rows, preferred_element_type=jnp.float32
    )
    grad_query = grad_query + jnp.einsum(
        "thj,hij->thi", grad_att, state_half, preferred_element_type=jnp.float32
    )
    grad_key = jnp.einsum("hts,thi->shi", grad_scores, queries, preferred_element_type=jnp.float32)
    grad_key = grad_key + jnp.einsum(
        "thj,hij->thi", val_rows, later_half, preferred_element_type=jnp.float32
    )
    grad_value = jnp.einsum(
        "hts,thj->shj", attn_weights, grad_att, preferred_element_type=jnp.float32
    )
    grad_value = grad_value + jnp.einsum(
        "thi,hij->thj", key_rows, later_half, preferred_element_type=jnp.float32
    )
    init_grad = adjoint_total
    return (
        mixed,
        grad_query.reshape(tok_rows, width).astype(jnp.bfloat16),
        grad_key.reshape(tok_rows, width).astype(jnp.bfloat16),
        grad_value.reshape(tok_rows, width).astype(jnp.bfloat16),
        init_grad,
    )


def solution(mesh):
    return jax.shard_map(
        shards,
        mesh=mesh,
        in_specs=(
            P("seq", "head"),
            P("seq", "head"),
            P("seq", "head"),
            P("head", None, None),
            P(("head", "seq"), None),
            P("seq", None),
        ),
        out_specs=(
            P("seq", "head"),
            P("seq", "head"),
            P("seq", "head"),
            P("seq", "head"),
            P("head", None, None),
        ),
        check_vma=False,
    )
```

```python
import functools

import jax
import jax.numpy as jnp
from jax import lax
from jax.experimental import pallas as pl
from jax.experimental.pallas import tpu as pltpu
from jax.sharding import PartitionSpec as P

EPS = 1e-06


MESH = pl.DeviceIdType.MESH


def butterfly_kernel(count, backward, value_ref, partial_ref, total_ref, sendbuf, recvbuf, send_sem, recv_sem):
    me = lax.axis_index("seq")
    head = lax.axis_index("head")
    rounds = count.bit_length() - 1
    partners = []
    for k in range(rounds):
        step = 1 << k
        bit = (me // step) % 2
        partners.append((me + step - 2 * step * bit, bit))
    barrier = pltpu.get_barrier_semaphore()
    for partner, _ in partners:
        pl.semaphore_signal(barrier, inc=1, device_id=(partner, head), device_id_type=MESH)
    pl.semaphore_wait(barrier, rounds)
    total = value_ref[...]
    partial = jnp.zeros_like(total)
    for k, (partner, bit) in enumerate(partners):
        sent = total.astype(jnp.bfloat16)
        sendbuf[k] = sent
        copy = pltpu.make_async_remote_copy(
            src_ref=sendbuf.at[k],
            dst_ref=recvbuf.at[k],
            send_sem=send_sem.at[k],
            recv_sem=recv_sem.at[k],
            device_id=(partner, head),
            device_id_type=MESH,
        )
        copy.start()
        copy.wait()
        other = recvbuf[k].astype(jnp.float32)
        take = (bit == 0) if backward else (bit == 1)
        partial = jnp.where(take, partial + other, partial)
        total = sent.astype(jnp.float32) + other
    partial_ref[...] = partial
    total_ref[...] = total


def butterfly(value, axis, backward):
    count = lax.axis_size(axis)
    rounds = count.bit_length() - 1
    shape = jax.ShapeDtypeStruct(value.shape, jnp.float32)
    return pl.pallas_call(
        functools.partial(butterfly_kernel, count, backward),
        out_shape=(shape, shape),
        in_specs=[pl.BlockSpec(memory_space=pltpu.VMEM)],
        out_specs=(pl.BlockSpec(memory_space=pltpu.VMEM), pl.BlockSpec(memory_space=pltpu.VMEM)),
        scratch_shapes=[
            pltpu.VMEM((rounds,) + value.shape, jnp.bfloat16),
            pltpu.VMEM((rounds,) + value.shape, jnp.bfloat16),
            pltpu.SemaphoreType.DMA((rounds,)),
            pltpu.SemaphoreType.DMA((rounds,)),
        ],
        compiler_params=pltpu.CompilerParams(
            collective_id=1 if backward else 0, has_side_effects=True
        ),
    )(value.astype(jnp.float32))


def gather_kernel(ny, ca, value_ref, w_ref, rows_ref, partial_ref, sendbuf, recvbuf, send_sem, recv_sem, bf_send, bf_recv, local_sem):
    me = lax.axis_index("seq")
    head = lax.axis_index("head")
    count = lax.axis_size("seq")
    nz = count // ny
    y = me % ny
    z = me // ny
    piece, cols = w_ref.shape
    A = pl.ds(0, ca)
    B = pl.ds(ca, cols - ca)
    hy, hz = ny // 2, nz // 2
    hb = (cols - ca) // 2
    B1 = pl.ds(ca, hb)
    B2 = pl.ds(ca + hb, cols - ca - hb)

    def zz(k):
        return (z + nz + k) % nz

    def yy(k):
        return (y + ny + k) % ny

    def dev(zi, yi):
        return (zi * ny + yi, head)

    rounds = count.bit_length() - 1
    partners = []
    for k in range(rounds):
        step = 1 << k
        bit = (me // step) % 2
        partners.append((me + step - 2 * step * bit, bit))
    ring = [dev(z, yy(1)), dev(z, yy(-1)), dev(zz(1), y), dev(zz(-1), y)]
    barrier = pltpu.get_barrier_semaphore()
    for target in ring:
        pl.semaphore_signal(barrier, inc=1, device_id=target, device_id_type=MESH)
    for partner, _ in partners:
        pl.semaphore_signal(barrier, inc=1, device_id=(partner, head), device_id_type=MESH)
    pl.semaphore_wait(barrier, len(ring) + rounds)

    local = pltpu.make_async_copy(w_ref, rows_ref.at[z, y], local_sem)
    local.start()
    R = rows_ref
    yr, yl, zr, zl = dev(z, yy(1)), dev(z, yy(-1)), dev(zz(1), y), dev(zz(-1), y)
    ticks = [
        [(w_ref.at[:, A], R.at[z, y, :, A], yr), (w_ref.at[:, A], R.at[z, y, :, A], yl),
         (w_ref.at[:, B], R.at[z, y, :, B], zr), (w_ref.at[:, B], R.at[z, y, :, B], zl)],
        [(R.at[z, yy(-1), :, A], R.at[z, yy(-1), :, A], yr),
         (R.at[zz(-1), y, :, B], R.at[zz(-1), y, :, B], zr), (R.at[zz(1), y, :, B], R.at[zz(1), y, :, B], zl)],
        [(R.at[z, :, :, A], R.at[z, :, :, A], zr), (R.at[z, :, :, A], R.at[z, :, :, A], zl),
         (R.at[zz(-2), y, :, B], R.at[zz(-2), y, :, B], zr), (R.at[zz(2), y, :, B], R.at[zz(2), y, :, B], zl)],
        [(R.at[zz(-1), :, :, A], R.at[zz(-1), :, :, A], zr), (R.at[zz(1), :, :, A], R.at[zz(1), :, :, A], zl),
         (R.at[zz(-3), y, :, B1], R.at[zz(-3), y, :, B1], zr),
         (R.at[zz(3), y, :, B2], R.at[zz(3), y, :, B2], zl)],
        [(R.at[zz(-2), :, :, A], R.at[zz(-2), :, :, A], zr), (R.at[zz(2), :, :, A], R.at[zz(2), :, :, A], zl),
         (R.at[:, y, :, B], R.at[:, y, :, B], yr), (R.at[:, y, :, B], R.at[:, y, :, B], yl)],
        [(R.at[zz(-3), pl.ds(0, hy), :, A], R.at[zz(-3), pl.ds(0, hy), :, A], zr),
         (R.at[zz(3), pl.ds(hy, ny - hy), :, A], R.at[zz(3), pl.ds(hy, ny - hy), :, A], zl),
         (R.at[pl.ds(0, hz), yy(-1), :, B], R.at[pl.ds(0, hz), yy(-1), :, B], yr),
         (R.at[pl.ds(hz, nz - hz), yy(1), :, B], R.at[pl.ds(hz, nz - hz), yy(1), :, B], yl)],
    ]
    total = value_ref[...]
    partial = jnp.zeros_like(total)
    n = 0
    for t, moves in enumerate(ticks):
        if t == 2:
            local.wait()
        started = []
        for src, dst, target in moves:
            copy = pltpu.make_async_remote_copy(
                src_ref=src, dst_ref=dst, send_sem=send_sem.at[n], recv_sem=recv_sem.at[n],
                device_id=target, device_id_type=MESH,
            )
            copy.start()
            started.append(copy)
            n += 1
        scan = None
        if t < rounds:
            partner, bit = partners[t]
            sent = total.astype(jnp.bfloat16)
            sendbuf[t] = sent
            scan = pltpu.make_async_remote_copy(
                src_ref=sendbuf.at[t], dst_ref=recvbuf.at[t], send_sem=bf_send.at[t],
                recv_sem=bf_recv.at[t], device_id=(partner, head), device_id_type=MESH,
            )
            scan.start()
        for copy in started:
            copy.wait()
        if scan is not None:
            scan.wait()
            other = recvbuf[t].astype(jnp.float32)
            partial = jnp.where(bit == 1, partial + other, partial)
            total = sent.astype(jnp.float32) + other
    partial_ref[...] = partial


def gather_and_scan(value, weight):
    count = lax.axis_size("seq")
    ny = 4
    piece, cols = weight.shape
    rounds = count.bit_length() - 1
    ca = (cols * 2 // 3) // 128 * 128
    n_copies = 23
    return pl.pallas_call(
        functools.partial(gather_kernel, ny, ca),
        out_shape=(
            jax.ShapeDtypeStruct((count // ny, ny, piece, cols), weight.dtype),
            jax.ShapeDtypeStruct(value.shape, jnp.float32),
        ),
        in_specs=[pl.BlockSpec(memory_space=pltpu.VMEM), pl.BlockSpec(memory_space=pl.ANY)],
        out_specs=(pl.BlockSpec(memory_space=pl.ANY), pl.BlockSpec(memory_space=pltpu.VMEM)),
        scratch_shapes=[
            pltpu.VMEM((rounds,) + value.shape, jnp.bfloat16),
            pltpu.VMEM((rounds,) + value.shape, jnp.bfloat16),
            pltpu.SemaphoreType.DMA((n_copies,)),
            pltpu.SemaphoreType.DMA((n_copies,)),
            pltpu.SemaphoreType.DMA((rounds,)),
            pltpu.SemaphoreType.DMA((rounds,)),
            pltpu.SemaphoreType.DMA(()),
        ],
        compiler_params=pltpu.CompilerParams(collective_id=2, has_side_effects=True),
    )(value.astype(jnp.float32), weight)


def normalize(attended):
    return attended * lax.rsqrt(jnp.mean(attended * attended, axis=-1, keepdims=True) + EPS)


def shards(query, key, value, init_state, out_weight, out_grad):
    tok_rows = query.shape[0]
    width = query.shape[1]
    heads_here = init_state.shape[0]
    head_dim = init_state.shape[2]
    queries = query.reshape(tok_rows, heads_here, head_dim)
    key_rows = key.reshape(tok_rows, heads_here, head_dim)
    val_rows = value.reshape(tok_rows, heads_here, head_dim)
    local_state = jnp.einsum("thi,thj->hij", key_rows, val_rows, preferred_element_type=jnp.float32)
    half = out_weight.shape[1] // 2
    gathered, earlier = gather_and_scan(local_state, out_weight[:, :half])
    other_half = lax.all_gather(out_weight[:, half:], "seq", axis=0, tiled=True)
    state_half = (init_state + earlier).astype(jnp.bfloat16)
    row_index = lax.broadcasted_iota(jnp.int32, (tok_rows, tok_rows), 0)
    col_index = lax.broadcasted_iota(jnp.int32, (tok_rows, tok_rows), 1)
    causal = col_index <= row_index
    scores = jnp.einsum("thi,shi->hts", queries, key_rows, preferred_element_type=jnp.float32)
    attn_weights = jnp.where(causal, scores, 0.0).astype(jnp.bfloat16)
    attended = jnp.einsum(
        "hts,shj->thj", attn_weights, val_rows, preferred_element_type=jnp.float32
    )
    attended = attended + jnp.einsum(
        "thi,hij->thj", queries, state_half, preferred_element_type=jnp.float32
    )
    normed = normalize(attended).astype(jnp.bfloat16).reshape(tok_rows, width)
    weight_rows = jnp.concatenate([gathered.reshape(-1, half), other_half], axis=1)
    projected = jnp.dot(normed, weight_rows, preferred_element_type=jnp.float32)
    grad_normed = lax.dot_general(
        out_grad, weight_rows, (((1,), (1,)), ((), ())), preferred_element_type=jnp.float32
    )
    mixed = lax.psum_scatter(
        projected.astype(jnp.bfloat16), "head", scatter_dimension=1, tiled=True
    )
    _, norm_back = jax.vjp(normalize, attended)
    grad_att = norm_back(grad_normed.reshape(tok_rows, heads_here, head_dim))[0].astype(
        jnp.bfloat16
    )
    grad_scores = jnp.einsum("thj,shj->hts", grad_att, val_rows, preferred_element_type=jnp.float32)
    grad_scores = jnp.where(causal, grad_scores, 0.0).astype(jnp.bfloat16)
    own_adjoint = jnp.einsum("thi,thj->hij", queries, grad_att, preferred_element_type=jnp.float32)
    later, adjoint_total = butterfly(own_adjoint, "seq", True)
    later_half = later.astype(jnp.bfloat16)
    grad_query = jnp.einsum(
        "hts,shi->thi", grad_scores, key_rows, preferred_element_type=jnp.float32
    )
    grad_query = grad_query + jnp.einsum(
        "thj,hij->thi", grad_att, state_half, preferred_element_type=jnp.float32
    )
    grad_key = jnp.einsum("hts,thi->shi", grad_scores, queries, preferred_element_type=jnp.float32)
    grad_key = grad_key + jnp.einsum(
        "thj,hij->thi", val_rows, later_half, preferred_element_type=jnp.float32
    )
    grad_value = jnp.einsum(
        "hts,thj->shj", attn_weights, grad_att, preferred_element_type=jnp.float32
    )
    grad_value = grad_value + jnp.einsum(
        "thi,hij->thj", key_rows, later_half, preferred_element_type=jnp.float32
    )
    init_grad = adjoint_total
    return (
        mixed,
        grad_query.reshape(tok_rows, width).astype(jnp.bfloat16),
        grad_key.reshape(tok_rows, width).astype(jnp.bfloat16),
        grad_value.reshape(tok_rows, width).astype(jnp.bfloat16),
        init_grad,
    )


def solution(mesh):
    return jax.shard_map(
        shards,
        mesh=mesh,
        in_specs=(
            P("seq", "head"),
            P("seq", "head"),
            P("seq", "head"),
            P("head", None, None),
            P(("head", "seq"), None),
            P("seq", None),
        ),
        out_specs=(
            P("seq", "head"),
            P("seq", "head"),
            P("seq", "head"),
            P("seq", "head"),
            P("head", None, None),
        ),
        check_vma=False,
    )
```

```python
import functools

import jax
import jax.numpy as jnp
from jax import lax
from jax.experimental import pallas as pl
from jax.experimental.pallas import tpu as pltpu
from jax.sharding import PartitionSpec as P

EPS = 1e-06


MESH = pl.DeviceIdType.MESH


def butterfly_kernel(count, backward, value_ref, partial_ref, total_ref, sendbuf, recvbuf, send_sem, recv_sem):
    me = lax.axis_index("seq")
    head = lax.axis_index("head")
    rounds = count.bit_length() - 1
    partners = []
    for k in range(rounds):
        step = 1 << k
        bit = (me // step) % 2
        partners.append((me + step - 2 * step * bit, bit))
    barrier = pltpu.get_barrier_semaphore()
    for partner, _ in partners:
        pl.semaphore_signal(barrier, inc=1, device_id=(partner, head), device_id_type=MESH)
    pl.semaphore_wait(barrier, rounds)
    total = value_ref[...]
    partial = jnp.zeros_like(total)
    for k, (partner, bit) in enumerate(partners):
        sent = total.astype(jnp.bfloat16)
        sendbuf[k] = sent
        copy = pltpu.make_async_remote_copy(
            src_ref=sendbuf.at[k],
            dst_ref=recvbuf.at[k],
            send_sem=send_sem.at[k],
            recv_sem=recv_sem.at[k],
            device_id=(partner, head),
            device_id_type=MESH,
        )
        copy.start()
        copy.wait()
        other = recvbuf[k].astype(jnp.float32)
        take = (bit == 0) if backward else (bit == 1)
        partial = jnp.where(take, partial + other, partial)
        total = sent.astype(jnp.float32) + other
    partial_ref[...] = partial
    total_ref[...] = total


def butterfly(value, axis, backward):
    count = lax.axis_size(axis)
    rounds = count.bit_length() - 1
    shape = jax.ShapeDtypeStruct(value.shape, jnp.float32)
    return pl.pallas_call(
        functools.partial(butterfly_kernel, count, backward),
        out_shape=(shape, shape),
        in_specs=[pl.BlockSpec(memory_space=pltpu.VMEM)],
        out_specs=(pl.BlockSpec(memory_space=pltpu.VMEM), pl.BlockSpec(memory_space=pltpu.VMEM)),
        scratch_shapes=[
            pltpu.VMEM((rounds,) + value.shape, jnp.bfloat16),
            pltpu.VMEM((rounds,) + value.shape, jnp.bfloat16),
            pltpu.SemaphoreType.DMA((rounds,)),
            pltpu.SemaphoreType.DMA((rounds,)),
        ],
        compiler_params=pltpu.CompilerParams(
            collective_id=1 if backward else 0, has_side_effects=True
        ),
    )(value.astype(jnp.float32))


def backward_kernel(adj_ref, q_ref, k_ref, v_ref, ga_ref, sh_ref, gq_ref, gk_ref, gv_ref, total_ref,
                    sendbuf, recvbuf, send_sem, recv_sem, gk_acc, gv_acc):
    me = lax.axis_index("seq")
    head = lax.axis_index("head")
    count = lax.axis_size("seq")
    rounds = count.bit_length() - 1
    heads = sh_ref.shape[0]
    dim = sh_ref.shape[2]
    rows = q_ref.shape[0]
    partners = []
    for k in range(rounds):
        step = 1 << k
        bit = (me // step) % 2
        partners.append((me + step - 2 * step * bit, bit))
    barrier = pltpu.get_barrier_semaphore()
    for partner, _ in partners:
        pl.semaphore_signal(barrier, inc=1, device_id=(partner, head), device_id_type=MESH)
    pl.semaphore_wait(barrier, rounds)
    causal = lax.broadcasted_iota(jnp.int32, (rows, rows), 1) <= lax.broadcasted_iota(jnp.int32, (rows, rows), 0)
    nt = (((1,), (1,)), ((), ()))
    tn = (((0,), (0,)), ((), ()))

    def head_work(h):
        cols = pl.ds(h * dim, dim)
        qh, kh, vh, gah = q_ref[:, cols], k_ref[:, cols], v_ref[:, cols], ga_ref[:, cols]
        gs = lax.dot_general(gah, vh, nt, preferred_element_type=jnp.float32)
        gs = jnp.where(causal, gs, 0.0).astype(jnp.bfloat16)
        aw = lax.dot_general(qh, kh, nt, preferred_element_type=jnp.float32)
        aw = jnp.where(causal, aw, 0.0).astype(jnp.bfloat16)
        gq = jnp.dot(gs, kh, preferred_element_type=jnp.float32)
        gq = gq + lax.dot_general(gah, sh_ref[h], nt, preferred_element_type=jnp.float32)
        gq_ref[:, cols] = gq.astype(gq_ref.dtype)
        gk_acc[:, cols] = lax.dot_general(gs, qh, tn, preferred_element_type=jnp.float32)
        gv_acc[:, cols] = lax.dot_general(aw, gah, tn, preferred_element_type=jnp.float32)

    order = [[] for _ in range(rounds)]
    for h in range(heads):
        order[min(h, rounds - 1)].append(h)
    total = adj_ref[...]
    partial = jnp.zeros_like(total)
    for t, (partner, bit) in enumerate(partners):
        sent = total.astype(jnp.bfloat16)
        sendbuf[t] = sent
        copy = pltpu.make_async_remote_copy(
            src_ref=sendbuf.at[t], dst_ref=recvbuf.at[t], send_sem=send_sem.at[t],
            recv_sem=recv_sem.at[t], device_id=(partner, head), device_id_type=MESH,
        )
        copy.start()
        for h in order[t]:
            head_work(h)
        copy.wait()
        other = recvbuf[t].astype(jnp.float32)
        partial = jnp.where(bit == 0, partial + other, partial)
        total = sent.astype(jnp.float32) + other
    total_ref[...] = total
    later = partial.astype(jnp.bfloat16)
    for h in range(heads):
        cols = pl.ds(h * dim, dim)
        gk = gk_acc[:, cols] + lax.dot_general(v_ref[:, cols], later[h], nt, preferred_element_type=jnp.float32)
        gk_ref[:, cols] = gk.astype(gk_ref.dtype)
        gv = gv_acc[:, cols] + jnp.dot(k_ref[:, cols], later[h], preferred_element_type=jnp.float32)
        gv_ref[:, cols] = gv.astype(gv_ref.dtype)


def backward_pass(own_adjoint, query, key, value, grad_att, state_half):
    count = lax.axis_size("seq")
    rounds = count.bit_length() - 1
    tokens = jax.ShapeDtypeStruct(query.shape, jnp.bfloat16)
    vmem = pl.BlockSpec(memory_space=pltpu.VMEM)
    return pl.pallas_call(
        backward_kernel,
        out_shape=(tokens, tokens, tokens, jax.ShapeDtypeStruct(own_adjoint.shape, jnp.float32)),
        in_specs=[vmem] * 6,
        out_specs=(vmem, vmem, vmem, vmem),
        scratch_shapes=[
            pltpu.VMEM((rounds,) + own_adjoint.shape, jnp.bfloat16),
            pltpu.VMEM((rounds,) + own_adjoint.shape, jnp.bfloat16),
            pltpu.SemaphoreType.DMA((rounds,)),
            pltpu.SemaphoreType.DMA((rounds,)),
            pltpu.VMEM(query.shape, jnp.float32),
            pltpu.VMEM(query.shape, jnp.float32),
        ],
        compiler_params=pltpu.CompilerParams(collective_id=1, has_side_effects=True),
    )(own_adjoint, query, key, value, grad_att, state_half)


def gather_kernel(ny, ca, value_ref, w_ref, rows_ref, partial_ref, sendbuf, recvbuf, send_sem, recv_sem, bf_send, bf_recv, local_sem):
    me = lax.axis_index("seq")
    head = lax.axis_index("head")
    count = lax.axis_size("seq")
    nz = count // ny
    y = me % ny
    z = me // ny
    piece, cols = w_ref.shape
    A = pl.ds(0, ca)
    B = pl.ds(ca, cols - ca)
    hy, hz = ny // 2, nz // 2
    hb = (cols - ca) // 2
    B1 = pl.ds(ca, hb)
    B2 = pl.ds(ca + hb, cols - ca - hb)

    def zz(k):
        return (z + nz + k) % nz

    def yy(k):
        return (y + ny + k) % ny

    def dev(zi, yi):
        return (zi * ny + yi, head)

    rounds = count.bit_length() - 1
    partners = []
    for k in range(rounds):
        step = 1 << k
        bit = (me // step) % 2
        partners.append((me + step - 2 * step * bit, bit))
    ring = [dev(z, yy(1)), dev(z, yy(-1)), dev(zz(1), y), dev(zz(-1), y)]
    barrier = pltpu.get_barrier_semaphore()
    for target in ring:
        pl.semaphore_signal(barrier, inc=1, device_id=target, device_id_type=MESH)
    for partner, _ in partners:
        pl.semaphore_signal(barrier, inc=1, device_id=(partner, head), device_id_type=MESH)
    pl.semaphore_wait(barrier, len(ring) + rounds)

    local = pltpu.make_async_copy(w_ref, rows_ref.at[z, y], local_sem)
    local.start()
    R = rows_ref
    yr, yl, zr, zl = dev(z, yy(1)), dev(z, yy(-1)), dev(zz(1), y), dev(zz(-1), y)
    ticks = [
        [(w_ref.at[:, A], R.at[z, y, :, A], yr), (w_ref.at[:, A], R.at[z, y, :, A], yl),
         (w_ref.at[:, B], R.at[z, y, :, B], zr), (w_ref.at[:, B], R.at[z, y, :, B], zl)],
        [(R.at[z, yy(-1), :, A], R.at[z, yy(-1), :, A], yr),
         (R.at[zz(-1), y, :, B], R.at[zz(-1), y, :, B], zr), (R.at[zz(1), y, :, B], R.at[zz(1), y, :, B], zl)],
        [(R.at[z, :, :, A], R.at[z, :, :, A], zr), (R.at[z, :, :, A], R.at[z, :, :, A], zl),
         (R.at[zz(-2), y, :, B], R.at[zz(-2), y, :, B], zr), (R.at[zz(2), y, :, B], R.at[zz(2), y, :, B], zl)],
        [(R.at[zz(-1), :, :, A], R.at[zz(-1), :, :, A], zr), (R.at[zz(1), :, :, A], R.at[zz(1), :, :, A], zl),
         (R.at[zz(-3), y, :, B1], R.at[zz(-3), y, :, B1], zr),
         (R.at[zz(3), y, :, B2], R.at[zz(3), y, :, B2], zl)],
        [(R.at[zz(-2), :, :, A], R.at[zz(-2), :, :, A], zr), (R.at[zz(2), :, :, A], R.at[zz(2), :, :, A], zl),
         (R.at[:, y, :, B], R.at[:, y, :, B], yr), (R.at[:, y, :, B], R.at[:, y, :, B], yl)],
        [(R.at[zz(-3), pl.ds(0, hy), :, A], R.at[zz(-3), pl.ds(0, hy), :, A], zr),
         (R.at[zz(3), pl.ds(hy, ny - hy), :, A], R.at[zz(3), pl.ds(hy, ny - hy), :, A], zl),
         (R.at[pl.ds(0, hz), yy(-1), :, B], R.at[pl.ds(0, hz), yy(-1), :, B], yr),
         (R.at[pl.ds(hz, nz - hz), yy(1), :, B], R.at[pl.ds(hz, nz - hz), yy(1), :, B], yl)],
    ]
    total = value_ref[...]
    partial = jnp.zeros_like(total)
    n = 0
    for t, moves in enumerate(ticks):
        if t == 2:
            local.wait()
        started = []
        for src, dst, target in moves:
            copy = pltpu.make_async_remote_copy(
                src_ref=src, dst_ref=dst, send_sem=send_sem.at[n], recv_sem=recv_sem.at[n],
                device_id=target, device_id_type=MESH,
            )
            copy.start()
            started.append(copy)
            n += 1
        scan = None
        if t < rounds:
            partner, bit = partners[t]
            sent = total.astype(jnp.bfloat16)
            sendbuf[t] = sent
            scan = pltpu.make_async_remote_copy(
                src_ref=sendbuf.at[t], dst_ref=recvbuf.at[t], send_sem=bf_send.at[t],
                recv_sem=bf_recv.at[t], device_id=(partner, head), device_id_type=MESH,
            )
            scan.start()
        for copy in started:
            copy.wait()
        if scan is not None:
            scan.wait()
            other = recvbuf[t].astype(jnp.float32)
            partial = jnp.where(bit == 1, partial + other, partial)
            total = sent.astype(jnp.float32) + other
    partial_ref[...] = partial


def gather_and_scan(value, weight):
    count = lax.axis_size("seq")
    ny = 4
    piece, cols = weight.shape
    rounds = count.bit_length() - 1
    ca = (cols * 2 // 3) // 128 * 128
    n_copies = 23
    return pl.pallas_call(
        functools.partial(gather_kernel, ny, ca),
        out_shape=(
            jax.ShapeDtypeStruct((count // ny, ny, piece, cols), weight.dtype),
            jax.ShapeDtypeStruct(value.shape, jnp.float32),
        ),
        in_specs=[pl.BlockSpec(memory_space=pltpu.VMEM), pl.BlockSpec(memory_space=pl.ANY)],
        out_specs=(pl.BlockSpec(memory_space=pl.ANY), pl.BlockSpec(memory_space=pltpu.VMEM)),
        scratch_shapes=[
            pltpu.VMEM((rounds,) + value.shape, jnp.bfloat16),
            pltpu.VMEM((rounds,) + value.shape, jnp.bfloat16),
            pltpu.SemaphoreType.DMA((n_copies,)),
            pltpu.SemaphoreType.DMA((n_copies,)),
            pltpu.SemaphoreType.DMA((rounds,)),
            pltpu.SemaphoreType.DMA((rounds,)),
            pltpu.SemaphoreType.DMA(()),
        ],
        compiler_params=pltpu.CompilerParams(collective_id=2, has_side_effects=True),
    )(value.astype(jnp.float32), weight)


def normalize(attended):
    return attended * lax.rsqrt(jnp.mean(attended * attended, axis=-1, keepdims=True) + EPS)


def shards(query, key, value, init_state, out_weight, out_grad):
    tok_rows = query.shape[0]
    width = query.shape[1]
    heads_here = init_state.shape[0]
    head_dim = init_state.shape[2]
    queries = query.reshape(tok_rows, heads_here, head_dim)
    key_rows = key.reshape(tok_rows, heads_here, head_dim)
    val_rows = value.reshape(tok_rows, heads_here, head_dim)
    local_state = jnp.einsum("thi,thj->hij", key_rows, val_rows, preferred_element_type=jnp.float32)
    half = out_weight.shape[1] // 2
    gathered, earlier = gather_and_scan(local_state, out_weight[:, :half])
    other_half = lax.all_gather(out_weight[:, half:], "seq", axis=0, tiled=True)
    state_half = (init_state + earlier).astype(jnp.bfloat16)
    row_index = lax.broadcasted_iota(jnp.int32, (tok_rows, tok_rows), 0)
    col_index = lax.broadcasted_iota(jnp.int32, (tok_rows, tok_rows), 1)
    causal = col_index <= row_index
    scores = jnp.einsum("thi,shi->hts", queries, key_rows, preferred_element_type=jnp.float32)
    attn_weights = jnp.where(causal, scores, 0.0).astype(jnp.bfloat16)
    attended = jnp.einsum(
        "hts,shj->thj", attn_weights, val_rows, preferred_element_type=jnp.float32
    )
    attended = attended + jnp.einsum(
        "thi,hij->thj", queries, state_half, preferred_element_type=jnp.float32
    )
    normed = normalize(attended).astype(jnp.bfloat16).reshape(tok_rows, width)
    weight_rows = jnp.concatenate([gathered.reshape(-1, half), other_half], axis=1)
    projected = jnp.dot(normed, weight_rows, preferred_element_type=jnp.float32)
    grad_normed = lax.dot_general(
        out_grad, weight_rows, (((1,), (1,)), ((), ())), preferred_element_type=jnp.float32
    )
    mixed = lax.psum_scatter(
        projected.astype(jnp.bfloat16), "head", scatter_dimension=1, tiled=True
    )
    _, norm_back = jax.vjp(normalize, attended)
    grad_att = norm_back(grad_normed.reshape(tok_rows, heads_here, head_dim))[0].astype(
        jnp.bfloat16
    )
    own_adjoint = jnp.einsum("thi,thj->hij", queries, grad_att, preferred_element_type=jnp.float32)
    grad_query, grad_key, grad_value, init_grad = backward_pass(
        own_adjoint, query, key, value, grad_att.reshape(tok_rows, width), state_half
    )
    return (mixed, grad_query, grad_key, grad_value, init_grad)


def solution(mesh):
    return jax.shard_map(
        shards,
        mesh=mesh,
        in_specs=(
            P("seq", "head"),
            P("seq", "head"),
            P("seq", "head"),
            P("head", None, None),
            P(("head", "seq"), None),
            P("seq", None),
        ),
        out_specs=(
            P("seq", "head"),
            P("seq", "head"),
            P("seq", "head"),
            P("seq", "head"),
            P("head", None, None),
        ),
        check_vma=False,
    )
```

```python
import functools

import jax
import jax.numpy as jnp
from jax import lax
from jax.experimental import pallas as pl
from jax.experimental.pallas import tpu as pltpu
from jax.sharding import PartitionSpec as P

EPS = 1e-06


MESH = pl.DeviceIdType.MESH


def butterfly_kernel(count, backward, value_ref, partial_ref, total_ref, sendbuf, recvbuf, send_sem, recv_sem):
    me = lax.axis_index("seq")
    head = lax.axis_index("head")
    rounds = count.bit_length() - 1
    partners = []
    for k in range(rounds):
        step = 1 << k
        bit = (me // step) % 2
        partners.append((me + step - 2 * step * bit, bit))
    barrier = pltpu.get_barrier_semaphore()
    for partner, _ in partners:
        pl.semaphore_signal(barrier, inc=1, device_id=(partner, head), device_id_type=MESH)
    pl.semaphore_wait(barrier, rounds)
    total = value_ref[...]
    partial = jnp.zeros_like(total)
    for k, (partner, bit) in enumerate(partners):
        sent = total.astype(jnp.bfloat16)
        sendbuf[k] = sent
        copy = pltpu.make_async_remote_copy(
            src_ref=sendbuf.at[k],
            dst_ref=recvbuf.at[k],
            send_sem=send_sem.at[k],
            recv_sem=recv_sem.at[k],
            device_id=(partner, head),
            device_id_type=MESH,
        )
        copy.start()
        copy.wait()
        other = recvbuf[k].astype(jnp.float32)
        take = (bit == 0) if backward else (bit == 1)
        partial = jnp.where(take, partial + other, partial)
        total = sent.astype(jnp.float32) + other
    partial_ref[...] = partial
    total_ref[...] = total


def butterfly(value, axis, backward):
    count = lax.axis_size(axis)
    rounds = count.bit_length() - 1
    shape = jax.ShapeDtypeStruct(value.shape, jnp.float32)
    return pl.pallas_call(
        functools.partial(butterfly_kernel, count, backward),
        out_shape=(shape, shape),
        in_specs=[pl.BlockSpec(memory_space=pltpu.VMEM)],
        out_specs=(pl.BlockSpec(memory_space=pltpu.VMEM), pl.BlockSpec(memory_space=pltpu.VMEM)),
        scratch_shapes=[
            pltpu.VMEM((rounds,) + value.shape, jnp.bfloat16),
            pltpu.VMEM((rounds,) + value.shape, jnp.bfloat16),
            pltpu.SemaphoreType.DMA((rounds,)),
            pltpu.SemaphoreType.DMA((rounds,)),
        ],
        compiler_params=pltpu.CompilerParams(
            collective_id=1 if backward else 0, has_side_effects=True
        ),
    )(value.astype(jnp.float32))


def backward_kernel(adj_ref, q_ref, k_ref, v_ref, ga_ref, sh_ref, gq_ref, gk_acc, gv_acc, later_ref, total_ref,
                    sendbuf, recvbuf, send_sem, recv_sem):
    me = lax.axis_index("seq")
    head = lax.axis_index("head")
    count = lax.axis_size("seq")
    rounds = count.bit_length() - 1
    heads = sh_ref.shape[0]
    dim = sh_ref.shape[2]
    rows = q_ref.shape[0]
    partners = []
    for k in range(rounds):
        step = 1 << k
        bit = (me // step) % 2
        partners.append((me + step - 2 * step * bit, bit))
    barrier = pltpu.get_barrier_semaphore()
    for partner, _ in partners:
        pl.semaphore_signal(barrier, inc=1, device_id=(partner, head), device_id_type=MESH)
    pl.semaphore_wait(barrier, rounds)
    causal = lax.broadcasted_iota(jnp.int32, (rows, rows), 1) <= lax.broadcasted_iota(jnp.int32, (rows, rows), 0)
    nt = (((1,), (1,)), ((), ()))
    tn = (((0,), (0,)), ((), ()))

    def head_work(h):
        cols = pl.ds(h * dim, dim)
        qh, kh, vh, gah = q_ref[:, cols], k_ref[:, cols], v_ref[:, cols], ga_ref[:, cols]
        gs = lax.dot_general(gah, vh, nt, preferred_element_type=jnp.float32)
        gs = jnp.where(causal, gs, 0.0).astype(jnp.bfloat16)
        aw = lax.dot_general(qh, kh, nt, preferred_element_type=jnp.float32)
        aw = jnp.where(causal, aw, 0.0).astype(jnp.bfloat16)
        gq = jnp.dot(gs, kh, preferred_element_type=jnp.float32)
        gq = gq + lax.dot_general(gah, sh_ref[h], nt, preferred_element_type=jnp.float32)
        gq_ref[:, cols] = gq.astype(gq_ref.dtype)
        gk_acc[:, cols] = lax.dot_general(gs, qh, tn, preferred_element_type=jnp.float32)
        gv_acc[:, cols] = lax.dot_general(aw, gah, tn, preferred_element_type=jnp.float32)

    order = [[] for _ in range(rounds)]
    for h in range(heads):
        order[min(h, rounds - 1)].append(h)
    total = adj_ref[...]
    partial = jnp.zeros_like(total)
    for t, (partner, bit) in enumerate(partners):
        sent = total.astype(jnp.bfloat16)
        sendbuf[t] = sent
        copy = pltpu.make_async_remote_copy(
            src_ref=sendbuf.at[t], dst_ref=recvbuf.at[t], send_sem=send_sem.at[t],
            recv_sem=recv_sem.at[t], device_id=(partner, head), device_id_type=MESH,
        )
        copy.start()
        for h in order[t]:
            head_work(h)
        copy.wait()
        other = recvbuf[t].astype(jnp.float32)
        partial = jnp.where(bit == 0, partial + other, partial)
        total = sent.astype(jnp.float32) + other
    total_ref[...] = total
    later_ref[...] = partial.astype(later_ref.dtype)


def finish_kernel(gq_in, gk_acc, gv_acc, v_ref, k_ref, later_ref, gq_ref, gk_ref, gv_ref):
    heads, dim = later_ref.shape[0], later_ref.shape[2]
    nt = (((1,), (1,)), ((), ()))
    gq_ref[...] = gq_in[...]
    for h in range(heads):
        cols = pl.ds(h * dim, dim)
        later = later_ref[h]
        gk = gk_acc[:, cols] + lax.dot_general(v_ref[:, cols], later, nt, preferred_element_type=jnp.float32)
        gk_ref[:, cols] = gk.astype(gk_ref.dtype)
        gv = gv_acc[:, cols] + jnp.dot(k_ref[:, cols], later, preferred_element_type=jnp.float32)
        gv_ref[:, cols] = gv.astype(gv_ref.dtype)


def backward_pass(own_adjoint, query, key, value, grad_att, state_half):
    count = lax.axis_size("seq")
    rounds = count.bit_length() - 1
    tokens = jax.ShapeDtypeStruct(query.shape, jnp.bfloat16)
    vmem = pl.BlockSpec(memory_space=pltpu.VMEM)
    accs = jax.ShapeDtypeStruct(query.shape, jnp.float32)
    gq, gk_acc, gv_acc, later, total = pl.pallas_call(
        backward_kernel,
        out_shape=(tokens, accs, accs, jax.ShapeDtypeStruct(own_adjoint.shape, jnp.bfloat16),
                   jax.ShapeDtypeStruct(own_adjoint.shape, jnp.float32)),
        in_specs=[vmem] * 6,
        out_specs=(vmem,) * 5,
        scratch_shapes=[
            pltpu.VMEM((rounds,) + own_adjoint.shape, jnp.bfloat16),
            pltpu.VMEM((rounds,) + own_adjoint.shape, jnp.bfloat16),
            pltpu.SemaphoreType.DMA((rounds,)),
            pltpu.SemaphoreType.DMA((rounds,)),
        ],
        compiler_params=pltpu.CompilerParams(collective_id=1, has_side_effects=True),
    )(own_adjoint, query, key, value, grad_att, state_half)
    gq, gk, gv = pl.pallas_call(
        finish_kernel,
        out_shape=(tokens, tokens, tokens),
        in_specs=[vmem] * 6,
        out_specs=(vmem,) * 3,
    )(gq, gk_acc, gv_acc, value, key, later)
    return gq, gk, gv, total


def gather_kernel(ny, ca, value_ref, w_ref, rows_ref, partial_ref, sendbuf, recvbuf, send_sem, recv_sem, bf_send, bf_recv, local_sem):
    me = lax.axis_index("seq")
    head = lax.axis_index("head")
    count = lax.axis_size("seq")
    nz = count // ny
    y = me % ny
    z = me // ny
    piece, cols = w_ref.shape
    A = pl.ds(0, ca)
    B = pl.ds(ca, cols - ca)
    hy, hz = ny // 2, nz // 2
    hb = (cols - ca) // 2
    B1 = pl.ds(ca, hb)
    B2 = pl.ds(ca + hb, cols - ca - hb)

    def zz(k):
        return (z + nz + k) % nz

    def yy(k):
        return (y + ny + k) % ny

    def dev(zi, yi):
        return (zi * ny + yi, head)

    rounds = count.bit_length() - 1
    partners = []
    for k in range(rounds):
        step = 1 << k
        bit = (me // step) % 2
        partners.append((me + step - 2 * step * bit, bit))
    ring = [dev(z, yy(1)), dev(z, yy(-1)), dev(zz(1), y), dev(zz(-1), y)]
    barrier = pltpu.get_barrier_semaphore()
    for target in ring:
        pl.semaphore_signal(barrier, inc=1, device_id=target, device_id_type=MESH)
    for partner, _ in partners:
        pl.semaphore_signal(barrier, inc=1, device_id=(partner, head), device_id_type=MESH)
    pl.semaphore_wait(barrier, len(ring) + rounds)

    local = pltpu.make_async_copy(w_ref, rows_ref.at[z, y], local_sem)
    local.start()
    R = rows_ref
    yr, yl, zr, zl = dev(z, yy(1)), dev(z, yy(-1)), dev(zz(1), y), dev(zz(-1), y)
    ticks = [
        [(w_ref.at[:, A], R.at[z, y, :, A], yr), (w_ref.at[:, A], R.at[z, y, :, A], yl),
         (w_ref.at[:, B], R.at[z, y, :, B], zr), (w_ref.at[:, B], R.at[z, y, :, B], zl)],
        [(R.at[z, yy(-1), :, A], R.at[z, yy(-1), :, A], yr),
         (R.at[zz(-1), y, :, B], R.at[zz(-1), y, :, B], zr), (R.at[zz(1), y, :, B], R.at[zz(1), y, :, B], zl)],
        [(R.at[z, :, :, A], R.at[z, :, :, A], zr), (R.at[z, :, :, A], R.at[z, :, :, A], zl),
         (R.at[zz(-2), y, :, B], R.at[zz(-2), y, :, B], zr), (R.at[zz(2), y, :, B], R.at[zz(2), y, :, B], zl)],
        [(R.at[zz(-1), :, :, A], R.at[zz(-1), :, :, A], zr), (R.at[zz(1), :, :, A], R.at[zz(1), :, :, A], zl),
         (R.at[zz(-3), y, :, B1], R.at[zz(-3), y, :, B1], zr),
         (R.at[zz(3), y, :, B2], R.at[zz(3), y, :, B2], zl)],
        [(R.at[zz(-2), :, :, A], R.at[zz(-2), :, :, A], zr), (R.at[zz(2), :, :, A], R.at[zz(2), :, :, A], zl),
         (R.at[:, y, :, B], R.at[:, y, :, B], yr), (R.at[:, y, :, B], R.at[:, y, :, B], yl)],
        [(R.at[zz(-3), pl.ds(0, hy), :, A], R.at[zz(-3), pl.ds(0, hy), :, A], zr),
         (R.at[zz(3), pl.ds(hy, ny - hy), :, A], R.at[zz(3), pl.ds(hy, ny - hy), :, A], zl),
         (R.at[pl.ds(0, hz), yy(-1), :, B], R.at[pl.ds(0, hz), yy(-1), :, B], yr),
         (R.at[pl.ds(hz, nz - hz), yy(1), :, B], R.at[pl.ds(hz, nz - hz), yy(1), :, B], yl)],
    ]
    total = value_ref[...]
    partial = jnp.zeros_like(total)
    n = 0
    for t, moves in enumerate(ticks):
        if t == 2:
            local.wait()
        started = []
        for src, dst, target in moves:
            copy = pltpu.make_async_remote_copy(
                src_ref=src, dst_ref=dst, send_sem=send_sem.at[n], recv_sem=recv_sem.at[n],
                device_id=target, device_id_type=MESH,
            )
            copy.start()
            started.append(copy)
            n += 1
        scan = None
        if t < rounds:
            partner, bit = partners[t]
            sent = total.astype(jnp.bfloat16)
            sendbuf[t] = sent
            scan = pltpu.make_async_remote_copy(
                src_ref=sendbuf.at[t], dst_ref=recvbuf.at[t], send_sem=bf_send.at[t],
                recv_sem=bf_recv.at[t], device_id=(partner, head), device_id_type=MESH,
            )
            scan.start()
        for copy in started:
            copy.wait()
        if scan is not None:
            scan.wait()
            other = recvbuf[t].astype(jnp.float32)
            partial = jnp.where(bit == 1, partial + other, partial)
            total = sent.astype(jnp.float32) + other
    partial_ref[...] = partial


def gather_and_scan(value, weight):
    count = lax.axis_size("seq")
    ny = 4
    piece, cols = weight.shape
    rounds = count.bit_length() - 1
    ca = (cols * 2 // 3) // 128 * 128
    n_copies = 23
    return pl.pallas_call(
        functools.partial(gather_kernel, ny, ca),
        out_shape=(
            jax.ShapeDtypeStruct((count // ny, ny, piece, cols), weight.dtype),
            jax.ShapeDtypeStruct(value.shape, jnp.float32),
        ),
        in_specs=[pl.BlockSpec(memory_space=pltpu.VMEM), pl.BlockSpec(memory_space=pl.ANY)],
        out_specs=(pl.BlockSpec(memory_space=pl.ANY), pl.BlockSpec(memory_space=pltpu.VMEM)),
        scratch_shapes=[
            pltpu.VMEM((rounds,) + value.shape, jnp.bfloat16),
            pltpu.VMEM((rounds,) + value.shape, jnp.bfloat16),
            pltpu.SemaphoreType.DMA((n_copies,)),
            pltpu.SemaphoreType.DMA((n_copies,)),
            pltpu.SemaphoreType.DMA((rounds,)),
            pltpu.SemaphoreType.DMA((rounds,)),
            pltpu.SemaphoreType.DMA(()),
        ],
        compiler_params=pltpu.CompilerParams(collective_id=2, has_side_effects=True),
    )(value.astype(jnp.float32), weight)


def normalize(attended):
    return attended * lax.rsqrt(jnp.mean(attended * attended, axis=-1, keepdims=True) + EPS)


def shards(query, key, value, init_state, out_weight, out_grad):
    tok_rows = query.shape[0]
    width = query.shape[1]
    heads_here = init_state.shape[0]
    head_dim = init_state.shape[2]
    queries = query.reshape(tok_rows, heads_here, head_dim)
    key_rows = key.reshape(tok_rows, heads_here, head_dim)
    val_rows = value.reshape(tok_rows, heads_here, head_dim)
    local_state = jnp.einsum("thi,thj->hij", key_rows, val_rows, preferred_element_type=jnp.float32)
    half = out_weight.shape[1] // 2
    gathered, earlier = gather_and_scan(local_state, out_weight[:, :half])
    other_half = lax.all_gather(out_weight[:, half:], "seq", axis=0, tiled=True)
    state_half = (init_state + earlier).astype(jnp.bfloat16)
    row_index = lax.broadcasted_iota(jnp.int32, (tok_rows, tok_rows), 0)
    col_index = lax.broadcasted_iota(jnp.int32, (tok_rows, tok_rows), 1)
    causal = col_index <= row_index
    scores = jnp.einsum("thi,shi->hts", queries, key_rows, preferred_element_type=jnp.float32)
    attn_weights = jnp.where(causal, scores, 0.0).astype(jnp.bfloat16)
    attended = jnp.einsum(
        "hts,shj->thj", attn_weights, val_rows, preferred_element_type=jnp.float32
    )
    attended = attended + jnp.einsum(
        "thi,hij->thj", queries, state_half, preferred_element_type=jnp.float32
    )
    normed = normalize(attended).astype(jnp.bfloat16).reshape(tok_rows, width)
    weight_rows = jnp.concatenate([gathered.reshape(-1, half), other_half], axis=1)
    projected = jnp.dot(normed, weight_rows, preferred_element_type=jnp.float32).astype(jnp.bfloat16)
    projected, weight_rows = lax.optimization_barrier((projected, weight_rows))
    grad_normed = lax.dot_general(
        out_grad, weight_rows, (((1,), (1,)), ((), ())), preferred_element_type=jnp.float32
    )
    mixed = lax.psum_scatter(
        projected, "head", scatter_dimension=1, tiled=True
    )
    _, norm_back = jax.vjp(normalize, attended)
    grad_att = norm_back(grad_normed.reshape(tok_rows, heads_here, head_dim))[0].astype(
        jnp.bfloat16
    )
    own_adjoint = jnp.einsum("thi,thj->hij", queries, grad_att, preferred_element_type=jnp.float32)
    grad_query, grad_key, grad_value, init_grad = backward_pass(
        own_adjoint, query, key, value, grad_att.reshape(tok_rows, width), state_half
    )
    return (mixed, grad_query, grad_key, grad_value, init_grad)


def solution(mesh):
    return jax.shard_map(
        shards,
        mesh=mesh,
        in_specs=(
            P("seq", "head"),
            P("seq", "head"),
            P("seq", "head"),
            P("head", None, None),
            P(("head", "seq"), None),
            P("seq", None),
        ),
        out_specs=(
            P("seq", "head"),
            P("seq", "head"),
            P("seq", "head"),
            P("seq", "head"),
            P("head", None, None),
        ),
        check_vma=False,
    )
```

```python
import functools

import jax
import jax.numpy as jnp
from jax import lax
from jax.experimental import pallas as pl
from jax.experimental.pallas import tpu as pltpu
from jax.sharding import PartitionSpec as P

EPS = 1e-06


MESH = pl.DeviceIdType.MESH


def butterfly_kernel(count, backward, value_ref, partial_ref, total_ref, sendbuf, recvbuf, send_sem, recv_sem):
    me = lax.axis_index("seq")
    head = lax.axis_index("head")
    rounds = count.bit_length() - 1
    partners = []
    for k in range(rounds):
        step = 1 << k
        bit = (me // step) % 2
        partners.append((me + step - 2 * step * bit, bit))
    barrier = pltpu.get_barrier_semaphore()
    for partner, _ in partners:
        pl.semaphore_signal(barrier, inc=1, device_id=(partner, head), device_id_type=MESH)
    pl.semaphore_wait(barrier, rounds)
    total = value_ref[...]
    partial = jnp.zeros_like(total)
    for k, (partner, bit) in enumerate(partners):
        sent = total.astype(jnp.bfloat16)
        sendbuf[k] = sent
        copy = pltpu.make_async_remote_copy(
            src_ref=sendbuf.at[k],
            dst_ref=recvbuf.at[k],
            send_sem=send_sem.at[k],
            recv_sem=recv_sem.at[k],
            device_id=(partner, head),
            device_id_type=MESH,
        )
        copy.start()
        copy.wait()
        other = recvbuf[k].astype(jnp.float32)
        take = (bit == 0) if backward else (bit == 1)
        partial = jnp.where(take, partial + other, partial)
        total = sent.astype(jnp.float32) + other
    partial_ref[...] = partial
    total_ref[...] = total


def butterfly(value, axis, backward):
    count = lax.axis_size(axis)
    rounds = count.bit_length() - 1
    shape = jax.ShapeDtypeStruct(value.shape, jnp.float32)
    return pl.pallas_call(
        functools.partial(butterfly_kernel, count, backward),
        out_shape=(shape, shape),
        in_specs=[pl.BlockSpec(memory_space=pltpu.VMEM)],
        out_specs=(pl.BlockSpec(memory_space=pltpu.VMEM), pl.BlockSpec(memory_space=pltpu.VMEM)),
        scratch_shapes=[
            pltpu.VMEM((rounds,) + value.shape, jnp.bfloat16),
            pltpu.VMEM((rounds,) + value.shape, jnp.bfloat16),
            pltpu.SemaphoreType.DMA((rounds,)),
            pltpu.SemaphoreType.DMA((rounds,)),
        ],
        compiler_params=pltpu.CompilerParams(
            collective_id=1 if backward else 0, has_side_effects=True
        ),
    )(value.astype(jnp.float32))


def backward_kernel(adj_ref, q_ref, k_ref, v_ref, ga_ref, sh_ref, gq_ref, gk_acc, gv_acc, later_ref, total_ref,
                    sendbuf, recvbuf, send_sem, recv_sem):
    me = lax.axis_index("seq")
    head = lax.axis_index("head")
    count = lax.axis_size("seq")
    rounds = count.bit_length() - 1
    heads = sh_ref.shape[0]
    dim = sh_ref.shape[2]
    rows = q_ref.shape[0]
    partners = []
    for k in range(rounds):
        step = 1 << k
        bit = (me // step) % 2
        partners.append((me + step - 2 * step * bit, bit))
    barrier = pltpu.get_barrier_semaphore()
    for partner, _ in partners:
        pl.semaphore_signal(barrier, inc=1, device_id=(partner, head), device_id_type=MESH)
    pl.semaphore_wait(barrier, rounds)
    causal = lax.broadcasted_iota(jnp.int32, (rows, rows), 1) <= lax.broadcasted_iota(jnp.int32, (rows, rows), 0)
    nt = (((1,), (1,)), ((), ()))
    tn = (((0,), (0,)), ((), ()))

    def head_work(h):
        cols = pl.ds(h * dim, dim)
        qh, kh, vh, gah = q_ref[:, cols], k_ref[:, cols], v_ref[:, cols], ga_ref[:, cols]
        gs = lax.dot_general(gah, vh, nt, preferred_element_type=jnp.float32)
        gs = jnp.where(causal, gs, 0.0).astype(jnp.bfloat16)
        aw = lax.dot_general(qh, kh, nt, preferred_element_type=jnp.float32)
        aw = jnp.where(causal, aw, 0.0).astype(jnp.bfloat16)
        gq = jnp.dot(gs, kh, preferred_element_type=jnp.float32)
        gq = gq + lax.dot_general(gah, sh_ref[h], nt, preferred_element_type=jnp.float32)
        gq_ref[:, cols] = gq.astype(gq_ref.dtype)
        gk_acc[:, cols] = lax.dot_general(gs, qh, tn, preferred_element_type=jnp.float32)
        gv_acc[:, cols] = lax.dot_general(aw, gah, tn, preferred_element_type=jnp.float32)

    order = [[] for _ in range(rounds)]
    for h in range(heads):
        order[min(h, rounds - 1)].append(h)
    total = adj_ref[...]
    partial = jnp.zeros_like(total)
    for t, (partner, bit) in enumerate(partners):
        sent = total.astype(jnp.bfloat16)
        sendbuf[t] = sent
        copy = pltpu.make_async_remote_copy(
            src_ref=sendbuf.at[t], dst_ref=recvbuf.at[t], send_sem=send_sem.at[t],
            recv_sem=recv_sem.at[t], device_id=(partner, head), device_id_type=MESH,
        )
        copy.start()
        for h in order[t]:
            head_work(h)
        copy.wait()
        other = recvbuf[t].astype(jnp.float32)
        partial = jnp.where(bit == 0, partial + other, partial)
        total = sent.astype(jnp.float32) + other
    total_ref[...] = total
    later_ref[...] = partial.astype(later_ref.dtype)


def finish_kernel(gq_in, gk_acc, gv_acc, v_ref, k_ref, later_ref, gq_ref, gk_ref, gv_ref):
    heads, dim = later_ref.shape[0], later_ref.shape[2]
    nt = (((1,), (1,)), ((), ()))
    gq_ref[...] = gq_in[...]
    for h in range(heads):
        cols = pl.ds(h * dim, dim)
        later = later_ref[h]
        gk = gk_acc[:, cols] + lax.dot_general(v_ref[:, cols], later, nt, preferred_element_type=jnp.float32)
        gk_ref[:, cols] = gk.astype(gk_ref.dtype)
        gv = gv_acc[:, cols] + jnp.dot(k_ref[:, cols], later, preferred_element_type=jnp.float32)
        gv_ref[:, cols] = gv.astype(gv_ref.dtype)


def backward_pass(own_adjoint, query, key, value, grad_att, state_half):
    count = lax.axis_size("seq")
    rounds = count.bit_length() - 1
    tokens = jax.ShapeDtypeStruct(query.shape, jnp.bfloat16)
    vmem = pl.BlockSpec(memory_space=pltpu.VMEM)
    accs = jax.ShapeDtypeStruct(query.shape, jnp.float32)
    gq, gk_acc, gv_acc, later, total = pl.pallas_call(
        backward_kernel,
        out_shape=(tokens, accs, accs, jax.ShapeDtypeStruct(own_adjoint.shape, jnp.bfloat16),
                   jax.ShapeDtypeStruct(own_adjoint.shape, jnp.float32)),
        in_specs=[vmem] * 6,
        out_specs=(vmem,) * 5,
        scratch_shapes=[
            pltpu.VMEM((rounds,) + own_adjoint.shape, jnp.bfloat16),
            pltpu.VMEM((rounds,) + own_adjoint.shape, jnp.bfloat16),
            pltpu.SemaphoreType.DMA((rounds,)),
            pltpu.SemaphoreType.DMA((rounds,)),
        ],
        compiler_params=pltpu.CompilerParams(collective_id=1, has_side_effects=True),
    )(own_adjoint, query, key, value, grad_att, state_half)
    gq, gk, gv = pl.pallas_call(
        finish_kernel,
        out_shape=(tokens, tokens, tokens),
        in_specs=[vmem] * 6,
        out_specs=(vmem,) * 3,
    )(gq, gk_acc, gv_acc, value, key, later)
    return gq, gk, gv, total


def gather_kernel(ny, ca, value_ref, w_ref, rows_ref, partial_ref, sendbuf, recvbuf, send_sem, recv_sem, bf_send, bf_recv, local_sem):
    me = lax.axis_index("seq")
    head = lax.axis_index("head")
    count = lax.axis_size("seq")
    nz = count // ny
    y = me % ny
    z = me // ny
    piece, cols = w_ref.shape
    A = pl.ds(0, ca)
    B = pl.ds(ca, cols - ca)
    hy, hz = ny // 2, nz // 2
    hb = (cols - ca) // 2
    B1 = pl.ds(ca, hb)
    B2 = pl.ds(ca + hb, cols - ca - hb)

    def zz(k):
        return (z + nz + k) % nz

    def yy(k):
        return (y + ny + k) % ny

    def dev(zi, yi):
        return (zi * ny + yi, head)

    rounds = count.bit_length() - 1
    partners = []
    for k in range(rounds):
        step = 1 << k
        bit = (me // step) % 2
        partners.append((me + step - 2 * step * bit, bit))
    ring = [dev(z, yy(1)), dev(z, yy(-1)), dev(zz(1), y), dev(zz(-1), y)]
    barrier = pltpu.get_barrier_semaphore()
    for target in ring:
        pl.semaphore_signal(barrier, inc=1, device_id=target, device_id_type=MESH)
    for partner, _ in partners:
        pl.semaphore_signal(barrier, inc=1, device_id=(partner, head), device_id_type=MESH)
    pl.semaphore_wait(barrier, len(ring) + rounds)

    local = pltpu.make_async_copy(w_ref, rows_ref.at[z, y], local_sem)
    local.start()
    R = rows_ref
    yr, yl, zr, zl = dev(z, yy(1)), dev(z, yy(-1)), dev(zz(1), y), dev(zz(-1), y)
    ticks = [
        [(w_ref.at[:, A], R.at[z, y, :, A], yr), (w_ref.at[:, A], R.at[z, y, :, A], yl),
         (w_ref.at[:, B], R.at[z, y, :, B], zr), (w_ref.at[:, B], R.at[z, y, :, B], zl)],
        [(R.at[z, yy(-1), :, A], R.at[z, yy(-1), :, A], yr),
         (R.at[zz(-1), y, :, B], R.at[zz(-1), y, :, B], zr), (R.at[zz(1), y, :, B], R.at[zz(1), y, :, B], zl)],
        [(R.at[z, :, :, A], R.at[z, :, :, A], zr), (R.at[z, :, :, A], R.at[z, :, :, A], zl),
         (R.at[zz(-2), y, :, B], R.at[zz(-2), y, :, B], zr), (R.at[zz(2), y, :, B], R.at[zz(2), y, :, B], zl)],
        [(R.at[zz(-1), :, :, A], R.at[zz(-1), :, :, A], zr), (R.at[zz(1), :, :, A], R.at[zz(1), :, :, A], zl),
         (R.at[zz(-3), y, :, B1], R.at[zz(-3), y, :, B1], zr),
         (R.at[zz(3), y, :, B2], R.at[zz(3), y, :, B2], zl)],
        [(R.at[zz(-2), :, :, A], R.at[zz(-2), :, :, A], zr), (R.at[zz(2), :, :, A], R.at[zz(2), :, :, A], zl),
         (R.at[:, y, :, B], R.at[:, y, :, B], yr), (R.at[:, y, :, B], R.at[:, y, :, B], yl)],
        [(R.at[zz(-3), pl.ds(0, hy), :, A], R.at[zz(-3), pl.ds(0, hy), :, A], zr),
         (R.at[zz(3), pl.ds(hy, ny - hy), :, A], R.at[zz(3), pl.ds(hy, ny - hy), :, A], zl),
         (R.at[pl.ds(0, hz), yy(-1), :, B], R.at[pl.ds(0, hz), yy(-1), :, B], yr),
         (R.at[pl.ds(hz, nz - hz), yy(1), :, B], R.at[pl.ds(hz, nz - hz), yy(1), :, B], yl)],
    ]
    total = value_ref[...]
    partial = jnp.zeros_like(total)
    n = 0
    for t, moves in enumerate(ticks):
        if t == 2:
            local.wait()
        started = []
        for src, dst, target in moves:
            copy = pltpu.make_async_remote_copy(
                src_ref=src, dst_ref=dst, send_sem=send_sem.at[n], recv_sem=recv_sem.at[n],
                device_id=target, device_id_type=MESH,
            )
            copy.start()
            started.append(copy)
            n += 1
        scan = None
        if t < rounds:
            partner, bit = partners[t]
            sent = total.astype(jnp.bfloat16)
            sendbuf[t] = sent
            scan = pltpu.make_async_remote_copy(
                src_ref=sendbuf.at[t], dst_ref=recvbuf.at[t], send_sem=bf_send.at[t],
                recv_sem=bf_recv.at[t], device_id=(partner, head), device_id_type=MESH,
            )
            scan.start()
        for copy in started:
            copy.wait()
        if scan is not None:
            scan.wait()
            other = recvbuf[t].astype(jnp.float32)
            partial = jnp.where(bit == 1, partial + other, partial)
            total = sent.astype(jnp.float32) + other
    partial_ref[...] = partial


def gather_and_scan(value, weight):
    count = lax.axis_size("seq")
    ny = 4
    piece, cols = weight.shape
    rounds = count.bit_length() - 1
    ca = (cols * 2 // 3) // 128 * 128
    n_copies = 23
    return pl.pallas_call(
        functools.partial(gather_kernel, ny, ca),
        out_shape=(
            jax.ShapeDtypeStruct((count // ny, ny, piece, cols), weight.dtype),
            jax.ShapeDtypeStruct(value.shape, jnp.float32),
        ),
        in_specs=[pl.BlockSpec(memory_space=pltpu.VMEM), pl.BlockSpec(memory_space=pl.ANY)],
        out_specs=(pl.BlockSpec(memory_space=pl.ANY), pl.BlockSpec(memory_space=pltpu.VMEM)),
        scratch_shapes=[
            pltpu.VMEM((rounds,) + value.shape, jnp.bfloat16),
            pltpu.VMEM((rounds,) + value.shape, jnp.bfloat16),
            pltpu.SemaphoreType.DMA((n_copies,)),
            pltpu.SemaphoreType.DMA((n_copies,)),
            pltpu.SemaphoreType.DMA((rounds,)),
            pltpu.SemaphoreType.DMA((rounds,)),
            pltpu.SemaphoreType.DMA(()),
        ],
        compiler_params=pltpu.CompilerParams(collective_id=2, has_side_effects=True),
    )(value.astype(jnp.float32), weight)


def normalize(attended):
    return attended * lax.rsqrt(jnp.mean(attended * attended, axis=-1, keepdims=True) + EPS)


def shards(query, key, value, init_state, out_weight, out_grad):
    tok_rows = query.shape[0]
    width = query.shape[1]
    heads_here = init_state.shape[0]
    head_dim = init_state.shape[2]
    queries = query.reshape(tok_rows, heads_here, head_dim)
    key_rows = key.reshape(tok_rows, heads_here, head_dim)
    val_rows = value.reshape(tok_rows, heads_here, head_dim)
    local_state = jnp.einsum("thi,thj->hij", key_rows, val_rows, preferred_element_type=jnp.float32)
    half = out_weight.shape[1] // 2
    gathered, earlier = gather_and_scan(local_state, out_weight[:, :half])
    other_half = lax.all_gather(out_weight[:, half:], "seq", axis=0, tiled=True)
    state_half = (init_state + earlier).astype(jnp.bfloat16)
    row_index = lax.broadcasted_iota(jnp.int32, (tok_rows, tok_rows), 0)
    col_index = lax.broadcasted_iota(jnp.int32, (tok_rows, tok_rows), 1)
    causal = col_index <= row_index
    scores = jnp.einsum("thi,shi->hts", queries, key_rows, preferred_element_type=jnp.float32)
    attn_weights = jnp.where(causal, scores, 0.0).astype(jnp.bfloat16)
    attended = jnp.einsum(
        "hts,shj->thj", attn_weights, val_rows, preferred_element_type=jnp.float32
    )
    attended = attended + jnp.einsum(
        "thi,hij->thj", queries, state_half, preferred_element_type=jnp.float32
    )
    normed = normalize(attended).astype(jnp.bfloat16).reshape(tok_rows, width)
    first_rows = gathered.reshape(-1, half)
    weight_rows = jnp.concatenate([first_rows, other_half], axis=1)
    projected = jnp.dot(normed, weight_rows, preferred_element_type=jnp.float32).astype(jnp.bfloat16)
    projected, first_rows, other_half = lax.optimization_barrier((projected, first_rows, other_half))
    contract = (((1,), (1,)), ((), ()))
    grad_normed = lax.dot_general(
        out_grad[:, :half], first_rows, contract, preferred_element_type=jnp.float32
    ) + lax.dot_general(out_grad[:, half:], other_half, contract, preferred_element_type=jnp.float32)
    mixed = lax.psum_scatter(
        projected, "head", scatter_dimension=1, tiled=True
    )
    _, norm_back = jax.vjp(normalize, attended)
    grad_att = norm_back(grad_normed.reshape(tok_rows, heads_here, head_dim))[0].astype(
        jnp.bfloat16
    )
    own_adjoint = jnp.einsum("thi,thj->hij", queries, grad_att, preferred_element_type=jnp.float32)
    grad_query, grad_key, grad_value, init_grad = backward_pass(
        own_adjoint, query, key, value, grad_att.reshape(tok_rows, width), state_half
    )
    return (mixed, grad_query, grad_key, grad_value, init_grad)


def solution(mesh):
    return jax.shard_map(
        shards,
        mesh=mesh,
        in_specs=(
            P("seq", "head"),
            P("seq", "head"),
            P("seq", "head"),
            P("head", None, None),
            P(("head", "seq"), None),
            P("seq", None),
        ),
        out_specs=(
            P("seq", "head"),
            P("seq", "head"),
            P("seq", "head"),
            P("seq", "head"),
            P("head", None, None),
        ),
        check_vma=False,
    )
```

```python
import functools

import jax
import jax.numpy as jnp
from jax import lax
from jax.experimental import pallas as pl
from jax.experimental.pallas import tpu as pltpu
from jax.sharding import PartitionSpec as P

EPS = 1e-06


MESH = pl.DeviceIdType.MESH


def butterfly_kernel(count, backward, value_ref, partial_ref, total_ref, sendbuf, recvbuf, send_sem, recv_sem):
    me = lax.axis_index("seq")
    head = lax.axis_index("head")
    rounds = count.bit_length() - 1
    partners = []
    for k in range(rounds):
        step = 1 << k
        bit = (me // step) % 2
        partners.append((me + step - 2 * step * bit, bit))
    barrier = pltpu.get_barrier_semaphore()
    for partner, _ in partners:
        pl.semaphore_signal(barrier, inc=1, device_id=(partner, head), device_id_type=MESH)
    pl.semaphore_wait(barrier, rounds)
    total = value_ref[...]
    partial = jnp.zeros_like(total)
    for k, (partner, bit) in enumerate(partners):
        sent = total.astype(jnp.bfloat16)
        sendbuf[k] = sent
        copy = pltpu.make_async_remote_copy(
            src_ref=sendbuf.at[k],
            dst_ref=recvbuf.at[k],
            send_sem=send_sem.at[k],
            recv_sem=recv_sem.at[k],
            device_id=(partner, head),
            device_id_type=MESH,
        )
        copy.start()
        copy.wait()
        other = recvbuf[k].astype(jnp.float32)
        take = (bit == 0) if backward else (bit == 1)
        partial = jnp.where(take, partial + other, partial)
        total = sent.astype(jnp.float32) + other
    partial_ref[...] = partial
    total_ref[...] = total


def butterfly(value, axis, backward):
    count = lax.axis_size(axis)
    rounds = count.bit_length() - 1
    shape = jax.ShapeDtypeStruct(value.shape, jnp.float32)
    return pl.pallas_call(
        functools.partial(butterfly_kernel, count, backward),
        out_shape=(shape, shape),
        in_specs=[pl.BlockSpec(memory_space=pltpu.VMEM)],
        out_specs=(pl.BlockSpec(memory_space=pltpu.VMEM), pl.BlockSpec(memory_space=pltpu.VMEM)),
        scratch_shapes=[
            pltpu.VMEM((rounds,) + value.shape, jnp.bfloat16),
            pltpu.VMEM((rounds,) + value.shape, jnp.bfloat16),
            pltpu.SemaphoreType.DMA((rounds,)),
            pltpu.SemaphoreType.DMA((rounds,)),
        ],
        compiler_params=pltpu.CompilerParams(
            collective_id=1 if backward else 0, has_side_effects=True
        ),
    )(value.astype(jnp.float32))


def backward_kernel(adj_ref, q_ref, k_ref, v_ref, ga_ref, sh_ref, gq_ref, gk_acc, gv_acc, later_ref, total_ref,
                    sendbuf, recvbuf, send_sem, recv_sem):
    me = lax.axis_index("seq")
    head = lax.axis_index("head")
    count = lax.axis_size("seq")
    rounds = count.bit_length() - 1
    heads = sh_ref.shape[0]
    dim = sh_ref.shape[2]
    rows = q_ref.shape[0]
    partners = []
    for k in range(rounds):
        step = 1 << k
        bit = (me // step) % 2
        partners.append((me + step - 2 * step * bit, bit))
    barrier = pltpu.get_barrier_semaphore()
    for partner, _ in partners:
        pl.semaphore_signal(barrier, inc=1, device_id=(partner, head), device_id_type=MESH)
    pl.semaphore_wait(barrier, rounds)
    causal = lax.broadcasted_iota(jnp.int32, (rows, rows), 1) <= lax.broadcasted_iota(jnp.int32, (rows, rows), 0)
    nt = (((1,), (1,)), ((), ()))
    tn = (((0,), (0,)), ((), ()))

    def head_work(h):
        cols = pl.ds(h * dim, dim)
        qh, kh, vh, gah = q_ref[:, cols], k_ref[:, cols], v_ref[:, cols], ga_ref[:, cols]
        gs = lax.dot_general(gah, vh, nt, preferred_element_type=jnp.float32)
        gs = jnp.where(causal, gs, 0.0).astype(jnp.bfloat16)
        aw = lax.dot_general(qh, kh, nt, preferred_element_type=jnp.float32)
        aw = jnp.where(causal, aw, 0.0).astype(jnp.bfloat16)
        gq = jnp.dot(gs, kh, preferred_element_type=jnp.float32)
        gq = gq + lax.dot_general(gah, sh_ref[h], nt, preferred_element_type=jnp.float32)
        gq_ref[:, cols] = gq.astype(gq_ref.dtype)
        gk_acc[:, cols] = lax.dot_general(gs, qh, tn, preferred_element_type=jnp.float32)
        gv_acc[:, cols] = lax.dot_general(aw, gah, tn, preferred_element_type=jnp.float32)

    order = [[] for _ in range(rounds)]
    for h in range(heads):
        order[min(h, rounds - 1)].append(h)
    total = adj_ref[...]
    partial = jnp.zeros_like(total)
    for t, (partner, bit) in enumerate(partners):
        sent = total.astype(jnp.bfloat16)
        sendbuf[t] = sent
        copy = pltpu.make_async_remote_copy(
            src_ref=sendbuf.at[t], dst_ref=recvbuf.at[t], send_sem=send_sem.at[t],
            recv_sem=recv_sem.at[t], device_id=(partner, head), device_id_type=MESH,
        )
        copy.start()
        for h in order[t]:
            head_work(h)
        copy.wait()
        other = recvbuf[t].astype(jnp.float32)
        partial = jnp.where(bit == 0, partial + other, partial)
        total = sent.astype(jnp.float32) + other
    total_ref[...] = total
    later_ref[...] = partial.astype(later_ref.dtype)


def finish_kernel(gq_in, gk_acc, gv_acc, v_ref, k_ref, later_ref, gq_ref, gk_ref, gv_ref):
    heads, dim = later_ref.shape[0], later_ref.shape[2]
    nt = (((1,), (1,)), ((), ()))
    gq_ref[...] = gq_in[...]
    for h in range(heads):
        cols = pl.ds(h * dim, dim)
        later = later_ref[h]
        gk = gk_acc[:, cols] + lax.dot_general(v_ref[:, cols], later, nt, preferred_element_type=jnp.float32)
        gk_ref[:, cols] = gk.astype(gk_ref.dtype)
        gv = gv_acc[:, cols] + jnp.dot(k_ref[:, cols], later, preferred_element_type=jnp.float32)
        gv_ref[:, cols] = gv.astype(gv_ref.dtype)


def backward_pass(own_adjoint, query, key, value, grad_att, state_half):
    count = lax.axis_size("seq")
    rounds = count.bit_length() - 1
    tokens = jax.ShapeDtypeStruct(query.shape, jnp.bfloat16)
    vmem = pl.BlockSpec(memory_space=pltpu.VMEM)
    accs = jax.ShapeDtypeStruct(query.shape, jnp.float32)
    gq, gk_acc, gv_acc, later, total = pl.pallas_call(
        backward_kernel,
        out_shape=(tokens, accs, accs, jax.ShapeDtypeStruct(own_adjoint.shape, jnp.bfloat16),
                   jax.ShapeDtypeStruct(own_adjoint.shape, jnp.float32)),
        in_specs=[vmem] * 6,
        out_specs=(vmem,) * 5,
        scratch_shapes=[
            pltpu.VMEM((rounds,) + own_adjoint.shape, jnp.bfloat16),
            pltpu.VMEM((rounds,) + own_adjoint.shape, jnp.bfloat16),
            pltpu.SemaphoreType.DMA((rounds,)),
            pltpu.SemaphoreType.DMA((rounds,)),
        ],
        compiler_params=pltpu.CompilerParams(collective_id=1, has_side_effects=True),
    )(own_adjoint, query, key, value, grad_att, state_half)
    gq, gk, gv = pl.pallas_call(
        finish_kernel,
        out_shape=(tokens, tokens, tokens),
        in_specs=[vmem] * 6,
        out_specs=(vmem,) * 3,
    )(gq, gk_acc, gv_acc, value, key, later)
    return gq, gk, gv, total


def gather_kernel(ny, ca, value_ref, init_ref, q_ref, k_ref, v_ref, w_ref, rows_ref, normed_ref, att_ref, sh_ref,
                  sendbuf, recvbuf, send_sem, recv_sem, bf_send, bf_recv, local_sem):
    me = lax.axis_index("seq")
    head = lax.axis_index("head")
    count = lax.axis_size("seq")
    nz = count // ny
    y = me % ny
    z = me // ny
    piece, cols = w_ref.shape
    A = pl.ds(0, ca)
    B = pl.ds(ca, cols - ca)
    hy, hz = ny // 2, nz // 2
    hb = (cols - ca) // 2
    B1 = pl.ds(ca, hb)
    B2 = pl.ds(ca + hb, cols - ca - hb)

    def zz(k):
        return (z + nz + k) % nz

    def yy(k):
        return (y + ny + k) % ny

    def dev(zi, yi):
        return (zi * ny + yi, head)

    rounds = count.bit_length() - 1
    partners = []
    for k in range(rounds):
        step = 1 << k
        bit = (me // step) % 2
        partners.append((me + step - 2 * step * bit, bit))
    ring = [dev(z, yy(1)), dev(z, yy(-1)), dev(zz(1), y), dev(zz(-1), y)]
    barrier = pltpu.get_barrier_semaphore()
    for target in ring:
        pl.semaphore_signal(barrier, inc=1, device_id=target, device_id_type=MESH)
    for partner, _ in partners:
        pl.semaphore_signal(barrier, inc=1, device_id=(partner, head), device_id_type=MESH)
    pl.semaphore_wait(barrier, len(ring) + rounds)

    local = pltpu.make_async_copy(w_ref, rows_ref.at[z, y], local_sem)
    local.start()
    R = rows_ref
    yr, yl, zr, zl = dev(z, yy(1)), dev(z, yy(-1)), dev(zz(1), y), dev(zz(-1), y)
    ticks = [
        [(w_ref.at[:, A], R.at[z, y, :, A], yr), (w_ref.at[:, A], R.at[z, y, :, A], yl),
         (w_ref.at[:, B], R.at[z, y, :, B], zr), (w_ref.at[:, B], R.at[z, y, :, B], zl)],
        [(R.at[z, yy(-1), :, A], R.at[z, yy(-1), :, A], yr),
         (R.at[zz(-1), y, :, B], R.at[zz(-1), y, :, B], zr), (R.at[zz(1), y, :, B], R.at[zz(1), y, :, B], zl)],
        [(R.at[z, :, :, A], R.at[z, :, :, A], zr), (R.at[z, :, :, A], R.at[z, :, :, A], zl),
         (R.at[zz(-2), y, :, B], R.at[zz(-2), y, :, B], zr), (R.at[zz(2), y, :, B], R.at[zz(2), y, :, B], zl)],
        [(R.at[zz(-1), :, :, A], R.at[zz(-1), :, :, A], zr), (R.at[zz(1), :, :, A], R.at[zz(1), :, :, A], zl),
         (R.at[zz(-3), y, :, B1], R.at[zz(-3), y, :, B1], zr),
         (R.at[zz(3), y, :, B2], R.at[zz(3), y, :, B2], zl)],
        [(R.at[zz(-2), :, :, A], R.at[zz(-2), :, :, A], zr), (R.at[zz(2), :, :, A], R.at[zz(2), :, :, A], zl),
         (R.at[:, y, :, B], R.at[:, y, :, B], yr), (R.at[:, y, :, B], R.at[:, y, :, B], yl)],
        [(R.at[zz(-3), pl.ds(0, hy), :, A], R.at[zz(-3), pl.ds(0, hy), :, A], zr),
         (R.at[zz(3), pl.ds(hy, ny - hy), :, A], R.at[zz(3), pl.ds(hy, ny - hy), :, A], zl),
         (R.at[pl.ds(0, hz), yy(-1), :, B], R.at[pl.ds(0, hz), yy(-1), :, B], yr),
         (R.at[pl.ds(hz, nz - hz), yy(1), :, B], R.at[pl.ds(hz, nz - hz), yy(1), :, B], yl)],
    ]
    heads, dim = sh_ref.shape[0], sh_ref.shape[2]
    tokens = q_ref.shape[0]
    causal = lax.broadcasted_iota(jnp.int32, (tokens, tokens), 1) <= lax.broadcasted_iota(jnp.int32, (tokens, tokens), 0)
    nt = (((1,), (1,)), ((), ()))

    def intra(h):
        cols = pl.ds(h * dim, dim)
        qh, kh = q_ref[:, cols], k_ref[:, cols]
        aw = lax.dot_general(qh, kh, nt, preferred_element_type=jnp.float32)
        aw = jnp.where(causal, aw, 0.0).astype(jnp.bfloat16)
        att_ref[:, cols] = jnp.dot(aw, v_ref[:, cols], preferred_element_type=jnp.float32)

    def finish(h):
        cols = pl.ds(h * dim, dim)
        a = att_ref[:, cols] + jnp.dot(q_ref[:, cols], sh_ref[h], preferred_element_type=jnp.float32)
        att_ref[:, cols] = a
        scale = lax.rsqrt(jnp.mean(a * a, axis=-1, keepdims=True) + EPS)
        normed_ref[:, cols] = (a * scale).astype(normed_ref.dtype)

    work = [[] for _ in ticks]
    for h in range(heads):
        work[min(h, 3)].append(h)
    total = value_ref[...]
    partial = jnp.zeros_like(total)
    n = 0
    for t, moves in enumerate(ticks):
        if t == 2:
            local.wait()
        started = []
        for src, dst, target in moves:
            copy = pltpu.make_async_remote_copy(
                src_ref=src, dst_ref=dst, send_sem=send_sem.at[n], recv_sem=recv_sem.at[n],
                device_id=target, device_id_type=MESH,
            )
            copy.start()
            started.append(copy)
            n += 1
        scan = None
        if t < rounds:
            partner, bit = partners[t]
            sent = total.astype(jnp.bfloat16)
            sendbuf[t] = sent
            scan = pltpu.make_async_remote_copy(
                src_ref=sendbuf.at[t], dst_ref=recvbuf.at[t], send_sem=bf_send.at[t],
                recv_sem=bf_recv.at[t], device_id=(partner, head), device_id_type=MESH,
            )
            scan.start()
        for h in work[t]:
            intra(h)
        if t == rounds:
            sh_ref[...] = (init_ref[...] + partial).astype(sh_ref.dtype)
            for h in range(heads):
                finish(h)
        for copy in started:
            copy.wait()
        if scan is not None:
            scan.wait()
            other = recvbuf[t].astype(jnp.float32)
            partial = jnp.where(bit == 1, partial + other, partial)
            total = sent.astype(jnp.float32) + other


def gather_and_scan(value, init_state, query, key, val, weight):
    count = lax.axis_size("seq")
    ny = 4
    piece, cols = weight.shape
    rounds = count.bit_length() - 1
    ca = (cols * 2 // 3) // 128 * 128
    n_copies = 23
    vmem = pl.BlockSpec(memory_space=pltpu.VMEM)
    return pl.pallas_call(
        functools.partial(gather_kernel, ny, ca),
        out_shape=(
            jax.ShapeDtypeStruct((count // ny, ny, piece, cols), weight.dtype),
            jax.ShapeDtypeStruct(query.shape, jnp.bfloat16),
            jax.ShapeDtypeStruct(query.shape, jnp.float32),
            jax.ShapeDtypeStruct(value.shape, jnp.bfloat16),
        ),
        in_specs=[vmem] * 5 + [pl.BlockSpec(memory_space=pl.ANY)],
        out_specs=(pl.BlockSpec(memory_space=pl.ANY), vmem, vmem, vmem),
        scratch_shapes=[
            pltpu.VMEM((rounds,) + value.shape, jnp.bfloat16),
            pltpu.VMEM((rounds,) + value.shape, jnp.bfloat16),
            pltpu.SemaphoreType.DMA((n_copies,)),
            pltpu.SemaphoreType.DMA((n_copies,)),
            pltpu.SemaphoreType.DMA((rounds,)),
            pltpu.SemaphoreType.DMA((rounds,)),
            pltpu.SemaphoreType.DMA(()),
        ],
        compiler_params=pltpu.CompilerParams(collective_id=2, has_side_effects=True),
    )(value.astype(jnp.float32), init_state, query, key, val, weight)


def normalize(attended):
    return attended * lax.rsqrt(jnp.mean(attended * attended, axis=-1, keepdims=True) + EPS)


def shards(query, key, value, init_state, out_weight, out_grad):
    tok_rows = query.shape[0]
    width = query.shape[1]
    heads_here = init_state.shape[0]
    head_dim = init_state.shape[2]
    queries = query.reshape(tok_rows, heads_here, head_dim)
    key_rows = key.reshape(tok_rows, heads_here, head_dim)
    val_rows = value.reshape(tok_rows, heads_here, head_dim)
    local_state = jnp.einsum("thi,thj->hij", key_rows, val_rows, preferred_element_type=jnp.float32)
    half = out_weight.shape[1] // 2
    gathered, normed, attended, state_half = gather_and_scan(
        local_state, init_state, query, key, value, out_weight[:, :half]
    )
    other_half = lax.all_gather(out_weight[:, half:], "seq", axis=0, tiled=True)
    attended = attended.reshape(tok_rows, heads_here, head_dim)
    first_rows = gathered.reshape(-1, half)
    weight_rows = jnp.concatenate([first_rows, other_half], axis=1)
    projected = jnp.dot(normed, weight_rows, preferred_element_type=jnp.float32).astype(jnp.bfloat16)
    projected, first_rows, other_half = lax.optimization_barrier((projected, first_rows, other_half))
    contract = (((1,), (1,)), ((), ()))
    grad_normed = lax.dot_general(
        out_grad[:, :half], first_rows, contract, preferred_element_type=jnp.float32
    ) + lax.dot_general(out_grad[:, half:], other_half, contract, preferred_element_type=jnp.float32)
    mixed = lax.psum_scatter(
        projected, "head", scatter_dimension=1, tiled=True
    )
    _, norm_back = jax.vjp(normalize, attended)
    grad_att = norm_back(grad_normed.reshape(tok_rows, heads_here, head_dim))[0].astype(
        jnp.bfloat16
    )
    own_adjoint = jnp.einsum("thi,thj->hij", queries, grad_att, preferred_element_type=jnp.float32)
    grad_query, grad_key, grad_value, init_grad = backward_pass(
        own_adjoint, query, key, value, grad_att.reshape(tok_rows, width), state_half
    )
    return (mixed, grad_query, grad_key, grad_value, init_grad)


def solution(mesh):
    return jax.shard_map(
        shards,
        mesh=mesh,
        in_specs=(
            P("seq", "head"),
            P("seq", "head"),
            P("seq", "head"),
            P("head", None, None),
            P(("head", "seq"), None),
            P("seq", None),
        ),
        out_specs=(
            P("seq", "head"),
            P("seq", "head"),
            P("seq", "head"),
            P("seq", "head"),
            P("head", None, None),
        ),
        check_vma=False,
    )
```

```python
import functools

import jax
import jax.numpy as jnp
from jax import lax
from jax.experimental import pallas as pl
from jax.experimental.pallas import tpu as pltpu
from jax.sharding import PartitionSpec as P

EPS = 1e-06


MESH = pl.DeviceIdType.MESH


def butterfly_kernel(count, backward, value_ref, partial_ref, total_ref, sendbuf, recvbuf, send_sem, recv_sem):
    me = lax.axis_index("seq")
    head = lax.axis_index("head")
    rounds = count.bit_length() - 1
    partners = []
    for k in range(rounds):
        step = 1 << k
        bit = (me // step) % 2
        partners.append((me + step - 2 * step * bit, bit))
    barrier = pltpu.get_barrier_semaphore()
    for partner, _ in partners:
        pl.semaphore_signal(barrier, inc=1, device_id=(partner, head), device_id_type=MESH)
    pl.semaphore_wait(barrier, rounds)
    total = value_ref[...]
    partial = jnp.zeros_like(total)
    for k, (partner, bit) in enumerate(partners):
        sent = total.astype(jnp.bfloat16)
        sendbuf[k] = sent
        copy = pltpu.make_async_remote_copy(
            src_ref=sendbuf.at[k],
            dst_ref=recvbuf.at[k],
            send_sem=send_sem.at[k],
            recv_sem=recv_sem.at[k],
            device_id=(partner, head),
            device_id_type=MESH,
        )
        copy.start()
        copy.wait()
        other = recvbuf[k].astype(jnp.float32)
        take = (bit == 0) if backward else (bit == 1)
        partial = jnp.where(take, partial + other, partial)
        total = sent.astype(jnp.float32) + other
    partial_ref[...] = partial
    total_ref[...] = total


def butterfly(value, axis, backward):
    count = lax.axis_size(axis)
    rounds = count.bit_length() - 1
    shape = jax.ShapeDtypeStruct(value.shape, jnp.float32)
    return pl.pallas_call(
        functools.partial(butterfly_kernel, count, backward),
        out_shape=(shape, shape),
        in_specs=[pl.BlockSpec(memory_space=pltpu.VMEM)],
        out_specs=(pl.BlockSpec(memory_space=pltpu.VMEM), pl.BlockSpec(memory_space=pltpu.VMEM)),
        scratch_shapes=[
            pltpu.VMEM((rounds,) + value.shape, jnp.bfloat16),
            pltpu.VMEM((rounds,) + value.shape, jnp.bfloat16),
            pltpu.SemaphoreType.DMA((rounds,)),
            pltpu.SemaphoreType.DMA((rounds,)),
        ],
        compiler_params=pltpu.CompilerParams(
            collective_id=1 if backward else 0, has_side_effects=True
        ),
    )(value.astype(jnp.float32))


def backward_kernel(adj_ref, q_ref, k_ref, v_ref, ga_ref, sh_ref, gq_ref, gk_ref, gv_ref, total_ref,
                    sendbuf, recvbuf, send_sem, recv_sem, gk_acc, gv_acc):
    me = lax.axis_index("seq")
    head = lax.axis_index("head")
    count = lax.axis_size("seq")
    rounds = count.bit_length() - 1
    heads = sh_ref.shape[0]
    dim = sh_ref.shape[2]
    rows = q_ref.shape[0]
    partners = []
    for k in range(rounds):
        step = 1 << k
        bit = (me // step) % 2
        partners.append((me + step - 2 * step * bit, bit))
    barrier = pltpu.get_barrier_semaphore()
    for partner, _ in partners:
        pl.semaphore_signal(barrier, inc=1, device_id=(partner, head), device_id_type=MESH)
    pl.semaphore_wait(barrier, rounds)
    causal = lax.broadcasted_iota(jnp.int32, (rows, rows), 1) <= lax.broadcasted_iota(jnp.int32, (rows, rows), 0)
    nt = (((1,), (1,)), ((), ()))
    tn = (((0,), (0,)), ((), ()))

    def head_work(h):
        cols = pl.ds(h * dim, dim)
        qh, kh, vh, gah = q_ref[:, cols], k_ref[:, cols], v_ref[:, cols], ga_ref[:, cols]
        gs = lax.dot_general(gah, vh, nt, preferred_element_type=jnp.float32)
        gs = jnp.where(causal, gs, 0.0).astype(jnp.bfloat16)
        aw = lax.dot_general(qh, kh, nt, preferred_element_type=jnp.float32)
        aw = jnp.where(causal, aw, 0.0).astype(jnp.bfloat16)
        gq = jnp.dot(gs, kh, preferred_element_type=jnp.float32)
        gq = gq + lax.dot_general(gah, sh_ref[h], nt, preferred_element_type=jnp.float32)
        gq_ref[:, cols] = gq.astype(gq_ref.dtype)
        gk_acc[:, cols] = lax.dot_general(gs, qh, tn, preferred_element_type=jnp.float32)
        gv_acc[:, cols] = lax.dot_general(aw, gah, tn, preferred_element_type=jnp.float32)

    order = [[] for _ in range(rounds)]
    for h in range(heads):
        order[min(h, rounds - 1)].append(h)
    total = adj_ref[...]
    partial = jnp.zeros_like(total)
    for t, (partner, bit) in enumerate(partners):
        sent = total.astype(jnp.bfloat16)
        sendbuf[t] = sent
        copy = pltpu.make_async_remote_copy(
            src_ref=sendbuf.at[t], dst_ref=recvbuf.at[t], send_sem=send_sem.at[t],
            recv_sem=recv_sem.at[t], device_id=(partner, head), device_id_type=MESH,
        )
        copy.start()
        for h in order[t]:
            head_work(h)
        copy.wait()
        other = recvbuf[t].astype(jnp.float32)
        partial = jnp.where(bit == 0, partial + other, partial)
        total = sent.astype(jnp.float32) + other
    total_ref[...] = total
    later = partial.astype(jnp.bfloat16)
    for h in range(heads):
        cols = pl.ds(h * dim, dim)
        gk = gk_acc[:, cols] + lax.dot_general(v_ref[:, cols], later[h], nt, preferred_element_type=jnp.float32)
        gk_ref[:, cols] = gk.astype(gk_ref.dtype)
        gv = gv_acc[:, cols] + jnp.dot(k_ref[:, cols], later[h], preferred_element_type=jnp.float32)
        gv_ref[:, cols] = gv.astype(gv_ref.dtype)


def backward_pass(own_adjoint, query, key, value, grad_att, state_half):
    count = lax.axis_size("seq")
    rounds = count.bit_length() - 1
    tokens = jax.ShapeDtypeStruct(query.shape, jnp.bfloat16)
    vmem = pl.BlockSpec(memory_space=pltpu.VMEM)
    return pl.pallas_call(
        backward_kernel,
        out_shape=(tokens, tokens, tokens, jax.ShapeDtypeStruct(own_adjoint.shape, jnp.float32)),
        in_specs=[vmem] * 6,
        out_specs=(vmem, vmem, vmem, vmem),
        scratch_shapes=[
            pltpu.VMEM((rounds,) + own_adjoint.shape, jnp.bfloat16),
            pltpu.VMEM((rounds,) + own_adjoint.shape, jnp.bfloat16),
            pltpu.SemaphoreType.DMA((rounds,)),
            pltpu.SemaphoreType.DMA((rounds,)),
            pltpu.VMEM(query.shape, jnp.float32),
            pltpu.VMEM(query.shape, jnp.float32),
        ],
        compiler_params=pltpu.CompilerParams(collective_id=1, has_side_effects=True),
    )(own_adjoint, query, key, value, grad_att, state_half)


def gather_kernel(ny, ca, value_ref, w_ref, rows_ref, partial_ref, sendbuf, recvbuf, send_sem, recv_sem, bf_send, bf_recv, local_sem):
    me = lax.axis_index("seq")
    head = lax.axis_index("head")
    count = lax.axis_size("seq")
    nz = count // ny
    y = me % ny
    z = me // ny
    piece, cols = w_ref.shape
    A = pl.ds(0, ca)
    B = pl.ds(ca, cols - ca)
    hy, hz = ny // 2, nz // 2
    hb = (cols - ca) // 2
    B1 = pl.ds(ca, hb)
    B2 = pl.ds(ca + hb, cols - ca - hb)

    def zz(k):
        return (z + nz + k) % nz

    def yy(k):
        return (y + ny + k) % ny

    def dev(zi, yi):
        return (zi * ny + yi, head)

    rounds = count.bit_length() - 1
    partners = []
    for k in range(rounds):
        step = 1 << k
        bit = (me // step) % 2
        partners.append((me + step - 2 * step * bit, bit))
    ring = [dev(z, yy(1)), dev(z, yy(-1)), dev(zz(1), y), dev(zz(-1), y)]
    barrier = pltpu.get_barrier_semaphore()
    for target in ring:
        pl.semaphore_signal(barrier, inc=1, device_id=target, device_id_type=MESH)
    for partner, _ in partners:
        pl.semaphore_signal(barrier, inc=1, device_id=(partner, head), device_id_type=MESH)
    pl.semaphore_wait(barrier, len(ring) + rounds)

    local = pltpu.make_async_copy(w_ref, rows_ref.at[z, y], local_sem)
    local.start()
    R = rows_ref
    yr, yl, zr, zl = dev(z, yy(1)), dev(z, yy(-1)), dev(zz(1), y), dev(zz(-1), y)
    ticks = [
        [(w_ref.at[:, A], R.at[z, y, :, A], yr), (w_ref.at[:, A], R.at[z, y, :, A], yl),
         (w_ref.at[:, B], R.at[z, y, :, B], zr), (w_ref.at[:, B], R.at[z, y, :, B], zl)],
        [(R.at[z, yy(-1), :, A], R.at[z, yy(-1), :, A], yr),
         (R.at[zz(-1), y, :, B], R.at[zz(-1), y, :, B], zr), (R.at[zz(1), y, :, B], R.at[zz(1), y, :, B], zl)],
        [(R.at[z, :, :, A], R.at[z, :, :, A], zr), (R.at[z, :, :, A], R.at[z, :, :, A], zl),
         (R.at[zz(-2), y, :, B], R.at[zz(-2), y, :, B], zr), (R.at[zz(2), y, :, B], R.at[zz(2), y, :, B], zl)],
        [(R.at[zz(-1), :, :, A], R.at[zz(-1), :, :, A], zr), (R.at[zz(1), :, :, A], R.at[zz(1), :, :, A], zl),
         (R.at[zz(-3), y, :, B1], R.at[zz(-3), y, :, B1], zr),
         (R.at[zz(3), y, :, B2], R.at[zz(3), y, :, B2], zl)],
        [(R.at[zz(-2), :, :, A], R.at[zz(-2), :, :, A], zr), (R.at[zz(2), :, :, A], R.at[zz(2), :, :, A], zl),
         (R.at[:, y, :, B], R.at[:, y, :, B], yr), (R.at[:, y, :, B], R.at[:, y, :, B], yl)],
        [(R.at[zz(-3), pl.ds(0, hy), :, A], R.at[zz(-3), pl.ds(0, hy), :, A], zr),
         (R.at[zz(3), pl.ds(hy, ny - hy), :, A], R.at[zz(3), pl.ds(hy, ny - hy), :, A], zl),
         (R.at[pl.ds(0, hz), yy(-1), :, B], R.at[pl.ds(0, hz), yy(-1), :, B], yr),
         (R.at[pl.ds(hz, nz - hz), yy(1), :, B], R.at[pl.ds(hz, nz - hz), yy(1), :, B], yl)],
    ]
    total = value_ref[...]
    partial = jnp.zeros_like(total)
    n = 0
    for t, moves in enumerate(ticks):
        if t == 2:
            local.wait()
        started = []
        for src, dst, target in moves:
            copy = pltpu.make_async_remote_copy(
                src_ref=src, dst_ref=dst, send_sem=send_sem.at[n], recv_sem=recv_sem.at[n],
                device_id=target, device_id_type=MESH,
            )
            copy.start()
            started.append(copy)
            n += 1
        scan = None
        if t < rounds:
            partner, bit = partners[t]
            sent = total.astype(jnp.bfloat16)
            sendbuf[t] = sent
            scan = pltpu.make_async_remote_copy(
                src_ref=sendbuf.at[t], dst_ref=recvbuf.at[t], send_sem=bf_send.at[t],
                recv_sem=bf_recv.at[t], device_id=(partner, head), device_id_type=MESH,
            )
            scan.start()
        for copy in started:
            copy.wait()
        if scan is not None:
            scan.wait()
            other = recvbuf[t].astype(jnp.float32)
            partial = jnp.where(bit == 1, partial + other, partial)
            total = sent.astype(jnp.float32) + other
    partial_ref[...] = partial


def gather_and_scan(value, weight):
    count = lax.axis_size("seq")
    ny = 4
    piece, cols = weight.shape
    rounds = count.bit_length() - 1
    ca = (cols * 2 // 3) // 128 * 128
    n_copies = 23
    return pl.pallas_call(
        functools.partial(gather_kernel, ny, ca),
        out_shape=(
            jax.ShapeDtypeStruct((count // ny, ny, piece, cols), weight.dtype),
            jax.ShapeDtypeStruct(value.shape, jnp.float32),
        ),
        in_specs=[pl.BlockSpec(memory_space=pltpu.VMEM), pl.BlockSpec(memory_space=pl.ANY)],
        out_specs=(pl.BlockSpec(memory_space=pl.ANY), pl.BlockSpec(memory_space=pltpu.VMEM)),
        scratch_shapes=[
            pltpu.VMEM((rounds,) + value.shape, jnp.bfloat16),
            pltpu.VMEM((rounds,) + value.shape, jnp.bfloat16),
            pltpu.SemaphoreType.DMA((n_copies,)),
            pltpu.SemaphoreType.DMA((n_copies,)),
            pltpu.SemaphoreType.DMA((rounds,)),
            pltpu.SemaphoreType.DMA((rounds,)),
            pltpu.SemaphoreType.DMA(()),
        ],
        compiler_params=pltpu.CompilerParams(collective_id=2, has_side_effects=True),
    )(value.astype(jnp.float32), weight)


def normalize(attended):
    return attended * lax.rsqrt(jnp.mean(attended * attended, axis=-1, keepdims=True) + EPS)


def shards(query, key, value, init_state, out_weight, out_grad):
    tok_rows = query.shape[0]
    width = query.shape[1]
    heads_here = init_state.shape[0]
    head_dim = init_state.shape[2]
    queries = query.reshape(tok_rows, heads_here, head_dim)
    key_rows = key.reshape(tok_rows, heads_here, head_dim)
    val_rows = value.reshape(tok_rows, heads_here, head_dim)
    local_state = jnp.einsum("thi,thj->hij", key_rows, val_rows, preferred_element_type=jnp.float32)
    half = out_weight.shape[1] // 2
    gathered, earlier = gather_and_scan(local_state, out_weight[:, :half])
    other_half = lax.all_gather(out_weight[:, half:], "seq", axis=0, tiled=True)
    state_half = (init_state + earlier).astype(jnp.bfloat16)
    row_index = lax.broadcasted_iota(jnp.int32, (tok_rows, tok_rows), 0)
    col_index = lax.broadcasted_iota(jnp.int32, (tok_rows, tok_rows), 1)
    causal = col_index <= row_index
    scores = jnp.einsum("thi,shi->hts", queries, key_rows, preferred_element_type=jnp.float32)
    attn_weights = jnp.where(causal, scores, 0.0).astype(jnp.bfloat16)
    attended = jnp.einsum(
        "hts,shj->thj", attn_weights, val_rows, preferred_element_type=jnp.float32
    )
    attended = attended + jnp.einsum(
        "thi,hij->thj", queries, state_half, preferred_element_type=jnp.float32
    )
    normed = normalize(attended).astype(jnp.bfloat16).reshape(tok_rows, width)
    first_rows = gathered.reshape(-1, half)
    weight_rows = jnp.concatenate([first_rows, other_half], axis=1)
    projected = jnp.dot(normed, weight_rows, preferred_element_type=jnp.float32).astype(jnp.bfloat16)
    projected, first_rows, other_half = lax.optimization_barrier((projected, first_rows, other_half))
    contract = (((1,), (1,)), ((), ()))
    grad_normed = lax.dot_general(
        out_grad[:, :half], first_rows, contract, preferred_element_type=jnp.float32
    ) + lax.dot_general(out_grad[:, half:], other_half, contract, preferred_element_type=jnp.float32)
    mixed = lax.psum_scatter(
        projected, "head", scatter_dimension=1, tiled=True
    )
    _, norm_back = jax.vjp(normalize, attended)
    grad_att = norm_back(grad_normed.reshape(tok_rows, heads_here, head_dim))[0].astype(
        jnp.bfloat16
    )
    own_adjoint = jnp.einsum("thi,thj->hij", queries, grad_att, preferred_element_type=jnp.float32)
    grad_query, grad_key, grad_value, init_grad = backward_pass(
        own_adjoint, query, key, value, grad_att.reshape(tok_rows, width), state_half
    )
    return (mixed, grad_query, grad_key, grad_value, init_grad)


def solution(mesh):
    return jax.shard_map(
        shards,
        mesh=mesh,
        in_specs=(
            P("seq", "head"),
            P("seq", "head"),
            P("seq", "head"),
            P("head", None, None),
            P(("head", "seq"), None),
            P("seq", None),
        ),
        out_specs=(
            P("seq", "head"),
            P("seq", "head"),
            P("seq", "head"),
            P("seq", "head"),
            P("head", None, None),
        ),
        check_vma=False,
    )
```

```python
import functools

import jax
import jax.numpy as jnp
from jax import lax
from jax.experimental import pallas as pl
from jax.experimental.pallas import tpu as pltpu
from jax.sharding import PartitionSpec as P

EPS = 1e-06


MESH = pl.DeviceIdType.MESH


def butterfly_kernel(count, backward, value_ref, partial_ref, total_ref, sendbuf, recvbuf, send_sem, recv_sem):
    me = lax.axis_index("seq")
    head = lax.axis_index("head")
    rounds = count.bit_length() - 1
    partners = []
    for k in range(rounds):
        step = 1 << k
        bit = (me // step) % 2
        partners.append((me + step - 2 * step * bit, bit))
    barrier = pltpu.get_barrier_semaphore()
    for partner, _ in partners:
        pl.semaphore_signal(barrier, inc=1, device_id=(partner, head), device_id_type=MESH)
    pl.semaphore_wait(barrier, rounds)
    total = value_ref[...]
    partial = jnp.zeros_like(total)
    for k, (partner, bit) in enumerate(partners):
        sent = total.astype(jnp.bfloat16)
        sendbuf[k] = sent
        copy = pltpu.make_async_remote_copy(
            src_ref=sendbuf.at[k],
            dst_ref=recvbuf.at[k],
            send_sem=send_sem.at[k],
            recv_sem=recv_sem.at[k],
            device_id=(partner, head),
            device_id_type=MESH,
        )
        copy.start()
        copy.wait()
        other = recvbuf[k].astype(jnp.float32)
        take = (bit == 0) if backward else (bit == 1)
        partial = jnp.where(take, partial + other, partial)
        total = sent.astype(jnp.float32) + other
    partial_ref[...] = partial
    total_ref[...] = total


def butterfly(value, axis, backward):
    count = lax.axis_size(axis)
    rounds = count.bit_length() - 1
    shape = jax.ShapeDtypeStruct(value.shape, jnp.float32)
    return pl.pallas_call(
        functools.partial(butterfly_kernel, count, backward),
        out_shape=(shape, shape),
        in_specs=[pl.BlockSpec(memory_space=pltpu.VMEM)],
        out_specs=(pl.BlockSpec(memory_space=pltpu.VMEM), pl.BlockSpec(memory_space=pltpu.VMEM)),
        scratch_shapes=[
            pltpu.VMEM((rounds,) + value.shape, jnp.bfloat16),
            pltpu.VMEM((rounds,) + value.shape, jnp.bfloat16),
            pltpu.SemaphoreType.DMA((rounds,)),
            pltpu.SemaphoreType.DMA((rounds,)),
        ],
        compiler_params=pltpu.CompilerParams(
            collective_id=1 if backward else 0, has_side_effects=True
        ),
    )(value.astype(jnp.float32))


def backward_kernel(adj_ref, q_ref, k_ref, v_ref, ga_ref, sh_ref, gq_ref, gk_acc, gv_acc, later_ref, total_ref,
                    sendbuf, recvbuf, send_sem, recv_sem):
    me = lax.axis_index("seq")
    head = lax.axis_index("head")
    count = lax.axis_size("seq")
    rounds = count.bit_length() - 1
    heads = sh_ref.shape[0]
    dim = sh_ref.shape[2]
    rows = q_ref.shape[0]
    partners = []
    for k in range(rounds):
        step = 1 << k
        bit = (me // step) % 2
        partners.append((me + step - 2 * step * bit, bit))
    barrier = pltpu.get_barrier_semaphore()
    for partner, _ in partners:
        pl.semaphore_signal(barrier, inc=1, device_id=(partner, head), device_id_type=MESH)
    pl.semaphore_wait(barrier, rounds)
    causal = lax.broadcasted_iota(jnp.int32, (rows, rows), 1) <= lax.broadcasted_iota(jnp.int32, (rows, rows), 0)
    nt = (((1,), (1,)), ((), ()))
    tn = (((0,), (0,)), ((), ()))

    def head_work(h):
        cols = pl.ds(h * dim, dim)
        qh, kh, vh, gah = q_ref[:, cols], k_ref[:, cols], v_ref[:, cols], ga_ref[:, cols]
        gs = lax.dot_general(gah, vh, nt, preferred_element_type=jnp.float32)
        gs = jnp.where(causal, gs, 0.0).astype(jnp.bfloat16)
        aw = lax.dot_general(qh, kh, nt, preferred_element_type=jnp.float32)
        aw = jnp.where(causal, aw, 0.0).astype(jnp.bfloat16)
        gq = jnp.dot(gs, kh, preferred_element_type=jnp.float32)
        gq = gq + lax.dot_general(gah, sh_ref[h], nt, preferred_element_type=jnp.float32)
        gq_ref[:, cols] = gq.astype(gq_ref.dtype)
        gk_acc[:, cols] = lax.dot_general(gs, qh, tn, preferred_element_type=jnp.float32)
        gv_acc[:, cols] = lax.dot_general(aw, gah, tn, preferred_element_type=jnp.float32)

    order = [[] for _ in range(rounds)]
    for h in range(heads):
        order[min(h, rounds - 1)].append(h)
    total = adj_ref[...]
    partial = jnp.zeros_like(total)
    for t, (partner, bit) in enumerate(partners):
        sent = total.astype(jnp.bfloat16)
        sendbuf[t] = sent
        copy = pltpu.make_async_remote_copy(
            src_ref=sendbuf.at[t], dst_ref=recvbuf.at[t], send_sem=send_sem.at[t],
            recv_sem=recv_sem.at[t], device_id=(partner, head), device_id_type=MESH,
        )
        copy.start()
        for h in order[t]:
            head_work(h)
        copy.wait()
        other = recvbuf[t].astype(jnp.float32)
        partial = jnp.where(bit == 0, partial + other, partial)
        total = sent.astype(jnp.float32) + other
    total_ref[...] = total
    later_ref[...] = partial.astype(later_ref.dtype)


def finish_kernel(gq_in, gk_acc, gv_acc, v_ref, k_ref, later_ref, gq_ref, gk_ref, gv_ref):
    heads, dim = later_ref.shape[0], later_ref.shape[2]
    nt = (((1,), (1,)), ((), ()))
    gq_ref[...] = gq_in[...]
    for h in range(heads):
        cols = pl.ds(h * dim, dim)
        later = later_ref[h]
        gk = gk_acc[:, cols] + lax.dot_general(v_ref[:, cols], later, nt, preferred_element_type=jnp.float32)
        gk_ref[:, cols] = gk.astype(gk_ref.dtype)
        gv = gv_acc[:, cols] + jnp.dot(k_ref[:, cols], later, preferred_element_type=jnp.float32)
        gv_ref[:, cols] = gv.astype(gv_ref.dtype)


def backward_pass(own_adjoint, query, key, value, grad_att, state_half):
    count = lax.axis_size("seq")
    rounds = count.bit_length() - 1
    tokens = jax.ShapeDtypeStruct(query.shape, jnp.bfloat16)
    vmem = pl.BlockSpec(memory_space=pltpu.VMEM)
    accs = jax.ShapeDtypeStruct(query.shape, jnp.float32)
    gq, gk_acc, gv_acc, later, total = pl.pallas_call(
        backward_kernel,
        out_shape=(tokens, accs, accs, jax.ShapeDtypeStruct(own_adjoint.shape, jnp.bfloat16),
                   jax.ShapeDtypeStruct(own_adjoint.shape, jnp.float32)),
        in_specs=[vmem] * 6,
        out_specs=(vmem,) * 5,
        scratch_shapes=[
            pltpu.VMEM((rounds,) + own_adjoint.shape, jnp.bfloat16),
            pltpu.VMEM((rounds,) + own_adjoint.shape, jnp.bfloat16),
            pltpu.SemaphoreType.DMA((rounds,)),
            pltpu.SemaphoreType.DMA((rounds,)),
        ],
        compiler_params=pltpu.CompilerParams(collective_id=1, has_side_effects=True),
    )(own_adjoint, query, key, value, grad_att, state_half)
    gq, gk, gv = pl.pallas_call(
        finish_kernel,
        out_shape=(tokens, tokens, tokens),
        in_specs=[vmem] * 6,
        out_specs=(vmem,) * 3,
    )(gq, gk_acc, gv_acc, value, key, later)
    return gq, gk, gv, total


def gather_kernel(ny, ca, value_ref, w_ref, rows_ref, partial_ref, sendbuf, recvbuf, send_sem, recv_sem, bf_send, bf_recv, local_sem):
    me = lax.axis_index("seq")
    head = lax.axis_index("head")
    count = lax.axis_size("seq")
    nz = count // ny
    y = me % ny
    z = me // ny
    piece, cols = w_ref.shape
    A = pl.ds(0, ca)
    B = pl.ds(ca, cols - ca)
    hy, hz = ny // 2, nz // 2
    hb = (cols - ca) // 2
    B1 = pl.ds(ca, hb)
    B2 = pl.ds(ca + hb, cols - ca - hb)

    def zz(k):
        return (z + nz + k) % nz

    def yy(k):
        return (y + ny + k) % ny

    def dev(zi, yi):
        return (zi * ny + yi, head)

    rounds = count.bit_length() - 1
    partners = []
    for k in range(rounds):
        step = 1 << k
        bit = (me // step) % 2
        partners.append((me + step - 2 * step * bit, bit))
    ring = [dev(z, yy(1)), dev(z, yy(-1)), dev(zz(1), y), dev(zz(-1), y)]
    barrier = pltpu.get_barrier_semaphore()
    for target in ring:
        pl.semaphore_signal(barrier, inc=1, device_id=target, device_id_type=MESH)
    for partner, _ in partners:
        pl.semaphore_signal(barrier, inc=1, device_id=(partner, head), device_id_type=MESH)
    pl.semaphore_wait(barrier, len(ring) + rounds)

    local = pltpu.make_async_copy(w_ref, rows_ref.at[z, y], local_sem)
    local.start()
    R = rows_ref
    yr, yl, zr, zl = dev(z, yy(1)), dev(z, yy(-1)), dev(zz(1), y), dev(zz(-1), y)
    ticks = [
        [(w_ref.at[:, A], R.at[z, y, :, A], yr), (w_ref.at[:, A], R.at[z, y, :, A], yl),
         (w_ref.at[:, B], R.at[z, y, :, B], zr), (w_ref.at[:, B], R.at[z, y, :, B], zl)],
        [(R.at[z, yy(-1), :, A], R.at[z, yy(-1), :, A], yr),
         (R.at[zz(-1), y, :, B], R.at[zz(-1), y, :, B], zr), (R.at[zz(1), y, :, B], R.at[zz(1), y, :, B], zl)],
        [(R.at[z, :, :, A], R.at[z, :, :, A], zr), (R.at[z, :, :, A], R.at[z, :, :, A], zl),
         (R.at[zz(-2), y, :, B], R.at[zz(-2), y, :, B], zr), (R.at[zz(2), y, :, B], R.at[zz(2), y, :, B], zl)],
        [(R.at[zz(-1), :, :, A], R.at[zz(-1), :, :, A], zr), (R.at[zz(1), :, :, A], R.at[zz(1), :, :, A], zl),
         (R.at[zz(-3), y, :, B1], R.at[zz(-3), y, :, B1], zr),
         (R.at[zz(3), y, :, B2], R.at[zz(3), y, :, B2], zl)],
        [(R.at[zz(-2), :, :, A], R.at[zz(-2), :, :, A], zr), (R.at[zz(2), :, :, A], R.at[zz(2), :, :, A], zl),
         (R.at[:, y, :, B], R.at[:, y, :, B], yr), (R.at[:, y, :, B], R.at[:, y, :, B], yl)],
        [(R.at[zz(-3), pl.ds(0, hy), :, A], R.at[zz(-3), pl.ds(0, hy), :, A], zr),
         (R.at[zz(3), pl.ds(hy, ny - hy), :, A], R.at[zz(3), pl.ds(hy, ny - hy), :, A], zl),
         (R.at[pl.ds(0, hz), yy(-1), :, B], R.at[pl.ds(0, hz), yy(-1), :, B], yr),
         (R.at[pl.ds(hz, nz - hz), yy(1), :, B], R.at[pl.ds(hz, nz - hz), yy(1), :, B], yl)],
    ]
    total = value_ref[...]
    partial = jnp.zeros_like(total)
    n = 0
    for t, moves in enumerate(ticks):
        if t == 2:
            local.wait()
        started = []
        for src, dst, target in moves:
            copy = pltpu.make_async_remote_copy(
                src_ref=src, dst_ref=dst, send_sem=send_sem.at[n], recv_sem=recv_sem.at[n],
                device_id=target, device_id_type=MESH,
            )
            copy.start()
            started.append(copy)
            n += 1
        scan = None
        if t < rounds:
            partner, bit = partners[t]
            sent = total.astype(jnp.bfloat16)
            sendbuf[t] = sent
            scan = pltpu.make_async_remote_copy(
                src_ref=sendbuf.at[t], dst_ref=recvbuf.at[t], send_sem=bf_send.at[t],
                recv_sem=bf_recv.at[t], device_id=(partner, head), device_id_type=MESH,
            )
            scan.start()
        for copy in started:
            copy.wait()
        if scan is not None:
            scan.wait()
            other = recvbuf[t].astype(jnp.float32)
            partial = jnp.where(bit == 1, partial + other, partial)
            total = sent.astype(jnp.float32) + other
    partial_ref[...] = partial


def gather_and_scan(value, weight):
    count = lax.axis_size("seq")
    ny = 4
    piece, cols = weight.shape
    rounds = count.bit_length() - 1
    ca = (cols * 2 // 3) // 128 * 128
    n_copies = 23
    return pl.pallas_call(
        functools.partial(gather_kernel, ny, ca),
        out_shape=(
            jax.ShapeDtypeStruct((count // ny, ny, piece, cols), weight.dtype),
            jax.ShapeDtypeStruct(value.shape, jnp.float32),
        ),
        in_specs=[pl.BlockSpec(memory_space=pltpu.VMEM), pl.BlockSpec(memory_space=pl.ANY)],
        out_specs=(pl.BlockSpec(memory_space=pl.ANY), pl.BlockSpec(memory_space=pltpu.VMEM)),
        scratch_shapes=[
            pltpu.VMEM((rounds,) + value.shape, jnp.bfloat16),
            pltpu.VMEM((rounds,) + value.shape, jnp.bfloat16),
            pltpu.SemaphoreType.DMA((n_copies,)),
            pltpu.SemaphoreType.DMA((n_copies,)),
            pltpu.SemaphoreType.DMA((rounds,)),
            pltpu.SemaphoreType.DMA((rounds,)),
            pltpu.SemaphoreType.DMA(()),
        ],
        compiler_params=pltpu.CompilerParams(collective_id=2, has_side_effects=True),
    )(value.astype(jnp.float32), weight)


def normalize(attended):
    return attended * lax.rsqrt(jnp.mean(attended * attended, axis=-1, keepdims=True) + EPS)


def shards(query, key, value, init_state, out_weight, out_grad):
    tok_rows = query.shape[0]
    width = query.shape[1]
    heads_here = init_state.shape[0]
    head_dim = init_state.shape[2]
    queries = query.reshape(tok_rows, heads_here, head_dim)
    key_rows = key.reshape(tok_rows, heads_here, head_dim)
    val_rows = value.reshape(tok_rows, heads_here, head_dim)
    local_state = jnp.einsum("thi,thj->hij", key_rows, val_rows, preferred_element_type=jnp.float32)
    half = out_weight.shape[1] // 2
    gathered, earlier = gather_and_scan(local_state, out_weight[:, :half])
    other_half = lax.all_gather(out_weight[:, half:], "seq", axis=0, tiled=True)
    state_half = (init_state + earlier).astype(jnp.bfloat16)
    row_index = lax.broadcasted_iota(jnp.int32, (tok_rows, tok_rows), 0)
    col_index = lax.broadcasted_iota(jnp.int32, (tok_rows, tok_rows), 1)
    causal = col_index <= row_index
    scores = jnp.einsum("thi,shi->hts", queries, key_rows, preferred_element_type=jnp.float32)
    attn_weights = jnp.where(causal, scores, 0.0).astype(jnp.bfloat16)
    attended = jnp.einsum(
        "hts,shj->thj", attn_weights, val_rows, preferred_element_type=jnp.float32
    )
    attended = attended + jnp.einsum(
        "thi,hij->thj", queries, state_half, preferred_element_type=jnp.float32
    )
    normed = normalize(attended).astype(jnp.bfloat16).reshape(tok_rows, width)
    first_rows = gathered.reshape(-1, half)
    projected = jnp.concatenate([
        jnp.dot(normed, first_rows, preferred_element_type=jnp.float32).astype(jnp.bfloat16),
        jnp.dot(normed, other_half, preferred_element_type=jnp.float32).astype(jnp.bfloat16),
    ], axis=1)
    projected, first_rows, other_half = lax.optimization_barrier((projected, first_rows, other_half))
    contract = (((1,), (1,)), ((), ()))
    grad_normed = lax.dot_general(
        out_grad[:, :half], first_rows, contract, preferred_element_type=jnp.float32
    ) + lax.dot_general(out_grad[:, half:], other_half, contract, preferred_element_type=jnp.float32)
    mixed = lax.psum_scatter(
        projected, "head", scatter_dimension=1, tiled=True
    )
    _, norm_back = jax.vjp(normalize, attended)
    grad_att = norm_back(grad_normed.reshape(tok_rows, heads_here, head_dim))[0].astype(
        jnp.bfloat16
    )
    own_adjoint = jnp.einsum("thi,thj->hij", queries, grad_att, preferred_element_type=jnp.float32)
    grad_query, grad_key, grad_value, init_grad = backward_pass(
        own_adjoint, query, key, value, grad_att.reshape(tok_rows, width), state_half
    )
    return (mixed, grad_query, grad_key, grad_value, init_grad)


def solution(mesh):
    return jax.shard_map(
        shards,
        mesh=mesh,
        in_specs=(
            P("seq", "head"),
            P("seq", "head"),
            P("seq", "head"),
            P("head", None, None),
            P(("head", "seq"), None),
            P("seq", None),
        ),
        out_specs=(
            P("seq", "head"),
            P("seq", "head"),
            P("seq", "head"),
            P("seq", "head"),
            P("head", None, None),
        ),
        check_vma=False,
    )
```

```python
import functools

import jax
import jax.numpy as jnp
from jax import lax
from jax.experimental import pallas as pl
from jax.experimental.pallas import tpu as pltpu
from jax.sharding import PartitionSpec as P

EPS = 1e-06


MESH = pl.DeviceIdType.MESH


def butterfly_kernel(count, backward, value_ref, partial_ref, total_ref, sendbuf, recvbuf, send_sem, recv_sem):
    me = lax.axis_index("seq")
    head = lax.axis_index("head")
    rounds = count.bit_length() - 1
    partners = []
    for k in range(rounds):
        step = 1 << k
        bit = (me // step) % 2
        partners.append((me + step - 2 * step * bit, bit))
    barrier = pltpu.get_barrier_semaphore()
    for partner, _ in partners:
        pl.semaphore_signal(barrier, inc=1, device_id=(partner, head), device_id_type=MESH)
    pl.semaphore_wait(barrier, rounds)
    total = value_ref[...]
    partial = jnp.zeros_like(total)
    for k, (partner, bit) in enumerate(partners):
        sent = total.astype(jnp.bfloat16)
        sendbuf[k] = sent
        copy = pltpu.make_async_remote_copy(
            src_ref=sendbuf.at[k],
            dst_ref=recvbuf.at[k],
            send_sem=send_sem.at[k],
            recv_sem=recv_sem.at[k],
            device_id=(partner, head),
            device_id_type=MESH,
        )
        copy.start()
        copy.wait()
        other = recvbuf[k].astype(jnp.float32)
        take = (bit == 0) if backward else (bit == 1)
        partial = jnp.where(take, partial + other, partial)
        total = sent.astype(jnp.float32) + other
    partial_ref[...] = partial
    total_ref[...] = total


def butterfly(value, axis, backward):
    count = lax.axis_size(axis)
    rounds = count.bit_length() - 1
    shape = jax.ShapeDtypeStruct(value.shape, jnp.float32)
    return pl.pallas_call(
        functools.partial(butterfly_kernel, count, backward),
        out_shape=(shape, shape),
        in_specs=[pl.BlockSpec(memory_space=pltpu.VMEM)],
        out_specs=(pl.BlockSpec(memory_space=pltpu.VMEM), pl.BlockSpec(memory_space=pltpu.VMEM)),
        scratch_shapes=[
            pltpu.VMEM((rounds,) + value.shape, jnp.bfloat16),
            pltpu.VMEM((rounds,) + value.shape, jnp.bfloat16),
            pltpu.SemaphoreType.DMA((rounds,)),
            pltpu.SemaphoreType.DMA((rounds,)),
        ],
        compiler_params=pltpu.CompilerParams(
            collective_id=1 if backward else 0, has_side_effects=True
        ),
    )(value.astype(jnp.float32))


def backward_kernel(adj_ref, q_hbm, k_hbm, v_hbm, ga_hbm, sh_ref, gq_ref, gk_acc, gv_acc, later_ref, total_ref,
                    sendbuf, recvbuf, send_sem, recv_sem, q_ref, k_ref, v_ref, ga_ref, load_sem):
    loads = [pltpu.make_async_copy(src, dst, load_sem.at[i])
             for i, (src, dst) in enumerate([(q_hbm, q_ref), (k_hbm, k_ref), (v_hbm, v_ref), (ga_hbm, ga_ref)])]
    for load in loads:
        load.start()
    me = lax.axis_index("seq")
    head = lax.axis_index("head")
    count = lax.axis_size("seq")
    rounds = count.bit_length() - 1
    heads = sh_ref.shape[0]
    dim = sh_ref.shape[2]
    rows = q_ref.shape[0]
    partners = []
    for k in range(rounds):
        step = 1 << k
        bit = (me // step) % 2
        partners.append((me + step - 2 * step * bit, bit))
    barrier = pltpu.get_barrier_semaphore()
    for partner, _ in partners:
        pl.semaphore_signal(barrier, inc=1, device_id=(partner, head), device_id_type=MESH)
    pl.semaphore_wait(barrier, rounds)
    causal = lax.broadcasted_iota(jnp.int32, (rows, rows), 1) <= lax.broadcasted_iota(jnp.int32, (rows, rows), 0)
    nt = (((1,), (1,)), ((), ()))
    tn = (((0,), (0,)), ((), ()))

    def head_work(h):
        cols = pl.ds(h * dim, dim)
        qh, kh, vh, gah = q_ref[:, cols], k_ref[:, cols], v_ref[:, cols], ga_ref[:, cols]
        gs = lax.dot_general(gah, vh, nt, preferred_element_type=jnp.float32)
        gs = jnp.where(causal, gs, 0.0).astype(jnp.bfloat16)
        aw = lax.dot_general(qh, kh, nt, preferred_element_type=jnp.float32)
        aw = jnp.where(causal, aw, 0.0).astype(jnp.bfloat16)
        gq = jnp.dot(gs, kh, preferred_element_type=jnp.float32)
        gq = gq + lax.dot_general(gah, sh_ref[h], nt, preferred_element_type=jnp.float32)
        gq_ref[:, cols] = gq.astype(gq_ref.dtype)
        gk_acc[:, cols] = lax.dot_general(gs, qh, tn, preferred_element_type=jnp.float32)
        gv_acc[:, cols] = lax.dot_general(aw, gah, tn, preferred_element_type=jnp.float32)

    order = [[] for _ in range(rounds)]
    for h in range(heads):
        order[min(h, rounds - 1)].append(h)
    total = adj_ref[...]
    partial = jnp.zeros_like(total)
    for t, (partner, bit) in enumerate(partners):
        sent = total.astype(jnp.bfloat16)
        sendbuf[t] = sent
        copy = pltpu.make_async_remote_copy(
            src_ref=sendbuf.at[t], dst_ref=recvbuf.at[t], send_sem=send_sem.at[t],
            recv_sem=recv_sem.at[t], device_id=(partner, head), device_id_type=MESH,
        )
        copy.start()
        if t == 0:
            for load in loads:
                load.wait()
        for h in order[t]:
            head_work(h)
        copy.wait()
        other = recvbuf[t].astype(jnp.float32)
        partial = jnp.where(bit == 0, partial + other, partial)
        total = sent.astype(jnp.float32) + other
    total_ref[...] = total
    later_ref[...] = partial.astype(later_ref.dtype)


def finish_kernel(gq_in, gk_acc, gv_acc, v_ref, k_ref, later_ref, gq_ref, gk_ref, gv_ref):
    heads, dim = later_ref.shape[0], later_ref.shape[2]
    nt = (((1,), (1,)), ((), ()))
    gq_ref[...] = gq_in[...]
    for h in range(heads):
        cols = pl.ds(h * dim, dim)
        later = later_ref[h]
        gk = gk_acc[:, cols] + lax.dot_general(v_ref[:, cols], later, nt, preferred_element_type=jnp.float32)
        gk_ref[:, cols] = gk.astype(gk_ref.dtype)
        gv = gv_acc[:, cols] + jnp.dot(k_ref[:, cols], later, preferred_element_type=jnp.float32)
        gv_ref[:, cols] = gv.astype(gv_ref.dtype)


def backward_pass(own_adjoint, query, key, value, grad_att, state_half):
    count = lax.axis_size("seq")
    rounds = count.bit_length() - 1
    tokens = jax.ShapeDtypeStruct(query.shape, jnp.bfloat16)
    vmem = pl.BlockSpec(memory_space=pltpu.VMEM)
    accs = jax.ShapeDtypeStruct(query.shape, jnp.float32)
    gq, gk_acc, gv_acc, later, total = pl.pallas_call(
        backward_kernel,
        out_shape=(tokens, accs, accs, jax.ShapeDtypeStruct(own_adjoint.shape, jnp.bfloat16),
                   jax.ShapeDtypeStruct(own_adjoint.shape, jnp.float32)),
        in_specs=[vmem] + [pl.BlockSpec(memory_space=pl.ANY)] * 4 + [vmem],
        out_specs=(vmem,) * 5,
        scratch_shapes=[
            pltpu.VMEM((rounds,) + own_adjoint.shape, jnp.bfloat16),
            pltpu.VMEM((rounds,) + own_adjoint.shape, jnp.bfloat16),
            pltpu.SemaphoreType.DMA((rounds,)),
            pltpu.SemaphoreType.DMA((rounds,)),
        ] + [pltpu.VMEM(query.shape, jnp.bfloat16)] * 4 + [pltpu.SemaphoreType.DMA((4,))],
        compiler_params=pltpu.CompilerParams(collective_id=1, has_side_effects=True),
    )(own_adjoint, query, key, value, grad_att, state_half)
    gq, gk, gv = pl.pallas_call(
        finish_kernel,
        out_shape=(tokens, tokens, tokens),
        in_specs=[vmem] * 6,
        out_specs=(vmem,) * 3,
    )(gq, gk_acc, gv_acc, value, key, later)
    return gq, gk, gv, total


def gather_kernel(ny, ca, value_ref, w_ref, rows_ref, partial_ref, sendbuf, recvbuf, send_sem, recv_sem, bf_send, bf_recv, local_sem):
    me = lax.axis_index("seq")
    head = lax.axis_index("head")
    count = lax.axis_size("seq")
    nz = count // ny
    y = me % ny
    z = me // ny
    piece, cols = w_ref.shape
    A = pl.ds(0, ca)
    B = pl.ds(ca, cols - ca)
    hy, hz = ny // 2, nz // 2
    hb = (cols - ca) // 2
    B1 = pl.ds(ca, hb)
    B2 = pl.ds(ca + hb, cols - ca - hb)

    def zz(k):
        return (z + nz + k) % nz

    def yy(k):
        return (y + ny + k) % ny

    def dev(zi, yi):
        return (zi * ny + yi, head)

    rounds = count.bit_length() - 1
    partners = []
    for k in range(rounds):
        step = 1 << k
        bit = (me // step) % 2
        partners.append((me + step - 2 * step * bit, bit))
    ring = [dev(z, yy(1)), dev(z, yy(-1)), dev(zz(1), y), dev(zz(-1), y)]
    barrier = pltpu.get_barrier_semaphore()
    for target in ring:
        pl.semaphore_signal(barrier, inc=1, device_id=target, device_id_type=MESH)
    for partner, _ in partners:
        pl.semaphore_signal(barrier, inc=1, device_id=(partner, head), device_id_type=MESH)
    pl.semaphore_wait(barrier, len(ring) + rounds)

    local = pltpu.make_async_copy(w_ref, rows_ref.at[z, y], local_sem)
    local.start()
    R = rows_ref
    yr, yl, zr, zl = dev(z, yy(1)), dev(z, yy(-1)), dev(zz(1), y), dev(zz(-1), y)
    ticks = [
        [(w_ref.at[:, A], R.at[z, y, :, A], yr), (w_ref.at[:, A], R.at[z, y, :, A], yl),
         (w_ref.at[:, B], R.at[z, y, :, B], zr), (w_ref.at[:, B], R.at[z, y, :, B], zl)],
        [(R.at[z, yy(-1), :, A], R.at[z, yy(-1), :, A], yr),
         (R.at[zz(-1), y, :, B], R.at[zz(-1), y, :, B], zr), (R.at[zz(1), y, :, B], R.at[zz(1), y, :, B], zl)],
        [(R.at[z, :, :, A], R.at[z, :, :, A], zr), (R.at[z, :, :, A], R.at[z, :, :, A], zl),
         (R.at[zz(-2), y, :, B], R.at[zz(-2), y, :, B], zr), (R.at[zz(2), y, :, B], R.at[zz(2), y, :, B], zl)],
        [(R.at[zz(-1), :, :, A], R.at[zz(-1), :, :, A], zr), (R.at[zz(1), :, :, A], R.at[zz(1), :, :, A], zl),
         (R.at[zz(-3), y, :, B1], R.at[zz(-3), y, :, B1], zr),
         (R.at[zz(3), y, :, B2], R.at[zz(3), y, :, B2], zl)],
        [(R.at[zz(-2), :, :, A], R.at[zz(-2), :, :, A], zr), (R.at[zz(2), :, :, A], R.at[zz(2), :, :, A], zl),
         (R.at[:, y, :, B], R.at[:, y, :, B], yr), (R.at[:, y, :, B], R.at[:, y, :, B], yl)],
        [(R.at[zz(-3), pl.ds(0, hy), :, A], R.at[zz(-3), pl.ds(0, hy), :, A], zr),
         (R.at[zz(3), pl.ds(hy, ny - hy), :, A], R.at[zz(3), pl.ds(hy, ny - hy), :, A], zl),
         (R.at[pl.ds(0, hz), yy(-1), :, B], R.at[pl.ds(0, hz), yy(-1), :, B], yr),
         (R.at[pl.ds(hz, nz - hz), yy(1), :, B], R.at[pl.ds(hz, nz - hz), yy(1), :, B], yl)],
    ]
    total = value_ref[...]
    partial = jnp.zeros_like(total)
    n = 0
    for t, moves in enumerate(ticks):
        if t == 2:
            local.wait()
        started = []
        for src, dst, target in moves:
            copy = pltpu.make_async_remote_copy(
                src_ref=src, dst_ref=dst, send_sem=send_sem.at[n], recv_sem=recv_sem.at[n],
                device_id=target, device_id_type=MESH,
            )
            copy.start()
            started.append(copy)
            n += 1
        scan = None
        if t < rounds:
            partner, bit = partners[t]
            sent = total.astype(jnp.bfloat16)
            sendbuf[t] = sent
            scan = pltpu.make_async_remote_copy(
                src_ref=sendbuf.at[t], dst_ref=recvbuf.at[t], send_sem=bf_send.at[t],
                recv_sem=bf_recv.at[t], device_id=(partner, head), device_id_type=MESH,
            )
            scan.start()
        for copy in started:
            copy.wait()
        if scan is not None:
            scan.wait()
            other = recvbuf[t].astype(jnp.float32)
            partial = jnp.where(bit == 1, partial + other, partial)
            total = sent.astype(jnp.float32) + other
    partial_ref[...] = partial


def gather_and_scan(value, weight):
    count = lax.axis_size("seq")
    ny = 4
    piece, cols = weight.shape
    rounds = count.bit_length() - 1
    ca = (cols * 2 // 3) // 128 * 128
    n_copies = 23
    return pl.pallas_call(
        functools.partial(gather_kernel, ny, ca),
        out_shape=(
            jax.ShapeDtypeStruct((count // ny, ny, piece, cols), weight.dtype),
            jax.ShapeDtypeStruct(value.shape, jnp.float32),
        ),
        in_specs=[pl.BlockSpec(memory_space=pltpu.VMEM), pl.BlockSpec(memory_space=pl.ANY)],
        out_specs=(pl.BlockSpec(memory_space=pl.ANY), pl.BlockSpec(memory_space=pltpu.VMEM)),
        scratch_shapes=[
            pltpu.VMEM((rounds,) + value.shape, jnp.bfloat16),
            pltpu.VMEM((rounds,) + value.shape, jnp.bfloat16),
            pltpu.SemaphoreType.DMA((n_copies,)),
            pltpu.SemaphoreType.DMA((n_copies,)),
            pltpu.SemaphoreType.DMA((rounds,)),
            pltpu.SemaphoreType.DMA((rounds,)),
            pltpu.SemaphoreType.DMA(()),
        ],
        compiler_params=pltpu.CompilerParams(collective_id=2, has_side_effects=True),
    )(value.astype(jnp.float32), weight)


def normalize(attended):
    return attended * lax.rsqrt(jnp.mean(attended * attended, axis=-1, keepdims=True) + EPS)


def shards(query, key, value, init_state, out_weight, out_grad):
    tok_rows = query.shape[0]
    width = query.shape[1]
    heads_here = init_state.shape[0]
    head_dim = init_state.shape[2]
    queries = query.reshape(tok_rows, heads_here, head_dim)
    key_rows = key.reshape(tok_rows, heads_here, head_dim)
    val_rows = value.reshape(tok_rows, heads_here, head_dim)
    local_state = jnp.einsum("thi,thj->hij", key_rows, val_rows, preferred_element_type=jnp.float32)
    half = out_weight.shape[1] // 2
    gathered, earlier = gather_and_scan(local_state, out_weight[:, :half])
    other_half = lax.all_gather(out_weight[:, half:], "seq", axis=0, tiled=True)
    state_half = (init_state + earlier).astype(jnp.bfloat16)
    row_index = lax.broadcasted_iota(jnp.int32, (tok_rows, tok_rows), 0)
    col_index = lax.broadcasted_iota(jnp.int32, (tok_rows, tok_rows), 1)
    causal = col_index <= row_index
    scores = jnp.einsum("thi,shi->hts", queries, key_rows, preferred_element_type=jnp.float32)
    attn_weights = jnp.where(causal, scores, 0.0).astype(jnp.bfloat16)
    attended = jnp.einsum(
        "hts,shj->thj", attn_weights, val_rows, preferred_element_type=jnp.float32
    )
    attended = attended + jnp.einsum(
        "thi,hij->thj", queries, state_half, preferred_element_type=jnp.float32
    )
    normed = normalize(attended).astype(jnp.bfloat16).reshape(tok_rows, width)
    first_rows = gathered.reshape(-1, half)
    weight_rows = jnp.concatenate([first_rows, other_half], axis=1)
    projected = jnp.dot(normed, weight_rows, preferred_element_type=jnp.float32).astype(jnp.bfloat16)
    projected, first_rows, other_half = lax.optimization_barrier((projected, first_rows, other_half))
    contract = (((1,), (1,)), ((), ()))
    grad_normed = lax.dot_general(
        out_grad[:, :half], first_rows, contract, preferred_element_type=jnp.float32
    ) + lax.dot_general(out_grad[:, half:], other_half, contract, preferred_element_type=jnp.float32)
    mixed = lax.psum_scatter(
        projected, "head", scatter_dimension=1, tiled=True
    )
    _, norm_back = jax.vjp(normalize, attended)
    grad_att = norm_back(grad_normed.reshape(tok_rows, heads_here, head_dim))[0].astype(
        jnp.bfloat16
    )
    own_adjoint = jnp.einsum("thi,thj->hij", queries, grad_att, preferred_element_type=jnp.float32)
    grad_query, grad_key, grad_value, init_grad = backward_pass(
        own_adjoint, query, key, value, grad_att.reshape(tok_rows, width), state_half
    )
    return (mixed, grad_query, grad_key, grad_value, init_grad)


def solution(mesh):
    return jax.shard_map(
        shards,
        mesh=mesh,
        in_specs=(
            P("seq", "head"),
            P("seq", "head"),
            P("seq", "head"),
            P("head", None, None),
            P(("head", "seq"), None),
            P("seq", None),
        ),
        out_specs=(
            P("seq", "head"),
            P("seq", "head"),
            P("seq", "head"),
            P("seq", "head"),
            P("head", None, None),
        ),
        check_vma=False,
    )
```

```python
import functools

import jax
import jax.numpy as jnp
from jax import lax
from jax.experimental import pallas as pl
from jax.experimental.pallas import tpu as pltpu
from jax.sharding import PartitionSpec as P

EPS = 1e-06


MESH = pl.DeviceIdType.MESH


def butterfly_kernel(count, backward, value_ref, partial_ref, total_ref, sendbuf, recvbuf, send_sem, recv_sem):
    me = lax.axis_index("seq")
    head = lax.axis_index("head")
    rounds = count.bit_length() - 1
    partners = []
    for k in range(rounds):
        step = 1 << k
        bit = (me // step) % 2
        partners.append((me + step - 2 * step * bit, bit))
    barrier = pltpu.get_barrier_semaphore()
    for partner, _ in partners:
        pl.semaphore_signal(barrier, inc=1, device_id=(partner, head), device_id_type=MESH)
    pl.semaphore_wait(barrier, rounds)
    total = value_ref[...]
    partial = jnp.zeros_like(total)
    for k, (partner, bit) in enumerate(partners):
        sent = total.astype(jnp.bfloat16)
        sendbuf[k] = sent
        copy = pltpu.make_async_remote_copy(
            src_ref=sendbuf.at[k],
            dst_ref=recvbuf.at[k],
            send_sem=send_sem.at[k],
            recv_sem=recv_sem.at[k],
            device_id=(partner, head),
            device_id_type=MESH,
        )
        copy.start()
        copy.wait()
        other = recvbuf[k].astype(jnp.float32)
        take = (bit == 0) if backward else (bit == 1)
        partial = jnp.where(take, partial + other, partial)
        total = sent.astype(jnp.float32) + other
    partial_ref[...] = partial
    total_ref[...] = total


def butterfly(value, axis, backward):
    count = lax.axis_size(axis)
    rounds = count.bit_length() - 1
    shape = jax.ShapeDtypeStruct(value.shape, jnp.float32)
    return pl.pallas_call(
        functools.partial(butterfly_kernel, count, backward),
        out_shape=(shape, shape),
        in_specs=[pl.BlockSpec(memory_space=pltpu.VMEM)],
        out_specs=(pl.BlockSpec(memory_space=pltpu.VMEM), pl.BlockSpec(memory_space=pltpu.VMEM)),
        scratch_shapes=[
            pltpu.VMEM((rounds,) + value.shape, jnp.bfloat16),
            pltpu.VMEM((rounds,) + value.shape, jnp.bfloat16),
            pltpu.SemaphoreType.DMA((rounds,)),
            pltpu.SemaphoreType.DMA((rounds,)),
        ],
        compiler_params=pltpu.CompilerParams(
            collective_id=1 if backward else 0, has_side_effects=True
        ),
    )(value.astype(jnp.float32))


def backward_kernel(adj_ref, q_hbm, k_hbm, v_hbm, ga_hbm, sh_ref, gq_hbm, gk_hbm, gv_hbm, later_ref, total_ref,
                    sendbuf, recvbuf, send_sem, recv_sem, q_ref, k_ref, v_ref, ga_ref, load_sem,
                    gq_ref, gk_acc, gv_acc, store_sem):
    loads = [pltpu.make_async_copy(src, dst, load_sem.at[i])
             for i, (src, dst) in enumerate([(q_hbm, q_ref), (k_hbm, k_ref), (v_hbm, v_ref), (ga_hbm, ga_ref)])]
    for load in loads:
        load.start()
    me = lax.axis_index("seq")
    head = lax.axis_index("head")
    count = lax.axis_size("seq")
    rounds = count.bit_length() - 1
    heads = sh_ref.shape[0]
    dim = sh_ref.shape[2]
    rows = q_ref.shape[0]
    partners = []
    for k in range(rounds):
        step = 1 << k
        bit = (me // step) % 2
        partners.append((me + step - 2 * step * bit, bit))
    barrier = pltpu.get_barrier_semaphore()
    for partner, _ in partners:
        pl.semaphore_signal(barrier, inc=1, device_id=(partner, head), device_id_type=MESH)
    pl.semaphore_wait(barrier, rounds)
    causal = lax.broadcasted_iota(jnp.int32, (rows, rows), 1) <= lax.broadcasted_iota(jnp.int32, (rows, rows), 0)
    nt = (((1,), (1,)), ((), ()))
    tn = (((0,), (0,)), ((), ()))

    def head_work(h):
        cols = pl.ds(h * dim, dim)
        qh, kh, vh, gah = q_ref[:, cols], k_ref[:, cols], v_ref[:, cols], ga_ref[:, cols]
        gs = lax.dot_general(gah, vh, nt, preferred_element_type=jnp.float32)
        gs = jnp.where(causal, gs, 0.0).astype(jnp.bfloat16)
        aw = lax.dot_general(qh, kh, nt, preferred_element_type=jnp.float32)
        aw = jnp.where(causal, aw, 0.0).astype(jnp.bfloat16)
        gq = jnp.dot(gs, kh, preferred_element_type=jnp.float32)
        gq = gq + lax.dot_general(gah, sh_ref[h], nt, preferred_element_type=jnp.float32)
        gq_ref[:, cols] = gq.astype(gq_ref.dtype)
        gk_acc[:, cols] = lax.dot_general(gs, qh, tn, preferred_element_type=jnp.float32)
        gv_acc[:, cols] = lax.dot_general(aw, gah, tn, preferred_element_type=jnp.float32)

    order = [[] for _ in range(rounds)]
    for h in range(heads):
        order[min(h, rounds - 1)].append(h)
    total = adj_ref[...]
    partial = jnp.zeros_like(total)
    for t, (partner, bit) in enumerate(partners):
        sent = total.astype(jnp.bfloat16)
        sendbuf[t] = sent
        copy = pltpu.make_async_remote_copy(
            src_ref=sendbuf.at[t], dst_ref=recvbuf.at[t], send_sem=send_sem.at[t],
            recv_sem=recv_sem.at[t], device_id=(partner, head), device_id_type=MESH,
        )
        copy.start()
        if t == 0:
            for load in loads:
                load.wait()
        for h in order[t]:
            head_work(h)
        if t == rounds - 1:
            stores = [pltpu.make_async_copy(src, dst, store_sem.at[i])
                      for i, (src, dst) in enumerate([(gq_ref, gq_hbm), (gk_acc, gk_hbm), (gv_acc, gv_hbm)])]
            for store in stores:
                store.start()
        copy.wait()
        other = recvbuf[t].astype(jnp.float32)
        partial = jnp.where(bit == 0, partial + other, partial)
        total = sent.astype(jnp.float32) + other
    total_ref[...] = total
    later_ref[...] = partial.astype(later_ref.dtype)
    for store in stores:
        store.wait()


def finish_kernel(gq_in, gk_acc, gv_acc, v_ref, k_ref, later_ref, gq_ref, gk_ref, gv_ref):
    heads, dim = later_ref.shape[0], later_ref.shape[2]
    nt = (((1,), (1,)), ((), ()))
    gq_ref[...] = gq_in[...]
    for h in range(heads):
        cols = pl.ds(h * dim, dim)
        later = later_ref[h]
        gk = gk_acc[:, cols] + lax.dot_general(v_ref[:, cols], later, nt, preferred_element_type=jnp.float32)
        gk_ref[:, cols] = gk.astype(gk_ref.dtype)
        gv = gv_acc[:, cols] + jnp.dot(k_ref[:, cols], later, preferred_element_type=jnp.float32)
        gv_ref[:, cols] = gv.astype(gv_ref.dtype)


def backward_pass(own_adjoint, query, key, value, grad_att, state_half):
    count = lax.axis_size("seq")
    rounds = count.bit_length() - 1
    tokens = jax.ShapeDtypeStruct(query.shape, jnp.bfloat16)
    vmem = pl.BlockSpec(memory_space=pltpu.VMEM)
    accs = jax.ShapeDtypeStruct(query.shape, jnp.float32)
    gq, gk_acc, gv_acc, later, total = pl.pallas_call(
        backward_kernel,
        out_shape=(tokens, accs, accs, jax.ShapeDtypeStruct(own_adjoint.shape, jnp.bfloat16),
                   jax.ShapeDtypeStruct(own_adjoint.shape, jnp.float32)),
        in_specs=[vmem] + [pl.BlockSpec(memory_space=pl.ANY)] * 4 + [vmem],
        out_specs=(pl.BlockSpec(memory_space=pl.ANY),) * 3 + (vmem, vmem),
        scratch_shapes=[
            pltpu.VMEM((rounds,) + own_adjoint.shape, jnp.bfloat16),
            pltpu.VMEM((rounds,) + own_adjoint.shape, jnp.bfloat16),
            pltpu.SemaphoreType.DMA((rounds,)),
            pltpu.SemaphoreType.DMA((rounds,)),
        ] + [pltpu.VMEM(query.shape, jnp.bfloat16)] * 4 + [pltpu.SemaphoreType.DMA((4,))]
        + [pltpu.VMEM(query.shape, jnp.bfloat16), pltpu.VMEM(query.shape, jnp.float32),
           pltpu.VMEM(query.shape, jnp.float32), pltpu.SemaphoreType.DMA((3,))],
        compiler_params=pltpu.CompilerParams(collective_id=1, has_side_effects=True),
    )(own_adjoint, query, key, value, grad_att, state_half)
    gq, gk, gv = pl.pallas_call(
        finish_kernel,
        out_shape=(tokens, tokens, tokens),
        in_specs=[vmem] * 6,
        out_specs=(vmem,) * 3,
    )(gq, gk_acc, gv_acc, value, key, later)
    return gq, gk, gv, total


def gather_kernel(ny, ca, value_ref, w_ref, rows_ref, partial_ref, sendbuf, recvbuf, send_sem, recv_sem, bf_send, bf_recv, local_sem):
    me = lax.axis_index("seq")
    head = lax.axis_index("head")
    count = lax.axis_size("seq")
    nz = count // ny
    y = me % ny
    z = me // ny
    piece, cols = w_ref.shape
    A = pl.ds(0, ca)
    B = pl.ds(ca, cols - ca)
    hy, hz = ny // 2, nz // 2
    hb = (cols - ca) // 2
    B1 = pl.ds(ca, hb)
    B2 = pl.ds(ca + hb, cols - ca - hb)

    def zz(k):
        return (z + nz + k) % nz

    def yy(k):
        return (y + ny + k) % ny

    def dev(zi, yi):
        return (zi * ny + yi, head)

    rounds = count.bit_length() - 1
    partners = []
    for k in range(rounds):
        step = 1 << k
        bit = (me // step) % 2
        partners.append((me + step - 2 * step * bit, bit))
    ring = [dev(z, yy(1)), dev(z, yy(-1)), dev(zz(1), y), dev(zz(-1), y)]
    barrier = pltpu.get_barrier_semaphore()
    for target in ring:
        pl.semaphore_signal(barrier, inc=1, device_id=target, device_id_type=MESH)
    for partner, _ in partners:
        pl.semaphore_signal(barrier, inc=1, device_id=(partner, head), device_id_type=MESH)
    pl.semaphore_wait(barrier, len(ring) + rounds)

    local = pltpu.make_async_copy(w_ref, rows_ref.at[z, y], local_sem)
    local.start()
    R = rows_ref
    yr, yl, zr, zl = dev(z, yy(1)), dev(z, yy(-1)), dev(zz(1), y), dev(zz(-1), y)
    ticks = [
        [(w_ref.at[:, A], R.at[z, y, :, A], yr), (w_ref.at[:, A], R.at[z, y, :, A], yl),
         (w_ref.at[:, B], R.at[z, y, :, B], zr), (w_ref.at[:, B], R.at[z, y, :, B], zl)],
        [(R.at[z, yy(-1), :, A], R.at[z, yy(-1), :, A], yr),
         (R.at[zz(-1), y, :, B], R.at[zz(-1), y, :, B], zr), (R.at[zz(1), y, :, B], R.at[zz(1), y, :, B], zl)],
        [(R.at[z, :, :, A], R.at[z, :, :, A], zr), (R.at[z, :, :, A], R.at[z, :, :, A], zl),
         (R.at[zz(-2), y, :, B], R.at[zz(-2), y, :, B], zr), (R.at[zz(2), y, :, B], R.at[zz(2), y, :, B], zl)],
        [(R.at[zz(-1), :, :, A], R.at[zz(-1), :, :, A], zr), (R.at[zz(1), :, :, A], R.at[zz(1), :, :, A], zl),
         (R.at[zz(-3), y, :, B1], R.at[zz(-3), y, :, B1], zr),
         (R.at[zz(3), y, :, B2], R.at[zz(3), y, :, B2], zl)],
        [(R.at[zz(-2), :, :, A], R.at[zz(-2), :, :, A], zr), (R.at[zz(2), :, :, A], R.at[zz(2), :, :, A], zl),
         (R.at[:, y, :, B], R.at[:, y, :, B], yr), (R.at[:, y, :, B], R.at[:, y, :, B], yl)],
        [(R.at[zz(-3), pl.ds(0, hy), :, A], R.at[zz(-3), pl.ds(0, hy), :, A], zr),
         (R.at[zz(3), pl.ds(hy, ny - hy), :, A], R.at[zz(3), pl.ds(hy, ny - hy), :, A], zl),
         (R.at[pl.ds(0, hz), yy(-1), :, B], R.at[pl.ds(0, hz), yy(-1), :, B], yr),
         (R.at[pl.ds(hz, nz - hz), yy(1), :, B], R.at[pl.ds(hz, nz - hz), yy(1), :, B], yl)],
    ]
    total = value_ref[...]
    partial = jnp.zeros_like(total)
    n = 0
    for t, moves in enumerate(ticks):
        if t == 2:
            local.wait()
        started = []
        for src, dst, target in moves:
            copy = pltpu.make_async_remote_copy(
                src_ref=src, dst_ref=dst, send_sem=send_sem.at[n], recv_sem=recv_sem.at[n],
                device_id=target, device_id_type=MESH,
            )
            copy.start()
            started.append(copy)
            n += 1
        scan = None
        if t < rounds:
            partner, bit = partners[t]
            sent = total.astype(jnp.bfloat16)
            sendbuf[t] = sent
            scan = pltpu.make_async_remote_copy(
                src_ref=sendbuf.at[t], dst_ref=recvbuf.at[t], send_sem=bf_send.at[t],
                recv_sem=bf_recv.at[t], device_id=(partner, head), device_id_type=MESH,
            )
            scan.start()
        for copy in started:
            copy.wait()
        if scan is not None:
            scan.wait()
            other = recvbuf[t].astype(jnp.float32)
            partial = jnp.where(bit == 1, partial + other, partial)
            total = sent.astype(jnp.float32) + other
    partial_ref[...] = partial


def gather_and_scan(value, weight):
    count = lax.axis_size("seq")
    ny = 4
    piece, cols = weight.shape
    rounds = count.bit_length() - 1
    ca = (cols * 2 // 3) // 128 * 128
    n_copies = 23
    return pl.pallas_call(
        functools.partial(gather_kernel, ny, ca),
        out_shape=(
            jax.ShapeDtypeStruct((count // ny, ny, piece, cols), weight.dtype),
            jax.ShapeDtypeStruct(value.shape, jnp.float32),
        ),
        in_specs=[pl.BlockSpec(memory_space=pltpu.VMEM), pl.BlockSpec(memory_space=pl.ANY)],
        out_specs=(pl.BlockSpec(memory_space=pl.ANY), pl.BlockSpec(memory_space=pltpu.VMEM)),
        scratch_shapes=[
            pltpu.VMEM((rounds,) + value.shape, jnp.bfloat16),
            pltpu.VMEM((rounds,) + value.shape, jnp.bfloat16),
            pltpu.SemaphoreType.DMA((n_copies,)),
            pltpu.SemaphoreType.DMA((n_copies,)),
            pltpu.SemaphoreType.DMA((rounds,)),
            pltpu.SemaphoreType.DMA((rounds,)),
            pltpu.SemaphoreType.DMA(()),
        ],
        compiler_params=pltpu.CompilerParams(collective_id=2, has_side_effects=True),
    )(value.astype(jnp.float32), weight)


def normalize(attended):
    return attended * lax.rsqrt(jnp.mean(attended * attended, axis=-1, keepdims=True) + EPS)


def shards(query, key, value, init_state, out_weight, out_grad):
    tok_rows = query.shape[0]
    width = query.shape[1]
    heads_here = init_state.shape[0]
    head_dim = init_state.shape[2]
    queries = query.reshape(tok_rows, heads_here, head_dim)
    key_rows = key.reshape(tok_rows, heads_here, head_dim)
    val_rows = value.reshape(tok_rows, heads_here, head_dim)
    local_state = jnp.einsum("thi,thj->hij", key_rows, val_rows, preferred_element_type=jnp.float32)
    half = out_weight.shape[1] // 2
    gathered, earlier = gather_and_scan(local_state, out_weight[:, :half])
    other_half = lax.all_gather(out_weight[:, half:], "seq", axis=0, tiled=True)
    state_half = (init_state + earlier).astype(jnp.bfloat16)
    row_index = lax.broadcasted_iota(jnp.int32, (tok_rows, tok_rows), 0)
    col_index = lax.broadcasted_iota(jnp.int32, (tok_rows, tok_rows), 1)
    causal = col_index <= row_index
    scores = jnp.einsum("thi,shi->hts", queries, key_rows, preferred_element_type=jnp.float32)
    attn_weights = jnp.where(causal, scores, 0.0).astype(jnp.bfloat16)
    attended = jnp.einsum(
        "hts,shj->thj", attn_weights, val_rows, preferred_element_type=jnp.float32
    )
    attended = attended + jnp.einsum(
        "thi,hij->thj", queries, state_half, preferred_element_type=jnp.float32
    )
    normed = normalize(attended).astype(jnp.bfloat16).reshape(tok_rows, width)
    first_rows = gathered.reshape(-1, half)
    weight_rows = jnp.concatenate([first_rows, other_half], axis=1)
    projected = jnp.dot(normed, weight_rows, preferred_element_type=jnp.float32).astype(jnp.bfloat16)
    projected, first_rows, other_half = lax.optimization_barrier((projected, first_rows, other_half))
    contract = (((1,), (1,)), ((), ()))
    grad_normed = lax.dot_general(
        out_grad[:, :half], first_rows, contract, preferred_element_type=jnp.float32
    ) + lax.dot_general(out_grad[:, half:], other_half, contract, preferred_element_type=jnp.float32)
    mixed = lax.psum_scatter(
        projected, "head", scatter_dimension=1, tiled=True
    )
    _, norm_back = jax.vjp(normalize, attended)
    grad_att = norm_back(grad_normed.reshape(tok_rows, heads_here, head_dim))[0].astype(
        jnp.bfloat16
    )
    own_adjoint = jnp.einsum("thi,thj->hij", queries, grad_att, preferred_element_type=jnp.float32)
    grad_query, grad_key, grad_value, init_grad = backward_pass(
        own_adjoint, query, key, value, grad_att.reshape(tok_rows, width), state_half
    )
    return (mixed, grad_query, grad_key, grad_value, init_grad)


def solution(mesh):
    return jax.shard_map(
        shards,
        mesh=mesh,
        in_specs=(
            P("seq", "head"),
            P("seq", "head"),
            P("seq", "head"),
            P("head", None, None),
            P(("head", "seq"), None),
            P("seq", None),
        ),
        out_specs=(
            P("seq", "head"),
            P("seq", "head"),
            P("seq", "head"),
            P("seq", "head"),
            P("head", None, None),
        ),
        check_vma=False,
    )
```

```python
import functools

import jax
import jax.numpy as jnp
from jax import lax
from jax.experimental import pallas as pl
from jax.experimental.pallas import tpu as pltpu
from jax.sharding import PartitionSpec as P

EPS = 1e-06


MESH = pl.DeviceIdType.MESH


def butterfly_kernel(count, backward, value_ref, partial_ref, total_ref, sendbuf, recvbuf, send_sem, recv_sem):
    me = lax.axis_index("seq")
    head = lax.axis_index("head")
    rounds = count.bit_length() - 1
    partners = []
    for k in range(rounds):
        step = 1 << k
        bit = (me // step) % 2
        partners.append((me + step - 2 * step * bit, bit))
    barrier = pltpu.get_barrier_semaphore()
    for partner, _ in partners:
        pl.semaphore_signal(barrier, inc=1, device_id=(partner, head), device_id_type=MESH)
    pl.semaphore_wait(barrier, rounds)
    total = value_ref[...]
    partial = jnp.zeros_like(total)
    for k, (partner, bit) in enumerate(partners):
        sent = total.astype(jnp.bfloat16)
        sendbuf[k] = sent
        copy = pltpu.make_async_remote_copy(
            src_ref=sendbuf.at[k],
            dst_ref=recvbuf.at[k],
            send_sem=send_sem.at[k],
            recv_sem=recv_sem.at[k],
            device_id=(partner, head),
            device_id_type=MESH,
        )
        copy.start()
        copy.wait()
        other = recvbuf[k].astype(jnp.float32)
        take = (bit == 0) if backward else (bit == 1)
        partial = jnp.where(take, partial + other, partial)
        total = sent.astype(jnp.float32) + other
    partial_ref[...] = partial
    total_ref[...] = total


def butterfly(value, axis, backward):
    count = lax.axis_size(axis)
    rounds = count.bit_length() - 1
    shape = jax.ShapeDtypeStruct(value.shape, jnp.float32)
    return pl.pallas_call(
        functools.partial(butterfly_kernel, count, backward),
        out_shape=(shape, shape),
        in_specs=[pl.BlockSpec(memory_space=pltpu.VMEM)],
        out_specs=(pl.BlockSpec(memory_space=pltpu.VMEM), pl.BlockSpec(memory_space=pltpu.VMEM)),
        scratch_shapes=[
            pltpu.VMEM((rounds,) + value.shape, jnp.bfloat16),
            pltpu.VMEM((rounds,) + value.shape, jnp.bfloat16),
            pltpu.SemaphoreType.DMA((rounds,)),
            pltpu.SemaphoreType.DMA((rounds,)),
        ],
        compiler_params=pltpu.CompilerParams(
            collective_id=1 if backward else 0, has_side_effects=True
        ),
    )(value.astype(jnp.float32))


def backward_kernel(adj_ref, q_hbm, k_hbm, v_hbm, ga_hbm, sh_ref, gq_hbm, gk_hbm, gv_hbm, later_ref, total_ref,
                    sendbuf, recvbuf, send_sem, recv_sem, q_ref, k_ref, v_ref, ga_ref, load_sem,
                    gq_ref, gk_acc, gv_acc, store_sem):
    loads = [pltpu.make_async_copy(src, dst, load_sem.at[i])
             for i, (src, dst) in enumerate([(q_hbm, q_ref), (k_hbm, k_ref), (v_hbm, v_ref), (ga_hbm, ga_ref)])]
    for load in loads:
        load.start()
    me = lax.axis_index("seq")
    head = lax.axis_index("head")
    count = lax.axis_size("seq")
    rounds = count.bit_length() - 1
    heads = sh_ref.shape[0]
    dim = sh_ref.shape[2]
    rows = q_ref.shape[0]
    partners = []
    for k in range(rounds):
        step = 1 << k
        bit = (me // step) % 2
        partners.append((me + step - 2 * step * bit, bit))
    barrier = pltpu.get_barrier_semaphore()
    for partner, _ in partners:
        pl.semaphore_signal(barrier, inc=1, device_id=(partner, head), device_id_type=MESH)
    pl.semaphore_wait(barrier, rounds)
    causal = lax.broadcasted_iota(jnp.int32, (rows, rows), 1) <= lax.broadcasted_iota(jnp.int32, (rows, rows), 0)
    nt = (((1,), (1,)), ((), ()))
    tn = (((0,), (0,)), ((), ()))

    def head_work(h):
        cols = pl.ds(h * dim, dim)
        qh, kh, vh, gah = q_ref[:, cols], k_ref[:, cols], v_ref[:, cols], ga_ref[:, cols]
        gs = lax.dot_general(gah, vh, nt, preferred_element_type=jnp.float32)
        gs = jnp.where(causal, gs, 0.0).astype(jnp.bfloat16)
        aw = lax.dot_general(qh, kh, nt, preferred_element_type=jnp.float32)
        aw = jnp.where(causal, aw, 0.0).astype(jnp.bfloat16)
        gq = jnp.dot(gs, kh, preferred_element_type=jnp.float32)
        gq = gq + lax.dot_general(gah, sh_ref[h], nt, preferred_element_type=jnp.float32)
        gq_ref[:, cols] = gq.astype(gq_ref.dtype)
        gk_acc[:, cols] = lax.dot_general(gs, qh, tn, preferred_element_type=jnp.float32)
        gv_acc[:, cols] = lax.dot_general(aw, gah, tn, preferred_element_type=jnp.float32)

    order = [[] for _ in range(rounds)]
    for h in range(heads):
        order[min(h, rounds - 1)].append(h)
    total = adj_ref[...]
    partial = jnp.zeros_like(total)
    for t, (partner, bit) in enumerate(partners):
        sent = total.astype(jnp.bfloat16)
        sendbuf[t] = sent
        copy = pltpu.make_async_remote_copy(
            src_ref=sendbuf.at[t], dst_ref=recvbuf.at[t], send_sem=send_sem.at[t],
            recv_sem=recv_sem.at[t], device_id=(partner, head), device_id_type=MESH,
        )
        copy.start()
        if t == 0:
            for load in loads:
                load.wait()
        for h in order[t]:
            head_work(h)
        if t == rounds - 1:
            stores = [pltpu.make_async_copy(src, dst, store_sem.at[i])
                      for i, (src, dst) in enumerate([(gq_ref, gq_hbm), (gk_acc, gk_hbm), (gv_acc, gv_hbm)])]
            for store in stores:
                store.start()
        copy.wait()
        other = recvbuf[t].astype(jnp.float32)
        partial = jnp.where(bit == 0, partial + other, partial)
        total = sent.astype(jnp.float32) + other
    total_ref[...] = total
    later_ref[...] = partial.astype(later_ref.dtype)
    for store in stores:
        store.wait()


def finish_kernel(gq_in, gk_hbm, gv_hbm, v_hbm, k_hbm, later_ref, gq_ref, gk_ref, gv_ref,
                  gk_acc, gv_acc, v_ref, k_ref, sems):
    heads, dim = later_ref.shape[0], later_ref.shape[2]
    nt = (((1,), (1,)), ((), ()))
    loads = [pltpu.make_async_copy(src, dst, sems.at[i]) for i, (src, dst) in
             enumerate([(gk_hbm, gk_acc), (v_hbm, v_ref), (gv_hbm, gv_acc), (k_hbm, k_ref)])]
    for load in loads:
        load.start()
    gq_ref[...] = gq_in[...]
    loads[0].wait()
    loads[1].wait()
    for h in range(heads):
        cols = pl.ds(h * dim, dim)
        gk = gk_acc[:, cols] + lax.dot_general(v_ref[:, cols], later_ref[h], nt, preferred_element_type=jnp.float32)
        gk_ref[:, cols] = gk.astype(gk_ref.dtype)
    loads[2].wait()
    loads[3].wait()
    for h in range(heads):
        cols = pl.ds(h * dim, dim)
        gv = gv_acc[:, cols] + jnp.dot(k_ref[:, cols], later_ref[h], preferred_element_type=jnp.float32)
        gv_ref[:, cols] = gv.astype(gv_ref.dtype)


def backward_pass(own_adjoint, query, key, value, grad_att, state_half):
    count = lax.axis_size("seq")
    rounds = count.bit_length() - 1
    tokens = jax.ShapeDtypeStruct(query.shape, jnp.bfloat16)
    vmem = pl.BlockSpec(memory_space=pltpu.VMEM)
    accs = jax.ShapeDtypeStruct(query.shape, jnp.float32)
    gq, gk_acc, gv_acc, later, total = pl.pallas_call(
        backward_kernel,
        out_shape=(tokens, accs, accs, jax.ShapeDtypeStruct(own_adjoint.shape, jnp.bfloat16),
                   jax.ShapeDtypeStruct(own_adjoint.shape, jnp.float32)),
        in_specs=[vmem] + [pl.BlockSpec(memory_space=pl.ANY)] * 4 + [vmem],
        out_specs=(pl.BlockSpec(memory_space=pl.ANY),) * 3 + (vmem, vmem),
        scratch_shapes=[
            pltpu.VMEM((rounds,) + own_adjoint.shape, jnp.bfloat16),
            pltpu.VMEM((rounds,) + own_adjoint.shape, jnp.bfloat16),
            pltpu.SemaphoreType.DMA((rounds,)),
            pltpu.SemaphoreType.DMA((rounds,)),
        ] + [pltpu.VMEM(query.shape, jnp.bfloat16)] * 4 + [pltpu.SemaphoreType.DMA((4,))]
        + [pltpu.VMEM(query.shape, jnp.bfloat16), pltpu.VMEM(query.shape, jnp.float32),
           pltpu.VMEM(query.shape, jnp.float32), pltpu.SemaphoreType.DMA((3,))],
        compiler_params=pltpu.CompilerParams(collective_id=1, has_side_effects=True),
    )(own_adjoint, query, key, value, grad_att, state_half)
    gq, gk, gv = pl.pallas_call(
        finish_kernel,
        out_shape=(tokens, tokens, tokens),
        in_specs=[vmem] + [pl.BlockSpec(memory_space=pl.ANY)] * 4 + [vmem],
        out_specs=(vmem,) * 3,
        scratch_shapes=[pltpu.VMEM(query.shape, jnp.float32), pltpu.VMEM(query.shape, jnp.float32),
                        pltpu.VMEM(query.shape, jnp.bfloat16), pltpu.VMEM(query.shape, jnp.bfloat16),
                        pltpu.SemaphoreType.DMA((4,))],
    )(gq, gk_acc, gv_acc, value, key, later)
    return gq, gk, gv, total


def gather_kernel(ny, ca, value_ref, w_ref, rows_ref, partial_ref, sendbuf, recvbuf, send_sem, recv_sem, bf_send, bf_recv, local_sem):
    me = lax.axis_index("seq")
    head = lax.axis_index("head")
    count = lax.axis_size("seq")
    nz = count // ny
    y = me % ny
    z = me // ny
    piece, cols = w_ref.shape
    A = pl.ds(0, ca)
    B = pl.ds(ca, cols - ca)
    hy, hz = ny // 2, nz // 2
    hb = (cols - ca) // 2
    B1 = pl.ds(ca, hb)
    B2 = pl.ds(ca + hb, cols - ca - hb)

    def zz(k):
        return (z + nz + k) % nz

    def yy(k):
        return (y + ny + k) % ny

    def dev(zi, yi):
        return (zi * ny + yi, head)

    rounds = count.bit_length() - 1
    partners = []
    for k in range(rounds):
        step = 1 << k
        bit = (me // step) % 2
        partners.append((me + step - 2 * step * bit, bit))
    ring = [dev(z, yy(1)), dev(z, yy(-1)), dev(zz(1), y), dev(zz(-1), y)]
    barrier = pltpu.get_barrier_semaphore()
    for target in ring:
        pl.semaphore_signal(barrier, inc=1, device_id=target, device_id_type=MESH)
    for partner, _ in partners:
        pl.semaphore_signal(barrier, inc=1, device_id=(partner, head), device_id_type=MESH)
    pl.semaphore_wait(barrier, len(ring) + rounds)

    local = pltpu.make_async_copy(w_ref, rows_ref.at[z, y], local_sem)
    local.start()
    R = rows_ref
    yr, yl, zr, zl = dev(z, yy(1)), dev(z, yy(-1)), dev(zz(1), y), dev(zz(-1), y)
    ticks = [
        [(w_ref.at[:, A], R.at[z, y, :, A], yr), (w_ref.at[:, A], R.at[z, y, :, A], yl),
         (w_ref.at[:, B], R.at[z, y, :, B], zr), (w_ref.at[:, B], R.at[z, y, :, B], zl)],
        [(R.at[z, yy(-1), :, A], R.at[z, yy(-1), :, A], yr),
         (R.at[zz(-1), y, :, B], R.at[zz(-1), y, :, B], zr), (R.at[zz(1), y, :, B], R.at[zz(1), y, :, B], zl)],
        [(R.at[z, :, :, A], R.at[z, :, :, A], zr), (R.at[z, :, :, A], R.at[z, :, :, A], zl),
         (R.at[zz(-2), y, :, B], R.at[zz(-2), y, :, B], zr), (R.at[zz(2), y, :, B], R.at[zz(2), y, :, B], zl)],
        [(R.at[zz(-1), :, :, A], R.at[zz(-1), :, :, A], zr), (R.at[zz(1), :, :, A], R.at[zz(1), :, :, A], zl),
         (R.at[zz(-3), y, :, B1], R.at[zz(-3), y, :, B1], zr),
         (R.at[zz(3), y, :, B2], R.at[zz(3), y, :, B2], zl)],
        [(R.at[zz(-2), :, :, A], R.at[zz(-2), :, :, A], zr), (R.at[zz(2), :, :, A], R.at[zz(2), :, :, A], zl),
         (R.at[:, y, :, B], R.at[:, y, :, B], yr), (R.at[:, y, :, B], R.at[:, y, :, B], yl)],
        [(R.at[zz(-3), pl.ds(0, hy), :, A], R.at[zz(-3), pl.ds(0, hy), :, A], zr),
         (R.at[zz(3), pl.ds(hy, ny - hy), :, A], R.at[zz(3), pl.ds(hy, ny - hy), :, A], zl),
         (R.at[pl.ds(0, hz), yy(-1), :, B], R.at[pl.ds(0, hz), yy(-1), :, B], yr),
         (R.at[pl.ds(hz, nz - hz), yy(1), :, B], R.at[pl.ds(hz, nz - hz), yy(1), :, B], yl)],
    ]
    total = value_ref[...]
    partial = jnp.zeros_like(total)
    n = 0
    for t, moves in enumerate(ticks):
        if t == 2:
            local.wait()
        started = []
        for src, dst, target in moves:
            copy = pltpu.make_async_remote_copy(
                src_ref=src, dst_ref=dst, send_sem=send_sem.at[n], recv_sem=recv_sem.at[n],
                device_id=target, device_id_type=MESH,
            )
            copy.start()
            started.append(copy)
            n += 1
        scan = None
        if t < rounds:
            partner, bit = partners[t]
            sent = total.astype(jnp.bfloat16)
            sendbuf[t] = sent
            scan = pltpu.make_async_remote_copy(
                src_ref=sendbuf.at[t], dst_ref=recvbuf.at[t], send_sem=bf_send.at[t],
                recv_sem=bf_recv.at[t], device_id=(partner, head), device_id_type=MESH,
            )
            scan.start()
        for copy in started:
            copy.wait()
        if scan is not None:
            scan.wait()
            other = recvbuf[t].astype(jnp.float32)
            partial = jnp.where(bit == 1, partial + other, partial)
            total = sent.astype(jnp.float32) + other
    partial_ref[...] = partial


def gather_and_scan(value, weight):
    count = lax.axis_size("seq")
    ny = 4
    piece, cols = weight.shape
    rounds = count.bit_length() - 1
    ca = (cols * 2 // 3) // 128 * 128
    n_copies = 23
    return pl.pallas_call(
        functools.partial(gather_kernel, ny, ca),
        out_shape=(
            jax.ShapeDtypeStruct((count // ny, ny, piece, cols), weight.dtype),
            jax.ShapeDtypeStruct(value.shape, jnp.float32),
        ),
        in_specs=[pl.BlockSpec(memory_space=pltpu.VMEM), pl.BlockSpec(memory_space=pl.ANY)],
        out_specs=(pl.BlockSpec(memory_space=pl.ANY), pl.BlockSpec(memory_space=pltpu.VMEM)),
        scratch_shapes=[
            pltpu.VMEM((rounds,) + value.shape, jnp.bfloat16),
            pltpu.VMEM((rounds,) + value.shape, jnp.bfloat16),
            pltpu.SemaphoreType.DMA((n_copies,)),
            pltpu.SemaphoreType.DMA((n_copies,)),
            pltpu.SemaphoreType.DMA((rounds,)),
            pltpu.SemaphoreType.DMA((rounds,)),
            pltpu.SemaphoreType.DMA(()),
        ],
        compiler_params=pltpu.CompilerParams(collective_id=2, has_side_effects=True),
    )(value.astype(jnp.float32), weight)


def normalize(attended):
    return attended * lax.rsqrt(jnp.mean(attended * attended, axis=-1, keepdims=True) + EPS)


def shards(query, key, value, init_state, out_weight, out_grad):
    tok_rows = query.shape[0]
    width = query.shape[1]
    heads_here = init_state.shape[0]
    head_dim = init_state.shape[2]
    queries = query.reshape(tok_rows, heads_here, head_dim)
    key_rows = key.reshape(tok_rows, heads_here, head_dim)
    val_rows = value.reshape(tok_rows, heads_here, head_dim)
    local_state = jnp.einsum("thi,thj->hij", key_rows, val_rows, preferred_element_type=jnp.float32)
    half = out_weight.shape[1] // 2
    gathered, earlier = gather_and_scan(local_state, out_weight[:, :half])
    other_half = lax.all_gather(out_weight[:, half:], "seq", axis=0, tiled=True)
    state_half = (init_state + earlier).astype(jnp.bfloat16)
    row_index = lax.broadcasted_iota(jnp.int32, (tok_rows, tok_rows), 0)
    col_index = lax.broadcasted_iota(jnp.int32, (tok_rows, tok_rows), 1)
    causal = col_index <= row_index
    scores = jnp.einsum("thi,shi->hts", queries, key_rows, preferred_element_type=jnp.float32)
    attn_weights = jnp.where(causal, scores, 0.0).astype(jnp.bfloat16)
    attended = jnp.einsum(
        "hts,shj->thj", attn_weights, val_rows, preferred_element_type=jnp.float32
    )
    attended = attended + jnp.einsum(
        "thi,hij->thj", queries, state_half, preferred_element_type=jnp.float32
    )
    normed = normalize(attended).astype(jnp.bfloat16).reshape(tok_rows, width)
    first_rows = gathered.reshape(-1, half)
    weight_rows = jnp.concatenate([first_rows, other_half], axis=1)
    projected = jnp.dot(normed, weight_rows, preferred_element_type=jnp.float32).astype(jnp.bfloat16)
    projected, first_rows, other_half = lax.optimization_barrier((projected, first_rows, other_half))
    contract = (((1,), (1,)), ((), ()))
    grad_normed = lax.dot_general(
        out_grad[:, :half], first_rows, contract, preferred_element_type=jnp.float32
    ) + lax.dot_general(out_grad[:, half:], other_half, contract, preferred_element_type=jnp.float32)
    mixed = lax.psum_scatter(
        projected, "head", scatter_dimension=1, tiled=True
    )
    _, norm_back = jax.vjp(normalize, attended)
    grad_att = norm_back(grad_normed.reshape(tok_rows, heads_here, head_dim))[0].astype(
        jnp.bfloat16
    )
    own_adjoint = jnp.einsum("thi,thj->hij", queries, grad_att, preferred_element_type=jnp.float32)
    grad_query, grad_key, grad_value, init_grad = backward_pass(
        own_adjoint, query, key, value, grad_att.reshape(tok_rows, width), state_half
    )
    return (mixed, grad_query, grad_key, grad_value, init_grad)


def solution(mesh):
    return jax.shard_map(
        shards,
        mesh=mesh,
        in_specs=(
            P("seq", "head"),
            P("seq", "head"),
            P("seq", "head"),
            P("head", None, None),
            P(("head", "seq"), None),
            P("seq", None),
        ),
        out_specs=(
            P("seq", "head"),
            P("seq", "head"),
            P("seq", "head"),
            P("seq", "head"),
            P("head", None, None),
        ),
        check_vma=False,
    )
```

```python
import functools

import jax
import jax.numpy as jnp
from jax import lax
from jax.experimental import pallas as pl
from jax.experimental.pallas import tpu as pltpu
from jax.sharding import PartitionSpec as P

EPS = 1e-06


MESH = pl.DeviceIdType.MESH


def butterfly_kernel(count, backward, value_ref, partial_ref, total_ref, sendbuf, recvbuf, send_sem, recv_sem):
    me = lax.axis_index("seq")
    head = lax.axis_index("head")
    rounds = count.bit_length() - 1
    partners = []
    for k in range(rounds):
        step = 1 << k
        bit = (me // step) % 2
        partners.append((me + step - 2 * step * bit, bit))
    barrier = pltpu.get_barrier_semaphore()
    for partner, _ in partners:
        pl.semaphore_signal(barrier, inc=1, device_id=(partner, head), device_id_type=MESH)
    pl.semaphore_wait(barrier, rounds)
    total = value_ref[...]
    partial = jnp.zeros_like(total)
    for k, (partner, bit) in enumerate(partners):
        sent = total.astype(jnp.bfloat16)
        sendbuf[k] = sent
        copy = pltpu.make_async_remote_copy(
            src_ref=sendbuf.at[k],
            dst_ref=recvbuf.at[k],
            send_sem=send_sem.at[k],
            recv_sem=recv_sem.at[k],
            device_id=(partner, head),
            device_id_type=MESH,
        )
        copy.start()
        copy.wait()
        other = recvbuf[k].astype(jnp.float32)
        take = (bit == 0) if backward else (bit == 1)
        partial = jnp.where(take, partial + other, partial)
        total = sent.astype(jnp.float32) + other
    partial_ref[...] = partial
    total_ref[...] = total


def butterfly(value, axis, backward):
    count = lax.axis_size(axis)
    rounds = count.bit_length() - 1
    shape = jax.ShapeDtypeStruct(value.shape, jnp.float32)
    return pl.pallas_call(
        functools.partial(butterfly_kernel, count, backward),
        out_shape=(shape, shape),
        in_specs=[pl.BlockSpec(memory_space=pltpu.VMEM)],
        out_specs=(pl.BlockSpec(memory_space=pltpu.VMEM), pl.BlockSpec(memory_space=pltpu.VMEM)),
        scratch_shapes=[
            pltpu.VMEM((rounds,) + value.shape, jnp.bfloat16),
            pltpu.VMEM((rounds,) + value.shape, jnp.bfloat16),
            pltpu.SemaphoreType.DMA((rounds,)),
            pltpu.SemaphoreType.DMA((rounds,)),
        ],
        compiler_params=pltpu.CompilerParams(
            collective_id=1 if backward else 0, has_side_effects=True
        ),
    )(value.astype(jnp.float32))


def backward_kernel(adj_ref, q_hbm, k_hbm, v_hbm, ga_hbm, sh_ref, gq_hbm, gk_hbm, gv_hbm, later_ref, total_ref,
                    sendbuf, recvbuf, send_sem, recv_sem, q_ref, k_ref, v_ref, ga_ref, load_sem,
                    gq_ref, gk_acc, gv_acc, store_sem):
    loads = [pltpu.make_async_copy(src, dst, load_sem.at[i])
             for i, (src, dst) in enumerate([(q_hbm, q_ref), (k_hbm, k_ref), (v_hbm, v_ref), (ga_hbm, ga_ref)])]
    for load in loads:
        load.start()
    me = lax.axis_index("seq")
    head = lax.axis_index("head")
    count = lax.axis_size("seq")
    rounds = count.bit_length() - 1
    heads = sh_ref.shape[0]
    dim = sh_ref.shape[2]
    rows = q_ref.shape[0]
    partners = []
    for k in range(rounds):
        step = 1 << k
        bit = (me // step) % 2
        partners.append((me + step - 2 * step * bit, bit))
    barrier = pltpu.get_barrier_semaphore()
    for partner, _ in partners:
        pl.semaphore_signal(barrier, inc=1, device_id=(partner, head), device_id_type=MESH)
    pl.semaphore_wait(barrier, rounds)
    causal = lax.broadcasted_iota(jnp.int32, (rows, rows), 1) <= lax.broadcasted_iota(jnp.int32, (rows, rows), 0)
    nt = (((1,), (1,)), ((), ()))
    tn = (((0,), (0,)), ((), ()))

    def head_work(h):
        cols = pl.ds(h * dim, dim)
        qh, kh, vh, gah = q_ref[:, cols], k_ref[:, cols], v_ref[:, cols], ga_ref[:, cols]
        gs = lax.dot_general(gah, vh, nt, preferred_element_type=jnp.float32)
        gs = jnp.where(causal, gs, 0.0).astype(jnp.bfloat16)
        aw = lax.dot_general(qh, kh, nt, preferred_element_type=jnp.float32)
        aw = jnp.where(causal, aw, 0.0).astype(jnp.bfloat16)
        gq = jnp.dot(gs, kh, preferred_element_type=jnp.float32)
        gq = gq + lax.dot_general(gah, sh_ref[h], nt, preferred_element_type=jnp.float32)
        gq_ref[:, cols] = gq.astype(gq_ref.dtype)
        gk_acc[:, cols] = lax.dot_general(gs, qh, tn, preferred_element_type=jnp.float32)
        gv_acc[:, cols] = lax.dot_general(aw, gah, tn, preferred_element_type=jnp.float32)

    order = [[] for _ in range(rounds)]
    for h in range(heads):
        order[min(h, rounds - 1)].append(h)
    total = adj_ref[...]
    partial = jnp.zeros_like(total)
    for t, (partner, bit) in enumerate(partners):
        sent = total.astype(jnp.bfloat16)
        sendbuf[t] = sent
        copy = pltpu.make_async_remote_copy(
            src_ref=sendbuf.at[t], dst_ref=recvbuf.at[t], send_sem=send_sem.at[t],
            recv_sem=recv_sem.at[t], device_id=(partner, head), device_id_type=MESH,
        )
        copy.start()
        if t == 0:
            for load in loads:
                load.wait()
        for h in order[t]:
            head_work(h)
        if t == rounds - 1:
            stores = [pltpu.make_async_copy(src, dst, store_sem.at[i])
                      for i, (src, dst) in enumerate([(gq_ref, gq_hbm), (gk_acc, gk_hbm), (gv_acc, gv_hbm)])]
            for store in stores:
                store.start()
        copy.wait()
        other = recvbuf[t].astype(jnp.float32)
        partial = jnp.where(bit == 0, partial + other, partial)
        total = sent.astype(jnp.float32) + other
    total_ref[...] = total
    later_ref[...] = partial.astype(later_ref.dtype)
    for store in stores:
        store.wait()


def finish_kernel(gq_in, gk_acc, gv_acc, v_ref, k_ref, later_ref, gq_ref, gk_ref, gv_ref):
    heads, dim = later_ref.shape[0], later_ref.shape[2]
    nt = (((1,), (1,)), ((), ()))
    gq_ref[...] = gq_in[...]
    for h in range(heads):
        cols = pl.ds(h * dim, dim)
        later = later_ref[h]
        gk = gk_acc[:, cols] + lax.dot_general(v_ref[:, cols], later, nt, preferred_element_type=jnp.float32)
        gk_ref[:, cols] = gk.astype(gk_ref.dtype)
        gv = gv_acc[:, cols] + jnp.dot(k_ref[:, cols], later, preferred_element_type=jnp.float32)
        gv_ref[:, cols] = gv.astype(gv_ref.dtype)


def backward_pass(own_adjoint, query, key, value, grad_att, state_half):
    count = lax.axis_size("seq")
    rounds = count.bit_length() - 1
    tokens = jax.ShapeDtypeStruct(query.shape, jnp.bfloat16)
    vmem = pl.BlockSpec(memory_space=pltpu.VMEM)
    accs = jax.ShapeDtypeStruct(query.shape, jnp.float32)
    gq, gk_acc, gv_acc, later, total = pl.pallas_call(
        backward_kernel,
        out_shape=(tokens, accs, accs, jax.ShapeDtypeStruct(own_adjoint.shape, jnp.bfloat16),
                   jax.ShapeDtypeStruct(own_adjoint.shape, jnp.float32)),
        in_specs=[vmem] + [pl.BlockSpec(memory_space=pl.ANY)] * 4 + [vmem],
        out_specs=(pl.BlockSpec(memory_space=pl.ANY),) * 3 + (vmem, vmem),
        scratch_shapes=[
            pltpu.VMEM((rounds,) + own_adjoint.shape, jnp.bfloat16),
            pltpu.VMEM((rounds,) + own_adjoint.shape, jnp.bfloat16),
            pltpu.SemaphoreType.DMA((rounds,)),
            pltpu.SemaphoreType.DMA((rounds,)),
        ] + [pltpu.VMEM(query.shape, jnp.bfloat16)] * 4 + [pltpu.SemaphoreType.DMA((4,))]
        + [pltpu.VMEM(query.shape, jnp.bfloat16), pltpu.VMEM(query.shape, jnp.float32),
           pltpu.VMEM(query.shape, jnp.float32), pltpu.SemaphoreType.DMA((3,))],
        compiler_params=pltpu.CompilerParams(collective_id=1, has_side_effects=True),
    )(own_adjoint, query, key, value, grad_att, state_half)
    gq, gk, gv = pl.pallas_call(
        finish_kernel,
        out_shape=(tokens, tokens, tokens),
        in_specs=[vmem] * 6,
        out_specs=(vmem,) * 3,
    )(gq, gk_acc, gv_acc, value, key, later)
    return gq, gk, gv, total


def gather_kernel(ny, ca, k_hbm, v_hbm, w_ref, rows_ref, partial_ref, sendbuf, recvbuf, send_sem, recv_sem, bf_send, bf_recv, local_sem,
                  k_ref, v_ref, load_sem):
    loads = [pltpu.make_async_copy(k_hbm, k_ref, load_sem.at[0]), pltpu.make_async_copy(v_hbm, v_ref, load_sem.at[1])]
    for load in loads:
        load.start()
    me = lax.axis_index("seq")
    head = lax.axis_index("head")
    count = lax.axis_size("seq")
    nz = count // ny
    y = me % ny
    z = me // ny
    piece, cols = w_ref.shape
    A = pl.ds(0, ca)
    B = pl.ds(ca, cols - ca)
    hy, hz = ny // 2, nz // 2
    hb = (cols - ca) // 2
    B1 = pl.ds(ca, hb)
    B2 = pl.ds(ca + hb, cols - ca - hb)

    def zz(k):
        return (z + nz + k) % nz

    def yy(k):
        return (y + ny + k) % ny

    def dev(zi, yi):
        return (zi * ny + yi, head)

    rounds = count.bit_length() - 1
    partners = []
    for k in range(rounds):
        step = 1 << k
        bit = (me // step) % 2
        partners.append((me + step - 2 * step * bit, bit))
    ring = [dev(z, yy(1)), dev(z, yy(-1)), dev(zz(1), y), dev(zz(-1), y)]
    barrier = pltpu.get_barrier_semaphore()
    for target in ring:
        pl.semaphore_signal(barrier, inc=1, device_id=target, device_id_type=MESH)
    for partner, _ in partners:
        pl.semaphore_signal(barrier, inc=1, device_id=(partner, head), device_id_type=MESH)
    pl.semaphore_wait(barrier, len(ring) + rounds)

    local = pltpu.make_async_copy(w_ref, rows_ref.at[z, y], local_sem)
    local.start()
    R = rows_ref
    yr, yl, zr, zl = dev(z, yy(1)), dev(z, yy(-1)), dev(zz(1), y), dev(zz(-1), y)
    ticks = [
        [(w_ref.at[:, A], R.at[z, y, :, A], yr), (w_ref.at[:, A], R.at[z, y, :, A], yl),
         (w_ref.at[:, B], R.at[z, y, :, B], zr), (w_ref.at[:, B], R.at[z, y, :, B], zl)],
        [(R.at[z, yy(-1), :, A], R.at[z, yy(-1), :, A], yr),
         (R.at[zz(-1), y, :, B], R.at[zz(-1), y, :, B], zr), (R.at[zz(1), y, :, B], R.at[zz(1), y, :, B], zl)],
        [(R.at[z, :, :, A], R.at[z, :, :, A], zr), (R.at[z, :, :, A], R.at[z, :, :, A], zl),
         (R.at[zz(-2), y, :, B], R.at[zz(-2), y, :, B], zr), (R.at[zz(2), y, :, B], R.at[zz(2), y, :, B], zl)],
        [(R.at[zz(-1), :, :, A], R.at[zz(-1), :, :, A], zr), (R.at[zz(1), :, :, A], R.at[zz(1), :, :, A], zl),
         (R.at[zz(-3), y, :, B1], R.at[zz(-3), y, :, B1], zr),
         (R.at[zz(3), y, :, B2], R.at[zz(3), y, :, B2], zl)],
        [(R.at[zz(-2), :, :, A], R.at[zz(-2), :, :, A], zr), (R.at[zz(2), :, :, A], R.at[zz(2), :, :, A], zl),
         (R.at[:, y, :, B], R.at[:, y, :, B], yr), (R.at[:, y, :, B], R.at[:, y, :, B], yl)],
        [(R.at[zz(-3), pl.ds(0, hy), :, A], R.at[zz(-3), pl.ds(0, hy), :, A], zr),
         (R.at[zz(3), pl.ds(hy, ny - hy), :, A], R.at[zz(3), pl.ds(hy, ny - hy), :, A], zl),
         (R.at[pl.ds(0, hz), yy(-1), :, B], R.at[pl.ds(0, hz), yy(-1), :, B], yr),
         (R.at[pl.ds(hz, nz - hz), yy(1), :, B], R.at[pl.ds(hz, nz - hz), yy(1), :, B], yl)],
    ]
    for load in loads:
        load.wait()
    heads, dim = partial_ref.shape[0], partial_ref.shape[2]
    tn = (((0,), (0,)), ((), ()))
    total = jnp.stack([
        lax.dot_general(k_ref[:, pl.ds(h * dim, dim)], v_ref[:, pl.ds(h * dim, dim)], tn,
                        preferred_element_type=jnp.float32)
        for h in range(heads)
    ])
    partial = jnp.zeros_like(total)
    n = 0
    for t, moves in enumerate(ticks):
        if t == 2:
            local.wait()
        started = []
        for src, dst, target in moves:
            copy = pltpu.make_async_remote_copy(
                src_ref=src, dst_ref=dst, send_sem=send_sem.at[n], recv_sem=recv_sem.at[n],
                device_id=target, device_id_type=MESH,
            )
            copy.start()
            started.append(copy)
            n += 1
        scan = None
        if t < rounds:
            partner, bit = partners[t]
            sent = total.astype(jnp.bfloat16)
            sendbuf[t] = sent
            scan = pltpu.make_async_remote_copy(
                src_ref=sendbuf.at[t], dst_ref=recvbuf.at[t], send_sem=bf_send.at[t],
                recv_sem=bf_recv.at[t], device_id=(partner, head), device_id_type=MESH,
            )
            scan.start()
        for copy in started:
            copy.wait()
        if scan is not None:
            scan.wait()
            other = recvbuf[t].astype(jnp.float32)
            partial = jnp.where(bit == 1, partial + other, partial)
            total = sent.astype(jnp.float32) + other
    partial_ref[...] = partial


def gather_and_scan(key, val, heads, dim, weight):
    count = lax.axis_size("seq")
    ny = 4
    piece, cols = weight.shape
    rounds = count.bit_length() - 1
    ca = (cols * 2 // 3) // 128 * 128
    n_copies = 23
    return pl.pallas_call(
        functools.partial(gather_kernel, ny, ca),
        out_shape=(
            jax.ShapeDtypeStruct((count // ny, ny, piece, cols), weight.dtype),
            jax.ShapeDtypeStruct((heads, dim, dim), jnp.float32),
        ),
        in_specs=[pl.BlockSpec(memory_space=pl.ANY)] * 3,
        out_specs=(pl.BlockSpec(memory_space=pl.ANY), pl.BlockSpec(memory_space=pltpu.VMEM)),
        scratch_shapes=[
            pltpu.VMEM((rounds, heads, dim, dim), jnp.bfloat16),
            pltpu.VMEM((rounds, heads, dim, dim), jnp.bfloat16),
            pltpu.SemaphoreType.DMA((n_copies,)),
            pltpu.SemaphoreType.DMA((n_copies,)),
            pltpu.SemaphoreType.DMA((rounds,)),
            pltpu.SemaphoreType.DMA((rounds,)),
            pltpu.SemaphoreType.DMA(()),
            pltpu.VMEM(key.shape, key.dtype),
            pltpu.VMEM(val.shape, val.dtype),
            pltpu.SemaphoreType.DMA((2,)),
        ],
        compiler_params=pltpu.CompilerParams(collective_id=2, has_side_effects=True),
    )(key, val, weight)


def normalize(attended):
    return attended * lax.rsqrt(jnp.mean(attended * attended, axis=-1, keepdims=True) + EPS)


def shards(query, key, value, init_state, out_weight, out_grad):
    tok_rows = query.shape[0]
    width = query.shape[1]
    heads_here = init_state.shape[0]
    head_dim = init_state.shape[2]
    queries = query.reshape(tok_rows, heads_here, head_dim)
    key_rows = key.reshape(tok_rows, heads_here, head_dim)
    val_rows = value.reshape(tok_rows, heads_here, head_dim)
    half = out_weight.shape[1] // 2
    gathered, earlier = gather_and_scan(key, value, heads_here, head_dim, out_weight[:, :half])
    other_half = lax.all_gather(out_weight[:, half:], "seq", axis=0, tiled=True)
    state_half = (init_state + earlier).astype(jnp.bfloat16)
    row_index = lax.broadcasted_iota(jnp.int32, (tok_rows, tok_rows), 0)
    col_index = lax.broadcasted_iota(jnp.int32, (tok_rows, tok_rows), 1)
    causal = col_index <= row_index
    scores = jnp.einsum("thi,shi->hts", queries, key_rows, preferred_element_type=jnp.float32)
    attn_weights = jnp.where(causal, scores, 0.0).astype(jnp.bfloat16)
    attended = jnp.einsum(
        "hts,shj->thj", attn_weights, val_rows, preferred_element_type=jnp.float32
    )
    attended = attended + jnp.einsum(
        "thi,hij->thj", queries, state_half, preferred_element_type=jnp.float32
    )
    normed = normalize(attended).astype(jnp.bfloat16).reshape(tok_rows, width)
    first_rows = gathered.reshape(-1, half)
    weight_rows = jnp.concatenate([first_rows, other_half], axis=1)
    projected = jnp.dot(normed, weight_rows, preferred_element_type=jnp.float32).astype(jnp.bfloat16)
    projected, first_rows, other_half = lax.optimization_barrier((projected, first_rows, other_half))
    contract = (((1,), (1,)), ((), ()))
    grad_normed = lax.dot_general(
        out_grad[:, :half], first_rows, contract, preferred_element_type=jnp.float32
    ) + lax.dot_general(out_grad[:, half:], other_half, contract, preferred_element_type=jnp.float32)
    mixed = lax.psum_scatter(
        projected, "head", scatter_dimension=1, tiled=True
    )
    _, norm_back = jax.vjp(normalize, attended)
    grad_att = norm_back(grad_normed.reshape(tok_rows, heads_here, head_dim))[0].astype(
        jnp.bfloat16
    )
    own_adjoint = jnp.einsum("thi,thj->hij", queries, grad_att, preferred_element_type=jnp.float32)
    grad_query, grad_key, grad_value, init_grad = backward_pass(
        own_adjoint, query, key, value, grad_att.reshape(tok_rows, width), state_half
    )
    return (mixed, grad_query, grad_key, grad_value, init_grad)


def solution(mesh):
    return jax.shard_map(
        shards,
        mesh=mesh,
        in_specs=(
            P("seq", "head"),
            P("seq", "head"),
            P("seq", "head"),
            P("head", None, None),
            P(("head", "seq"), None),
            P("seq", None),
        ),
        out_specs=(
            P("seq", "head"),
            P("seq", "head"),
            P("seq", "head"),
            P("seq", "head"),
            P("head", None, None),
        ),
        check_vma=False,
    )
```

```python
import functools

import jax
import jax.numpy as jnp
from jax import lax
from jax.experimental import pallas as pl
from jax.experimental.pallas import tpu as pltpu
from jax.sharding import PartitionSpec as P

EPS = 1e-06


MESH = pl.DeviceIdType.MESH


def butterfly_kernel(count, backward, value_ref, partial_ref, total_ref, sendbuf, recvbuf, send_sem, recv_sem):
    me = lax.axis_index("seq")
    head = lax.axis_index("head")
    rounds = count.bit_length() - 1
    partners = []
    for k in range(rounds):
        step = 1 << k
        bit = (me // step) % 2
        partners.append((me + step - 2 * step * bit, bit))
    barrier = pltpu.get_barrier_semaphore()
    for partner, _ in partners:
        pl.semaphore_signal(barrier, inc=1, device_id=(partner, head), device_id_type=MESH)
    pl.semaphore_wait(barrier, rounds)
    total = value_ref[...]
    partial = jnp.zeros_like(total)
    for k, (partner, bit) in enumerate(partners):
        sent = total.astype(jnp.bfloat16)
        sendbuf[k] = sent
        copy = pltpu.make_async_remote_copy(
            src_ref=sendbuf.at[k],
            dst_ref=recvbuf.at[k],
            send_sem=send_sem.at[k],
            recv_sem=recv_sem.at[k],
            device_id=(partner, head),
            device_id_type=MESH,
        )
        copy.start()
        copy.wait()
        other = recvbuf[k].astype(jnp.float32)
        take = (bit == 0) if backward else (bit == 1)
        partial = jnp.where(take, partial + other, partial)
        total = sent.astype(jnp.float32) + other
    partial_ref[...] = partial
    total_ref[...] = total


def butterfly(value, axis, backward):
    count = lax.axis_size(axis)
    rounds = count.bit_length() - 1
    shape = jax.ShapeDtypeStruct(value.shape, jnp.float32)
    return pl.pallas_call(
        functools.partial(butterfly_kernel, count, backward),
        out_shape=(shape, shape),
        in_specs=[pl.BlockSpec(memory_space=pltpu.VMEM)],
        out_specs=(pl.BlockSpec(memory_space=pltpu.VMEM), pl.BlockSpec(memory_space=pltpu.VMEM)),
        scratch_shapes=[
            pltpu.VMEM((rounds,) + value.shape, jnp.bfloat16),
            pltpu.VMEM((rounds,) + value.shape, jnp.bfloat16),
            pltpu.SemaphoreType.DMA((rounds,)),
            pltpu.SemaphoreType.DMA((rounds,)),
        ],
        compiler_params=pltpu.CompilerParams(
            collective_id=1 if backward else 0, has_side_effects=True
        ),
    )(value.astype(jnp.float32))


def backward_kernel(adj_ref, q_hbm, k_hbm, v_hbm, ga_hbm, sh_ref, gq_hbm, gk_hbm, gv_hbm, later_ref, total_ref,
                    sendbuf, recvbuf, send_sem, recv_sem, q_ref, k_ref, v_ref, ga_ref, load_sem,
                    gq_ref, gk_acc, gv_acc, store_sem):
    loads = [pltpu.make_async_copy(src, dst, load_sem.at[i])
             for i, (src, dst) in enumerate([(q_hbm, q_ref), (k_hbm, k_ref), (v_hbm, v_ref), (ga_hbm, ga_ref)])]
    for load in loads:
        load.start()
    me = lax.axis_index("seq")
    head = lax.axis_index("head")
    count = lax.axis_size("seq")
    rounds = count.bit_length() - 1
    heads = sh_ref.shape[0]
    dim = sh_ref.shape[2]
    rows = q_ref.shape[0]
    partners = []
    for k in range(rounds):
        step = 1 << k
        bit = (me // step) % 2
        partners.append((me + step - 2 * step * bit, bit))
    barrier = pltpu.get_barrier_semaphore()
    for partner, _ in partners:
        pl.semaphore_signal(barrier, inc=1, device_id=(partner, head), device_id_type=MESH)
    pl.semaphore_wait(barrier, rounds)
    causal = lax.broadcasted_iota(jnp.int32, (rows, rows), 1) <= lax.broadcasted_iota(jnp.int32, (rows, rows), 0)
    nt = (((1,), (1,)), ((), ()))
    tn = (((0,), (0,)), ((), ()))

    def head_work(h):
        cols = pl.ds(h * dim, dim)
        qh, kh, vh, gah = q_ref[:, cols], k_ref[:, cols], v_ref[:, cols], ga_ref[:, cols]
        gs = lax.dot_general(gah, vh, nt, preferred_element_type=jnp.float32)
        gs = jnp.where(causal, gs, 0.0).astype(jnp.bfloat16)
        aw = lax.dot_general(qh, kh, nt, preferred_element_type=jnp.float32)
        aw = jnp.where(causal, aw, 0.0).astype(jnp.bfloat16)
        gq = jnp.dot(gs, kh, preferred_element_type=jnp.float32)
        gq = gq + lax.dot_general(gah, sh_ref[h], nt, preferred_element_type=jnp.float32)
        gq_ref[:, cols] = gq.astype(gq_ref.dtype)
        gk_acc[:, cols] = lax.dot_general(gs, qh, tn, preferred_element_type=jnp.float32).astype(gk_acc.dtype)
        gv_acc[:, cols] = lax.dot_general(aw, gah, tn, preferred_element_type=jnp.float32).astype(gv_acc.dtype)

    order = [[] for _ in range(rounds)]
    for h in range(heads):
        order[min(h, rounds - 1)].append(h)
    total = adj_ref[...]
    partial = jnp.zeros_like(total)
    for t, (partner, bit) in enumerate(partners):
        sent = total.astype(jnp.bfloat16)
        sendbuf[t] = sent
        copy = pltpu.make_async_remote_copy(
            src_ref=sendbuf.at[t], dst_ref=recvbuf.at[t], send_sem=send_sem.at[t],
            recv_sem=recv_sem.at[t], device_id=(partner, head), device_id_type=MESH,
        )
        copy.start()
        if t == 0:
            for load in loads:
                load.wait()
        for h in order[t]:
            head_work(h)
        if t == rounds - 1:
            stores = [pltpu.make_async_copy(src, dst, store_sem.at[i])
                      for i, (src, dst) in enumerate([(gq_ref, gq_hbm), (gk_acc, gk_hbm), (gv_acc, gv_hbm)])]
            for store in stores:
                store.start()
        copy.wait()
        other = recvbuf[t].astype(jnp.float32)
        partial = jnp.where(bit == 0, partial + other, partial)
        total = sent.astype(jnp.float32) + other
    total_ref[...] = total
    later_ref[...] = partial.astype(later_ref.dtype)
    for store in stores:
        store.wait()


def finish_kernel(gq_in, gk_acc, gv_acc, v_ref, k_ref, later_ref, gq_ref, gk_ref, gv_ref):
    heads, dim = later_ref.shape[0], later_ref.shape[2]
    nt = (((1,), (1,)), ((), ()))
    gq_ref[...] = gq_in[...]
    for h in range(heads):
        cols = pl.ds(h * dim, dim)
        later = later_ref[h]
        gk = gk_acc[:, cols].astype(jnp.float32) + lax.dot_general(v_ref[:, cols], later, nt, preferred_element_type=jnp.float32)
        gk_ref[:, cols] = gk.astype(gk_ref.dtype)
        gv = gv_acc[:, cols].astype(jnp.float32) + jnp.dot(k_ref[:, cols], later, preferred_element_type=jnp.float32)
        gv_ref[:, cols] = gv.astype(gv_ref.dtype)


def backward_pass(own_adjoint, query, key, value, grad_att, state_half):
    count = lax.axis_size("seq")
    rounds = count.bit_length() - 1
    tokens = jax.ShapeDtypeStruct(query.shape, jnp.bfloat16)
    vmem = pl.BlockSpec(memory_space=pltpu.VMEM)
    accs = jax.ShapeDtypeStruct(query.shape, jnp.bfloat16)
    gq, gk_acc, gv_acc, later, total = pl.pallas_call(
        backward_kernel,
        out_shape=(tokens, accs, accs, jax.ShapeDtypeStruct(own_adjoint.shape, jnp.bfloat16),
                   jax.ShapeDtypeStruct(own_adjoint.shape, jnp.float32)),
        in_specs=[vmem] + [pl.BlockSpec(memory_space=pl.ANY)] * 4 + [vmem],
        out_specs=(pl.BlockSpec(memory_space=pl.ANY),) * 3 + (vmem, vmem),
        scratch_shapes=[
            pltpu.VMEM((rounds,) + own_adjoint.shape, jnp.bfloat16),
            pltpu.VMEM((rounds,) + own_adjoint.shape, jnp.bfloat16),
            pltpu.SemaphoreType.DMA((rounds,)),
            pltpu.SemaphoreType.DMA((rounds,)),
        ] + [pltpu.VMEM(query.shape, jnp.bfloat16)] * 4 + [pltpu.SemaphoreType.DMA((4,))]
        + [pltpu.VMEM(query.shape, jnp.bfloat16), pltpu.VMEM(query.shape, jnp.bfloat16),
           pltpu.VMEM(query.shape, jnp.bfloat16), pltpu.SemaphoreType.DMA((3,))],
        compiler_params=pltpu.CompilerParams(collective_id=1, has_side_effects=True),
    )(own_adjoint, query, key, value, grad_att, state_half)
    gq, gk, gv = pl.pallas_call(
        finish_kernel,
        out_shape=(tokens, tokens, tokens),
        in_specs=[vmem] * 6,
        out_specs=(vmem,) * 3,
    )(gq, gk_acc, gv_acc, value, key, later)
    return gq, gk, gv, total


def gather_kernel(ny, ca, value_ref, w_ref, rows_ref, partial_ref, sendbuf, recvbuf, send_sem, recv_sem, bf_send, bf_recv, local_sem):
    me = lax.axis_index("seq")
    head = lax.axis_index("head")
    count = lax.axis_size("seq")
    nz = count // ny
    y = me % ny
    z = me // ny
    piece, cols = w_ref.shape
    A = pl.ds(0, ca)
    B = pl.ds(ca, cols - ca)
    hy, hz = ny // 2, nz // 2
    hb = (cols - ca) // 2
    B1 = pl.ds(ca, hb)
    B2 = pl.ds(ca + hb, cols - ca - hb)

    def zz(k):
        return (z + nz + k) % nz

    def yy(k):
        return (y + ny + k) % ny

    def dev(zi, yi):
        return (zi * ny + yi, head)

    rounds = count.bit_length() - 1
    partners = []
    for k in range(rounds):
        step = 1 << k
        bit = (me // step) % 2
        partners.append((me + step - 2 * step * bit, bit))
    ring = [dev(z, yy(1)), dev(z, yy(-1)), dev(zz(1), y), dev(zz(-1), y)]
    barrier = pltpu.get_barrier_semaphore()
    for target in ring:
        pl.semaphore_signal(barrier, inc=1, device_id=target, device_id_type=MESH)
    for partner, _ in partners:
        pl.semaphore_signal(barrier, inc=1, device_id=(partner, head), device_id_type=MESH)
    pl.semaphore_wait(barrier, len(ring) + rounds)

    local = pltpu.make_async_copy(w_ref, rows_ref.at[z, y], local_sem)
    local.start()
    R = rows_ref
    yr, yl, zr, zl = dev(z, yy(1)), dev(z, yy(-1)), dev(zz(1), y), dev(zz(-1), y)
    ticks = [
        [(w_ref.at[:, A], R.at[z, y, :, A], yr), (w_ref.at[:, A], R.at[z, y, :, A], yl),
         (w_ref.at[:, B], R.at[z, y, :, B], zr), (w_ref.at[:, B], R.at[z, y, :, B], zl)],
        [(R.at[z, yy(-1), :, A], R.at[z, yy(-1), :, A], yr),
         (R.at[zz(-1), y, :, B], R.at[zz(-1), y, :, B], zr), (R.at[zz(1), y, :, B], R.at[zz(1), y, :, B], zl)],
        [(R.at[z, :, :, A], R.at[z, :, :, A], zr), (R.at[z, :, :, A], R.at[z, :, :, A], zl),
         (R.at[zz(-2), y, :, B], R.at[zz(-2), y, :, B], zr), (R.at[zz(2), y, :, B], R.at[zz(2), y, :, B], zl)],
        [(R.at[zz(-1), :, :, A], R.at[zz(-1), :, :, A], zr), (R.at[zz(1), :, :, A], R.at[zz(1), :, :, A], zl),
         (R.at[zz(-3), y, :, B1], R.at[zz(-3), y, :, B1], zr),
         (R.at[zz(3), y, :, B2], R.at[zz(3), y, :, B2], zl)],
        [(R.at[zz(-2), :, :, A], R.at[zz(-2), :, :, A], zr), (R.at[zz(2), :, :, A], R.at[zz(2), :, :, A], zl),
         (R.at[:, y, :, B], R.at[:, y, :, B], yr), (R.at[:, y, :, B], R.at[:, y, :, B], yl)],
        [(R.at[zz(-3), pl.ds(0, hy), :, A], R.at[zz(-3), pl.ds(0, hy), :, A], zr),
         (R.at[zz(3), pl.ds(hy, ny - hy), :, A], R.at[zz(3), pl.ds(hy, ny - hy), :, A], zl),
         (R.at[pl.ds(0, hz), yy(-1), :, B], R.at[pl.ds(0, hz), yy(-1), :, B], yr),
         (R.at[pl.ds(hz, nz - hz), yy(1), :, B], R.at[pl.ds(hz, nz - hz), yy(1), :, B], yl)],
    ]
    total = value_ref[...]
    partial = jnp.zeros_like(total)
    n = 0
    for t, moves in enumerate(ticks):
        if t == 2:
            local.wait()
        started = []
        for src, dst, target in moves:
            copy = pltpu.make_async_remote_copy(
                src_ref=src, dst_ref=dst, send_sem=send_sem.at[n], recv_sem=recv_sem.at[n],
                device_id=target, device_id_type=MESH,
            )
            copy.start()
            started.append(copy)
            n += 1
        scan = None
        if t < rounds:
            partner, bit = partners[t]
            sent = total.astype(jnp.bfloat16)
            sendbuf[t] = sent
            scan = pltpu.make_async_remote_copy(
                src_ref=sendbuf.at[t], dst_ref=recvbuf.at[t], send_sem=bf_send.at[t],
                recv_sem=bf_recv.at[t], device_id=(partner, head), device_id_type=MESH,
            )
            scan.start()
        for copy in started:
            copy.wait()
        if scan is not None:
            scan.wait()
            other = recvbuf[t].astype(jnp.float32)
            partial = jnp.where(bit == 1, partial + other, partial)
            total = sent.astype(jnp.float32) + other
    partial_ref[...] = partial


def gather_and_scan(value, weight):
    count = lax.axis_size("seq")
    ny = 4
    piece, cols = weight.shape
    rounds = count.bit_length() - 1
    ca = (cols * 2 // 3) // 128 * 128
    n_copies = 23
    return pl.pallas_call(
        functools.partial(gather_kernel, ny, ca),
        out_shape=(
            jax.ShapeDtypeStruct((count // ny, ny, piece, cols), weight.dtype),
            jax.ShapeDtypeStruct(value.shape, jnp.float32),
        ),
        in_specs=[pl.BlockSpec(memory_space=pltpu.VMEM), pl.BlockSpec(memory_space=pl.ANY)],
        out_specs=(pl.BlockSpec(memory_space=pl.ANY), pl.BlockSpec(memory_space=pltpu.VMEM)),
        scratch_shapes=[
            pltpu.VMEM((rounds,) + value.shape, jnp.bfloat16),
            pltpu.VMEM((rounds,) + value.shape, jnp.bfloat16),
            pltpu.SemaphoreType.DMA((n_copies,)),
            pltpu.SemaphoreType.DMA((n_copies,)),
            pltpu.SemaphoreType.DMA((rounds,)),
            pltpu.SemaphoreType.DMA((rounds,)),
            pltpu.SemaphoreType.DMA(()),
        ],
        compiler_params=pltpu.CompilerParams(collective_id=2, has_side_effects=True),
    )(value.astype(jnp.float32), weight)


def normalize(attended):
    return attended * lax.rsqrt(jnp.mean(attended * attended, axis=-1, keepdims=True) + EPS)


def shards(query, key, value, init_state, out_weight, out_grad):
    tok_rows = query.shape[0]
    width = query.shape[1]
    heads_here = init_state.shape[0]
    head_dim = init_state.shape[2]
    queries = query.reshape(tok_rows, heads_here, head_dim)
    key_rows = key.reshape(tok_rows, heads_here, head_dim)
    val_rows = value.reshape(tok_rows, heads_here, head_dim)
    local_state = jnp.einsum("thi,thj->hij", key_rows, val_rows, preferred_element_type=jnp.float32)
    half = out_weight.shape[1] // 2
    gathered, earlier = gather_and_scan(local_state, out_weight[:, :half])
    other_half = lax.all_gather(out_weight[:, half:], "seq", axis=0, tiled=True)
    state_half = (init_state + earlier).astype(jnp.bfloat16)
    row_index = lax.broadcasted_iota(jnp.int32, (tok_rows, tok_rows), 0)
    col_index = lax.broadcasted_iota(jnp.int32, (tok_rows, tok_rows), 1)
    causal = col_index <= row_index
    scores = jnp.einsum("thi,shi->hts", queries, key_rows, preferred_element_type=jnp.float32)
    attn_weights = jnp.where(causal, scores, 0.0).astype(jnp.bfloat16)
    attended = jnp.einsum(
        "hts,shj->thj", attn_weights, val_rows, preferred_element_type=jnp.float32
    )
    attended = attended + jnp.einsum(
        "thi,hij->thj", queries, state_half, preferred_element_type=jnp.float32
    )
    normed = normalize(attended).astype(jnp.bfloat16).reshape(tok_rows, width)
    first_rows = gathered.reshape(-1, half)
    weight_rows = jnp.concatenate([first_rows, other_half], axis=1)
    projected = jnp.dot(normed, weight_rows, preferred_element_type=jnp.float32).astype(jnp.bfloat16)
    projected, first_rows, other_half = lax.optimization_barrier((projected, first_rows, other_half))
    contract = (((1,), (1,)), ((), ()))
    grad_normed = lax.dot_general(
        out_grad[:, :half], first_rows, contract, preferred_element_type=jnp.float32
    ) + lax.dot_general(out_grad[:, half:], other_half, contract, preferred_element_type=jnp.float32)
    mixed = lax.psum_scatter(
        projected, "head", scatter_dimension=1, tiled=True
    )
    _, norm_back = jax.vjp(normalize, attended)
    grad_att = norm_back(grad_normed.reshape(tok_rows, heads_here, head_dim))[0].astype(
        jnp.bfloat16
    )
    own_adjoint = jnp.einsum("thi,thj->hij", queries, grad_att, preferred_element_type=jnp.float32)
    grad_query, grad_key, grad_value, init_grad = backward_pass(
        own_adjoint, query, key, value, grad_att.reshape(tok_rows, width), state_half
    )
    return (mixed, grad_query, grad_key, grad_value, init_grad)


def solution(mesh):
    return jax.shard_map(
        shards,
        mesh=mesh,
        in_specs=(
            P("seq", "head"),
            P("seq", "head"),
            P("seq", "head"),
            P("head", None, None),
            P(("head", "seq"), None),
            P("seq", None),
        ),
        out_specs=(
            P("seq", "head"),
            P("seq", "head"),
            P("seq", "head"),
            P("seq", "head"),
            P("head", None, None),
        ),
        check_vma=False,
    )
```

```python
import functools

import jax
import jax.numpy as jnp
from jax import lax
from jax.experimental import pallas as pl
from jax.experimental.pallas import tpu as pltpu
from jax.sharding import PartitionSpec as P

EPS = 1e-06


MESH = pl.DeviceIdType.MESH


def butterfly_kernel(count, backward, value_ref, partial_ref, total_ref, sendbuf, recvbuf, send_sem, recv_sem):
    me = lax.axis_index("seq")
    head = lax.axis_index("head")
    rounds = count.bit_length() - 1
    partners = []
    for k in range(rounds):
        step = 1 << k
        bit = (me // step) % 2
        partners.append((me + step - 2 * step * bit, bit))
    barrier = pltpu.get_barrier_semaphore()
    for partner, _ in partners:
        pl.semaphore_signal(barrier, inc=1, device_id=(partner, head), device_id_type=MESH)
    pl.semaphore_wait(barrier, rounds)
    total = value_ref[...]
    partial = jnp.zeros_like(total)
    for k, (partner, bit) in enumerate(partners):
        sent = total.astype(jnp.bfloat16)
        sendbuf[k] = sent
        copy = pltpu.make_async_remote_copy(
            src_ref=sendbuf.at[k],
            dst_ref=recvbuf.at[k],
            send_sem=send_sem.at[k],
            recv_sem=recv_sem.at[k],
            device_id=(partner, head),
            device_id_type=MESH,
        )
        copy.start()
        copy.wait()
        other = recvbuf[k].astype(jnp.float32)
        take = (bit == 0) if backward else (bit == 1)
        partial = jnp.where(take, partial + other, partial)
        total = sent.astype(jnp.float32) + other
    partial_ref[...] = partial
    total_ref[...] = total


def butterfly(value, axis, backward):
    count = lax.axis_size(axis)
    rounds = count.bit_length() - 1
    shape = jax.ShapeDtypeStruct(value.shape, jnp.float32)
    return pl.pallas_call(
        functools.partial(butterfly_kernel, count, backward),
        out_shape=(shape, shape),
        in_specs=[pl.BlockSpec(memory_space=pltpu.VMEM)],
        out_specs=(pl.BlockSpec(memory_space=pltpu.VMEM), pl.BlockSpec(memory_space=pltpu.VMEM)),
        scratch_shapes=[
            pltpu.VMEM((rounds,) + value.shape, jnp.bfloat16),
            pltpu.VMEM((rounds,) + value.shape, jnp.bfloat16),
            pltpu.SemaphoreType.DMA((rounds,)),
            pltpu.SemaphoreType.DMA((rounds,)),
        ],
        compiler_params=pltpu.CompilerParams(
            collective_id=1 if backward else 0, has_side_effects=True
        ),
    )(value.astype(jnp.float32))


def backward_kernel(q_hbm, k_hbm, v_hbm, ga_hbm, sh_ref, gq_hbm, gk_hbm, gv_hbm, later_ref, total_ref,
                    sendbuf, recvbuf, send_sem, recv_sem, q_ref, k_ref, v_ref, ga_ref, load_sem,
                    gq_ref, gk_acc, gv_acc, store_sem):
    loads = [pltpu.make_async_copy(src, dst, load_sem.at[i])
             for i, (src, dst) in enumerate([(q_hbm, q_ref), (k_hbm, k_ref), (v_hbm, v_ref), (ga_hbm, ga_ref)])]
    for load in loads:
        load.start()
    me = lax.axis_index("seq")
    head = lax.axis_index("head")
    count = lax.axis_size("seq")
    rounds = count.bit_length() - 1
    heads = sh_ref.shape[0]
    dim = sh_ref.shape[2]
    rows = q_ref.shape[0]
    partners = []
    for k in range(rounds):
        step = 1 << k
        bit = (me // step) % 2
        partners.append((me + step - 2 * step * bit, bit))
    barrier = pltpu.get_barrier_semaphore()
    for partner, _ in partners:
        pl.semaphore_signal(barrier, inc=1, device_id=(partner, head), device_id_type=MESH)
    pl.semaphore_wait(barrier, rounds)
    causal = lax.broadcasted_iota(jnp.int32, (rows, rows), 1) <= lax.broadcasted_iota(jnp.int32, (rows, rows), 0)
    nt = (((1,), (1,)), ((), ()))
    tn = (((0,), (0,)), ((), ()))

    def head_work(h):
        cols = pl.ds(h * dim, dim)
        qh, kh, vh, gah = q_ref[:, cols], k_ref[:, cols], v_ref[:, cols], ga_ref[:, cols]
        gs = lax.dot_general(gah, vh, nt, preferred_element_type=jnp.float32)
        gs = jnp.where(causal, gs, 0.0).astype(jnp.bfloat16)
        aw = lax.dot_general(qh, kh, nt, preferred_element_type=jnp.float32)
        aw = jnp.where(causal, aw, 0.0).astype(jnp.bfloat16)
        gq = jnp.dot(gs, kh, preferred_element_type=jnp.float32)
        gq = gq + lax.dot_general(gah, sh_ref[h], nt, preferred_element_type=jnp.float32)
        gq_ref[:, cols] = gq.astype(gq_ref.dtype)
        gk_acc[:, cols] = lax.dot_general(gs, qh, tn, preferred_element_type=jnp.float32).astype(gk_acc.dtype)
        gv_acc[:, cols] = lax.dot_general(aw, gah, tn, preferred_element_type=jnp.float32).astype(gv_acc.dtype)

    order = [[] for _ in range(rounds)]
    for h in range(heads):
        order[min(h, rounds - 1)].append(h)
    for load in loads:
        load.wait()
    total = jnp.stack([
        lax.dot_general(q_ref[:, pl.ds(h * dim, dim)], ga_ref[:, pl.ds(h * dim, dim)], tn,
                        preferred_element_type=jnp.float32)
        for h in range(heads)
    ])
    partial = jnp.zeros_like(total)
    for t, (partner, bit) in enumerate(partners):
        sent = total.astype(jnp.bfloat16)
        sendbuf[t] = sent
        copy = pltpu.make_async_remote_copy(
            src_ref=sendbuf.at[t], dst_ref=recvbuf.at[t], send_sem=send_sem.at[t],
            recv_sem=recv_sem.at[t], device_id=(partner, head), device_id_type=MESH,
        )
        copy.start()
        for h in order[t]:
            head_work(h)
        if t == rounds - 1:
            stores = [pltpu.make_async_copy(src, dst, store_sem.at[i])
                      for i, (src, dst) in enumerate([(gq_ref, gq_hbm), (gk_acc, gk_hbm), (gv_acc, gv_hbm)])]
            for store in stores:
                store.start()
        copy.wait()
        other = recvbuf[t].astype(jnp.float32)
        partial = jnp.where(bit == 0, partial + other, partial)
        total = sent.astype(jnp.float32) + other
    total_ref[...] = total
    later_ref[...] = partial.astype(later_ref.dtype)
    for store in stores:
        store.wait()


def finish_kernel(gq_in, gk_acc, gv_acc, v_ref, k_ref, later_ref, gq_ref, gk_ref, gv_ref):
    heads, dim = later_ref.shape[0], later_ref.shape[2]
    nt = (((1,), (1,)), ((), ()))
    gq_ref[...] = gq_in[...]
    for h in range(heads):
        cols = pl.ds(h * dim, dim)
        later = later_ref[h]
        gk = gk_acc[:, cols].astype(jnp.float32) + lax.dot_general(v_ref[:, cols], later, nt, preferred_element_type=jnp.float32)
        gk_ref[:, cols] = gk.astype(gk_ref.dtype)
        gv = gv_acc[:, cols].astype(jnp.float32) + jnp.dot(k_ref[:, cols], later, preferred_element_type=jnp.float32)
        gv_ref[:, cols] = gv.astype(gv_ref.dtype)


def backward_pass(query, key, value, grad_att, state_half):
    own_adjoint = jax.ShapeDtypeStruct(state_half.shape, jnp.float32)
    count = lax.axis_size("seq")
    rounds = count.bit_length() - 1
    tokens = jax.ShapeDtypeStruct(query.shape, jnp.bfloat16)
    vmem = pl.BlockSpec(memory_space=pltpu.VMEM)
    accs = jax.ShapeDtypeStruct(query.shape, jnp.bfloat16)
    gq, gk_acc, gv_acc, later, total = pl.pallas_call(
        backward_kernel,
        out_shape=(tokens, accs, accs, jax.ShapeDtypeStruct(own_adjoint.shape, jnp.bfloat16),
                   jax.ShapeDtypeStruct(own_adjoint.shape, jnp.float32)),
        in_specs=[pl.BlockSpec(memory_space=pl.ANY)] * 4 + [vmem],
        out_specs=(pl.BlockSpec(memory_space=pl.ANY),) * 3 + (vmem, vmem),
        scratch_shapes=[
            pltpu.VMEM((rounds,) + own_adjoint.shape, jnp.bfloat16),
            pltpu.VMEM((rounds,) + own_adjoint.shape, jnp.bfloat16),
            pltpu.SemaphoreType.DMA((rounds,)),
            pltpu.SemaphoreType.DMA((rounds,)),
        ] + [pltpu.VMEM(query.shape, jnp.bfloat16)] * 4 + [pltpu.SemaphoreType.DMA((4,))]
        + [pltpu.VMEM(query.shape, jnp.bfloat16), pltpu.VMEM(query.shape, jnp.bfloat16),
           pltpu.VMEM(query.shape, jnp.bfloat16), pltpu.SemaphoreType.DMA((3,))],
        compiler_params=pltpu.CompilerParams(collective_id=1, has_side_effects=True),
    )(query, key, value, grad_att, state_half)
    gq, gk, gv = pl.pallas_call(
        finish_kernel,
        out_shape=(tokens, tokens, tokens),
        in_specs=[vmem] * 6,
        out_specs=(vmem,) * 3,
    )(gq, gk_acc, gv_acc, value, key, later)
    return gq, gk, gv, total


def gather_kernel(ny, ca, value_ref, w_ref, rows_ref, partial_ref, sendbuf, recvbuf, send_sem, recv_sem, bf_send, bf_recv, local_sem):
    me = lax.axis_index("seq")
    head = lax.axis_index("head")
    count = lax.axis_size("seq")
    nz = count // ny
    y = me % ny
    z = me // ny
    piece, cols = w_ref.shape
    A = pl.ds(0, ca)
    B = pl.ds(ca, cols - ca)
    hy, hz = ny // 2, nz // 2
    hb = (cols - ca) // 2
    B1 = pl.ds(ca, hb)
    B2 = pl.ds(ca + hb, cols - ca - hb)

    def zz(k):
        return (z + nz + k) % nz

    def yy(k):
        return (y + ny + k) % ny

    def dev(zi, yi):
        return (zi * ny + yi, head)

    rounds = count.bit_length() - 1
    partners = []
    for k in range(rounds):
        step = 1 << k
        bit = (me // step) % 2
        partners.append((me + step - 2 * step * bit, bit))
    ring = [dev(z, yy(1)), dev(z, yy(-1)), dev(zz(1), y), dev(zz(-1), y)]
    barrier = pltpu.get_barrier_semaphore()
    for target in ring:
        pl.semaphore_signal(barrier, inc=1, device_id=target, device_id_type=MESH)
    for partner, _ in partners:
        pl.semaphore_signal(barrier, inc=1, device_id=(partner, head), device_id_type=MESH)
    pl.semaphore_wait(barrier, len(ring) + rounds)

    local = pltpu.make_async_copy(w_ref, rows_ref.at[z, y], local_sem)
    local.start()
    R = rows_ref
    yr, yl, zr, zl = dev(z, yy(1)), dev(z, yy(-1)), dev(zz(1), y), dev(zz(-1), y)
    ticks = [
        [(w_ref.at[:, A], R.at[z, y, :, A], yr), (w_ref.at[:, A], R.at[z, y, :, A], yl),
         (w_ref.at[:, B], R.at[z, y, :, B], zr), (w_ref.at[:, B], R.at[z, y, :, B], zl)],
        [(R.at[z, yy(-1), :, A], R.at[z, yy(-1), :, A], yr),
         (R.at[zz(-1), y, :, B], R.at[zz(-1), y, :, B], zr), (R.at[zz(1), y, :, B], R.at[zz(1), y, :, B], zl)],
        [(R.at[z, :, :, A], R.at[z, :, :, A], zr), (R.at[z, :, :, A], R.at[z, :, :, A], zl),
         (R.at[zz(-2), y, :, B], R.at[zz(-2), y, :, B], zr), (R.at[zz(2), y, :, B], R.at[zz(2), y, :, B], zl)],
        [(R.at[zz(-1), :, :, A], R.at[zz(-1), :, :, A], zr), (R.at[zz(1), :, :, A], R.at[zz(1), :, :, A], zl),
         (R.at[zz(-3), y, :, B1], R.at[zz(-3), y, :, B1], zr),
         (R.at[zz(3), y, :, B2], R.at[zz(3), y, :, B2], zl)],
        [(R.at[zz(-2), :, :, A], R.at[zz(-2), :, :, A], zr), (R.at[zz(2), :, :, A], R.at[zz(2), :, :, A], zl),
         (R.at[:, y, :, B], R.at[:, y, :, B], yr), (R.at[:, y, :, B], R.at[:, y, :, B], yl)],
        [(R.at[zz(-3), pl.ds(0, hy), :, A], R.at[zz(-3), pl.ds(0, hy), :, A], zr),
         (R.at[zz(3), pl.ds(hy, ny - hy), :, A], R.at[zz(3), pl.ds(hy, ny - hy), :, A], zl),
         (R.at[pl.ds(0, hz), yy(-1), :, B], R.at[pl.ds(0, hz), yy(-1), :, B], yr),
         (R.at[pl.ds(hz, nz - hz), yy(1), :, B], R.at[pl.ds(hz, nz - hz), yy(1), :, B], yl)],
    ]
    total = value_ref[...]
    partial = jnp.zeros_like(total)
    n = 0
    for t, moves in enumerate(ticks):
        if t == 2:
            local.wait()
        started = []
        for src, dst, target in moves:
            copy = pltpu.make_async_remote_copy(
                src_ref=src, dst_ref=dst, send_sem=send_sem.at[n], recv_sem=recv_sem.at[n],
                device_id=target, device_id_type=MESH,
            )
            copy.start()
            started.append(copy)
            n += 1
        scan = None
        if t < rounds:
            partner, bit = partners[t]
            sent = total.astype(jnp.bfloat16)
            sendbuf[t] = sent
            scan = pltpu.make_async_remote_copy(
                src_ref=sendbuf.at[t], dst_ref=recvbuf.at[t], send_sem=bf_send.at[t],
                recv_sem=bf_recv.at[t], device_id=(partner, head), device_id_type=MESH,
            )
            scan.start()
        for copy in started:
            copy.wait()
        if scan is not None:
            scan.wait()
            other = recvbuf[t].astype(jnp.float32)
            partial = jnp.where(bit == 1, partial + other, partial)
            total = sent.astype(jnp.float32) + other
    partial_ref[...] = partial


def gather_and_scan(value, weight):
    count = lax.axis_size("seq")
    ny = 4
    piece, cols = weight.shape
    rounds = count.bit_length() - 1
    ca = (cols * 2 // 3) // 128 * 128
    n_copies = 23
    return pl.pallas_call(
        functools.partial(gather_kernel, ny, ca),
        out_shape=(
            jax.ShapeDtypeStruct((count // ny, ny, piece, cols), weight.dtype),
            jax.ShapeDtypeStruct(value.shape, jnp.float32),
        ),
        in_specs=[pl.BlockSpec(memory_space=pltpu.VMEM), pl.BlockSpec(memory_space=pl.ANY)],
        out_specs=(pl.BlockSpec(memory_space=pl.ANY), pl.BlockSpec(memory_space=pltpu.VMEM)),
        scratch_shapes=[
            pltpu.VMEM((rounds,) + value.shape, jnp.bfloat16),
            pltpu.VMEM((rounds,) + value.shape, jnp.bfloat16),
            pltpu.SemaphoreType.DMA((n_copies,)),
            pltpu.SemaphoreType.DMA((n_copies,)),
            pltpu.SemaphoreType.DMA((rounds,)),
            pltpu.SemaphoreType.DMA((rounds,)),
            pltpu.SemaphoreType.DMA(()),
        ],
        compiler_params=pltpu.CompilerParams(collective_id=2, has_side_effects=True),
    )(value.astype(jnp.float32), weight)


def normalize(attended):
    return attended * lax.rsqrt(jnp.mean(attended * attended, axis=-1, keepdims=True) + EPS)


def shards(query, key, value, init_state, out_weight, out_grad):
    tok_rows = query.shape[0]
    width = query.shape[1]
    heads_here = init_state.shape[0]
    head_dim = init_state.shape[2]
    queries = query.reshape(tok_rows, heads_here, head_dim)
    key_rows = key.reshape(tok_rows, heads_here, head_dim)
    val_rows = value.reshape(tok_rows, heads_here, head_dim)
    local_state = jnp.einsum("thi,thj->hij", key_rows, val_rows, preferred_element_type=jnp.float32)
    half = out_weight.shape[1] // 2
    gathered, earlier = gather_and_scan(local_state, out_weight[:, :half])
    other_half = lax.all_gather(out_weight[:, half:], "seq", axis=0, tiled=True)
    state_half = (init_state + earlier).astype(jnp.bfloat16)
    row_index = lax.broadcasted_iota(jnp.int32, (tok_rows, tok_rows), 0)
    col_index = lax.broadcasted_iota(jnp.int32, (tok_rows, tok_rows), 1)
    causal = col_index <= row_index
    scores = jnp.einsum("thi,shi->hts", queries, key_rows, preferred_element_type=jnp.float32)
    attn_weights = jnp.where(causal, scores, 0.0).astype(jnp.bfloat16)
    attended = jnp.einsum(
        "hts,shj->thj", attn_weights, val_rows, preferred_element_type=jnp.float32
    )
    attended = attended + jnp.einsum(
        "thi,hij->thj", queries, state_half, preferred_element_type=jnp.float32
    )
    normed = normalize(attended).astype(jnp.bfloat16).reshape(tok_rows, width)
    first_rows = gathered.reshape(-1, half)
    weight_rows = jnp.concatenate([first_rows, other_half], axis=1)
    projected = jnp.dot(normed, weight_rows, preferred_element_type=jnp.float32).astype(jnp.bfloat16)
    projected, first_rows, other_half = lax.optimization_barrier((projected, first_rows, other_half))
    contract = (((1,), (1,)), ((), ()))
    grad_normed = lax.dot_general(
        out_grad[:, :half], first_rows, contract, preferred_element_type=jnp.float32
    ) + lax.dot_general(out_grad[:, half:], other_half, contract, preferred_element_type=jnp.float32)
    mixed = lax.psum_scatter(
        projected, "head", scatter_dimension=1, tiled=True
    )
    _, norm_back = jax.vjp(normalize, attended)
    grad_att = norm_back(grad_normed.reshape(tok_rows, heads_here, head_dim))[0].astype(
        jnp.bfloat16
    )
    grad_query, grad_key, grad_value, init_grad = backward_pass(
        query, key, value, grad_att.reshape(tok_rows, width), state_half
    )
    return (mixed, grad_query, grad_key, grad_value, init_grad)


def solution(mesh):
    return jax.shard_map(
        shards,
        mesh=mesh,
        in_specs=(
            P("seq", "head"),
            P("seq", "head"),
            P("seq", "head"),
            P("head", None, None),
            P(("head", "seq"), None),
            P("seq", None),
        ),
        out_specs=(
            P("seq", "head"),
            P("seq", "head"),
            P("seq", "head"),
            P("seq", "head"),
            P("head", None, None),
        ),
        check_vma=False,
    )
```
